32 devices in a mesh: dp: 8 (over z, x), narrow: 4 (over y, core).
Axes of the slice: x: 2, y: 2, z: 4, core: 2. Of those that a mesh axis runs over, the one named last changes fastest.
Arguments:
- patches: bfloat16 [32768, 768], P(('dp', 'narrow')), may hold values from -6 to 6
- pos_index: int32 [32768], P(('dp', 'narrow')), may hold values from 0 to 196, as said below
- segments: int32 [32768], P(('dp', 'narrow')), may hold values from 0 to 27, as said below
- cls_row: int32 [768], P(('dp', 'narrow')), may hold values from 0 to 1023, as said below
- labels: int32 [768], P(('dp', 'narrow')), may hold values from 0 to 999
- img_count: int32 [128], P(('dp', 'narrow')), may hold values from 1 to 6, as said below
- embed_w: float32 [965, 384], P(None, 'dp'), may hold values from -0.21875 to 0.21875
- embed_m: float32 [965, 384], P(None, 'dp')
- embed_v: float32 [965, 384], P(None, 'dp')
- embed_e: float32 [965, 384], P(None, 'dp'), may hold values from -0.21875 to 0.21875
- vector_w: float32 [14, 384], P(None, 'dp')
- vector_m: float32 [14, 384], P(None, 'dp')
- vector_v: float32 [14, 384], P(None, 'dp')
- vector_e: float32 [14, 384], P(None, 'dp')
- mats_w: float32 [3, 384, 4608], P(None, None, 'dp')
- mats_m: float32 [3, 384, 4608], P(None, None, 'dp')
- mats_v: float32 [3, 384, 4608], P(None, None, 'dp')
- mats_e: float32 [3, 384, 4608], P(None, None, 'dp')
- rff_w: float32 [384, 4096], P(None, 'narrow'), may hold values from -0.4375 to 0.4375
- rff_m: float32 [384, 4096], P(None, 'narrow')
- rff_v: float32 [384, 4096], P(None, 'narrow')
- rff_e: float32 [384, 4096], P(None, 'narrow'), may hold values from -0.4375 to 0.4375
- read_w: float32 [4096, 1000], P('narrow')
- read_m: float32 [4096, 1000], P('narrow')
- read_v: float32 [4096, 1000], P('narrow')
- read_e: float32 [4096, 1000], P('narrow'), may hold values from -0.09375 to 0.09375
Outputs:
- loss_sum: float32 [], replicated
- image_total: float32 [], replicated
- clip_norm: float32 [], replicated
- embed_new: float32 [965, 384], P(None, 'dp')
- embed_first: float32 [965, 384], P(None, 'dp')
- embed_second: float32 [965, 384], P(None, 'dp')
- embed_ema: float32 [965, 384], P(None, 'dp')
- embed_copy: bfloat16 [965, 384], P(None, 'dp')
- vector_new: float32 [14, 384], P(None, 'dp')
- vector_first: float32 [14, 384], P(None, 'dp')
- vector_second: float32 [14, 384], P(None, 'dp')
- vector_ema: float32 [14, 384], P(None, 'dp')
- vector_copy: bfloat16 [14, 384], P(None, 'dp')
- mats_new: float32 [3, 384, 4608], P(None, None, 'dp')
- mats_first: float32 [3, 384, 4608], P(None, None, 'dp')
- mats_second: float32 [3, 384, 4608], P(None, None, 'dp')
- mats_ema: float32 [3, 384, 4608], P(None, None, 'dp')
- mats_copy: bfloat16 [3, 384, 4608], P(None, None, 'dp')
- rff_new: float32 [384, 4096], P(None, 'narrow')
- rff_first: float32 [384, 4096], P(None, 'narrow')
- rff_second: float32 [384, 4096], P(None, 'narrow')
- rff_ema: float32 [384, 4096], P(None, 'narrow')
- rff_copy: bfloat16 [384, 4096], P(None, 'narrow')
- read_new: float32 [4096, 1000], P('narrow')
- read_first: float32 [4096, 1000], P('narrow')
- read_second: float32 [4096, 1000], P('narrow')
- read_ema: float32 [4096, 1000], P('narrow')
- read_copy: bfloat16 [4096, 1000], P('narrow')
The draws below stay inside these ranges and needn't reach their ends.
Inputs may be any that keep to these rules, and one draw needn't show every extreme that they name: `pos_index`: each sequence holds whole images one after another from its first row, then pad rows. An image of s x s patches (s = 4, 7 or 10) has its class row, with index 0, followed by its patches in row-major order with index 1 + 10 * row + column. Pad rows have indices from 1 to 196, the first pad row of each sequence 197 - 1. `segments`: the rows of one image share a segment number, the pad rows of one sequence share another, and numbers of different sequences of one device differ; every sequence ends in pad rows. `cls_row`: for slot k of a sequence with k below its count, the row of that image's class token within the device's rows; other slots hold the sequence's last row. `img_count`: in every draw some device's sequences all hold 6 images.
All inputs are finite; a program needn't handle non-finite values.
Results may differ from the reference program's by a relative error of at most 0.035.
Values may be sent and summed in bfloat16 or wider, within the bound.
No kernel may reach another device: no remote copies, remote signals or barrier semaphores. Data moves between devices by JAX's collectives and lax.ppermute only.
A program may use at most 256 MiB of HBM per device.

```python
import math
import jax
import jax.numpy as jnp
from jax import lax

D = 384
HEADS = 6
HD = 64
MLP = 1536
PATCH = 768
POS = 197
RFF = 4096
CLASSES = 1000
L = 3
SEQ = 256
IMG_SEQ = 6
STEP = 10
SEQ_DEV = 4
TOK_DEV = 1024
BLOCK = 512
IMG_DEV = 24
TOKENS = 32768
IMAGES = 768
EMB = 965
NVEC = 14
WIDE = 4608
P_ALL = 11353216
N_DP = 8
N_NARROW = 4


def packing(key):
    base = jax.random.fold_in(key, 7117)
    device_total = N_DP * N_NARROW
    device_ids = jnp.arange(device_total)
    row_dp = device_ids // N_NARROW
    row_narrow = device_ids % N_NARROW
    tilt = (3 * (row_dp * 1000 // max(N_DP - 1, 1)) + row_narrow * 1000 // max(N_NARROW - 1, 1)) // 4
    picks = jax.random.randint(jax.random.fold_in(base, 1), (device_total, SEQ_DEV, IMG_SEQ), 0, 1000)
    small_cut = (50 + 8 * tilt // 10)[:, None, None]
    large_cut = small_cut + 100
    kinds = jnp.where(picks < small_cut, 0, jnp.where(picks >= large_cut, 2, 1))
    forced = jax.random.randint(jax.random.fold_in(base, 2), (), 0, device_total)
    crowded = (forced + 1) % device_total
    kinds = jnp.where((device_ids == forced)[:, None, None], 0, kinds)
    kinds = jnp.where((device_ids == crowded)[:, None, None], 2, kinds)
    image_rows = jnp.where(kinds == 0, 17, jnp.where(kinds == 1, 50, 101))
    image_side = jnp.where(kinds == 0, 4, jnp.where(kinds == 1, 7, 10))
    ends = jnp.cumsum(image_rows, axis=-1)
    keep = ends <= SEQ
    counts = jnp.sum(keep.astype(jnp.int32), axis=-1)
    starts = ends - image_rows
    used = jnp.sum(jnp.where(keep, image_rows, 0), axis=-1)
    places = jnp.arange(SEQ)
    inside = keep[..., None] & (places[None, None, None, :] >= starts[..., None])
    which = jnp.sum(inside.astype(jnp.int32), axis=2) - 1
    padded = places[None, None, :] >= used[..., None]
    chosen = jnp.arange(IMG_SEQ)[None, None, :, None] == which[:, :, None, :]
    start_row = jnp.sum(jnp.where(chosen, starts[..., None], 0), axis=2)
    side = jnp.maximum(jnp.sum(jnp.where(chosen, image_side[..., None], 0), axis=2), 1)
    offset = places[None, None, :] - start_row
    patch_id = jnp.maximum(offset - 1, 0)
    grid_cell = 1 + patch_id // side * 10 + patch_id % side
    pad_place = jnp.maximum(places[None, None, :] - used[..., None], 0)
    pad_index = POS - 1 - pad_place % (POS - 1)
    pos_rows = jnp.where(padded, pad_index, jnp.where(offset == 0, 0, grid_cell))
    seq_ids = jnp.arange(SEQ_DEV)[None, :, None]
    segment_rows = seq_ids * (IMG_SEQ + 1) + jnp.where(padded, IMG_SEQ, which)
    class_rows = jnp.where(keep, seq_ids * SEQ + starts, seq_ids * SEQ + SEQ - 1)
    return (pos_rows.reshape(-1).astype(jnp.int32), segment_rows.reshape(-1).astype(jnp.int32), class_rows.reshape(-1).astype(jnp.int32), counts.reshape(-1).astype(jnp.int32))


def draw_pos_index(key, part):
    return packing(key)[0]


def draw_segments(key, part):
    return packing(key)[1]


def draw_cls_row(key, part):
    return packing(key)[2]


def draw_img_count(key, part):
    return packing(key)[3]


def grad_scale():
    return 0.02 / math.sqrt(P_ALL)


def first_law(key, shape, factor):
    return factor * grad_scale() * jax.random.normal(key, shape, jnp.float32)


def second_law(key, shape, factor):
    level = jax.random.uniform(key, shape, jnp.float32, 0.0, math.log(4.0))
    return jnp.exp(level) * (factor * grad_scale()) ** 2


def vector_law(key, spread):
    column = jnp.arange(D).astype(jnp.float32) / D
    gains = (0.6 + 1.2 * column) * jax.random.uniform(jax.random.fold_in(key, 1), (NVEC, D), jnp.float32, 1.0 - spread, 1.0 + spread)
    shifts = 0.3 * jax.random.normal(jax.random.fold_in(key, 2), (NVEC, D), jnp.float32)
    is_gain = (jnp.arange(NVEC) % 2 == 0)[:, None]
    return jnp.where(is_gain, gains, shifts)


def mats_law(key):
    column = jnp.arange(WIDE)
    scale = jnp.where(column < 3 * D, D ** (-0.5), jnp.where(column < 4 * D, 4.0 * D ** (-0.5), jnp.where(column < 4 * D + MLP, D ** (-0.5), MLP ** (-0.5))))
    return jax.random.normal(key, (L, D, WIDE), jnp.float32) * scale


def draw_read_w(key, part):
    shard_rows = RFF // N_NARROW
    row_ids = jnp.arange(RFF)
    within = (row_ids % shard_rows).astype(jnp.float32) / shard_rows
    shard = (row_ids // shard_rows).astype(jnp.float32) / max(N_NARROW - 1, 1)
    noise = jax.random.normal(jax.random.fold_in(key, 61), (RFF, CLASSES), jnp.float32)
    scale = 0.4 * (1.0 + 2.0 * within) * (1.0 + shard)
    return noise * scale[:, None] * RFF ** (-0.5)


def draw_embed_m(key, part):
    return first_law(jax.random.fold_in(key, 11), (EMB, D), 1.0)


def draw_embed_v(key, part):
    return second_law(jax.random.fold_in(key, 12), (EMB, D), 1.0)


def draw_vector_w(key, part):
    return vector_law(jax.random.fold_in(key, 21), 0.2)


def draw_vector_m(key, part):
    return first_law(jax.random.fold_in(key, 22), (NVEC, D), 3.0)


def draw_vector_v(key, part):
    return second_law(jax.random.fold_in(key, 23), (NVEC, D), 3.0)


def draw_vector_e(key, part):
    return vector_law(jax.random.fold_in(key, 24), 0.5)


def draw_mats_w(key, part):
    return mats_law(jax.random.fold_in(key, 31))


def draw_mats_m(key, part):
    return first_law(jax.random.fold_in(key, 32), (L, D, WIDE), 1.0)


def draw_mats_v(key, part):
    return second_law(jax.random.fold_in(key, 33), (L, D, WIDE), 1.0)


def draw_mats_e(key, part):
    return mats_law(jax.random.fold_in(key, 34))


def draw_rff_m(key, part):
    return first_law(jax.random.fold_in(key, 41), (D, RFF), 1.0)


def draw_rff_v(key, part):
    return second_law(jax.random.fold_in(key, 42), (D, RFF), 1.0)


def draw_read_m(key, part):
    return first_law(jax.random.fold_in(key, 51), (RFF, CLASSES), 1.0)


def draw_read_v(key, part):
    return second_law(jax.random.fold_in(key, 52), (RFF, CLASSES), 1.0)


def place_ends(array, own_key, low, high):
    index_at = [jax.random.randint(jax.random.fold_in(own_key, axis), (), 0, length) for axis, length in enumerate(array.shape)]
    longest = array.shape.index(max(array.shape))
    neighbour = index_at[:longest] + [(index_at[longest] + 1) % array.shape[longest]] + index_at[longest + 1:]
    return array.at[tuple(index_at)].set(low).at[tuple(neighbour)].set(high)


def level_of(stream_key, extent, shards, smallest, top_value):
    loudness = 1.0
    for position, shards_of in shards:
        steps = jax.random.uniform(jax.random.fold_in(jax.random.fold_in(stream_key, 6), position), (shards_of,), jnp.float32, smallest / len(shards), top_value / len(shards))
        loudness = loudness * jnp.repeat(jnp.exp(steps), extent[position] // shards_of).reshape((-1,) + (1,) * (len(extent) - 1 - position))
    return loudness


def normal_values(key, dims, deviation, most, cuts=(), dtype=jnp.bfloat16):
    entries = deviation * jax.random.normal(key, dims, jnp.float32)
    if cuts:
        entries = entries * level_of(key, dims, cuts, -0.22, 0.18)
    return jnp.clip(entries, -most, most).astype(dtype)


def setup_inputs(seed: int = 0) -> dict:
    seeds = jax.random.split(jax.random.key(seed), 27)
    return {
        "patches": normal_values(seeds[0], (TOKENS, PATCH), 1.0, 6.0, ((0, 32),)),
        "pos_index": draw_pos_index(jax.random.fold_in(seeds[26], 71), 0),
        "segments": draw_segments(jax.random.fold_in(seeds[26], 71), 0),
        "cls_row": draw_cls_row(jax.random.fold_in(seeds[26], 71), 0),
        "labels": place_ends(jax.random.randint(seeds[4], (IMAGES,), 0, CLASSES), jax.random.fold_in(seeds[4], 1), 0, CLASSES - 1).astype(jnp.int32),
        "img_count": draw_img_count(jax.random.fold_in(seeds[26], 71), 0),
        "embed_w": normal_values(seeds[6], (EMB, D), PATCH ** -0.5, 0.21875, ((1, 8),), jnp.float32),
        "embed_m": draw_embed_m(jax.random.fold_in(seeds[26], 71), 0),
        "embed_v": draw_embed_v(jax.random.fold_in(seeds[26], 71), 0),
        "embed_e": normal_values(seeds[9], (EMB, D), PATCH ** -0.5, 0.21875, ((1, 8),), jnp.float32),
        "vector_w": draw_vector_w(jax.random.fold_in(seeds[26], 71), 0),
        "vector_m": draw_vector_m(jax.random.fold_in(seeds[26], 71), 0),
        "vector_v": draw_vector_v(jax.random.fold_in(seeds[26], 71), 0),
        "vector_e": draw_vector_e(jax.random.fold_in(seeds[26], 71), 0),
        "mats_w": draw_mats_w(jax.random.fold_in(seeds[26], 71), 0),
        "mats_m": draw_mats_m(jax.random.fold_in(seeds[26], 71), 0),
        "mats_v": draw_mats_v(jax.random.fold_in(seeds[26], 71), 0),
        "mats_e": draw_mats_e(jax.random.fold_in(seeds[26], 71), 0),
        "rff_w": normal_values(seeds[18], (D, RFF), (D // 2) ** -0.5, 0.4375, ((1, 4),), jnp.float32),
        "rff_m": draw_rff_m(jax.random.fold_in(seeds[26], 71), 0),
        "rff_v": draw_rff_v(jax.random.fold_in(seeds[26], 71), 0),
        "rff_e": normal_values(seeds[21], (D, RFF), (D // 2) ** -0.5, 0.4375, ((1, 4),), jnp.float32),
        "read_w": draw_read_w(jax.random.fold_in(seeds[26], 71), 0),
        "read_m": draw_read_m(jax.random.fold_in(seeds[26], 71), 0),
        "read_v": draw_read_v(jax.random.fold_in(seeds[26], 71), 0),
        "read_e": normal_values(seeds[25], (RFF, CLASSES), RFF ** -0.5, 0.09375, ((0, 4),), jnp.float32),
    }


@jax.custom_vjp
def low(v):
    return lax.optimization_barrier(v.astype(jnp.bfloat16)).astype(jnp.float32)

@jax.custom_vjp
def low_back(v):
    return v

def low_keep(v):
    return (low(v), None)

def low_pass(kept, grad):
    return (grad,)

def back_keep(v):
    return (v, None)

def back_low(kept, grad):
    return (low(grad),)
low.defvjp(low_keep, low_pass)
low_back.defvjp(back_keep, back_low)
norm_eps = 1e-06
clip_bound = 0.02
l2_weight = 0.1
beta_first = 0.5
beta_second = 0.5
adam_eps = 1e-08
weight_decay = 0.05
rate_matrix = 0.05
rate_vector = 0.5
ema_rate = 0.5
highest = lax.Precision.HIGHEST

def matmul(left, right):
    return jnp.dot(left, right, precision=highest, preferred_element_type=jnp.float32)

def layer_norm(rows_in, gain, shift):
    centred = rows_in - lax.optimization_barrier(jnp.mean(rows_in, axis=-1, keepdims=True))
    spread = lax.optimization_barrier(jnp.mean(centred * centred, axis=-1, keepdims=True))
    return centred * lax.rsqrt(spread + norm_eps) * gain + shift

def attention(projected, same_segment):
    query_heads = projected[:, :D].reshape(-1, HEADS, HD)
    key_heads = projected[:, D:2 * D].reshape(-1, HEADS, HD)
    value_heads = projected[:, 2 * D:].reshape(-1, HEADS, HD)
    scores = jnp.einsum('qhd,khd->hqk', query_heads, key_heads, precision=highest) * HD ** (-0.5)
    scores = jnp.where(same_segment[None], low_back(scores), -1e+30)
    probability = low(jax.nn.softmax(scores, axis=-1))
    attended = jnp.einsum('hqk,khd->qhd', probability, value_heads, precision=highest)
    return low(low_back(attended.reshape(-1, D)))

def block_forward(embed_b, vector_b, mats_b, patch_rows, pos_rows, seg_rows):
    is_patch = (pos_rows != 0).astype(jnp.float32)[:, None]
    onehot_table = (pos_rows[:, None] == jnp.arange(POS)[None, :]).astype(jnp.float32)
    state = low_back(matmul(jnp.concatenate([patch_rows * is_patch, onehot_table], axis=1), embed_b))
    same_segment = seg_rows[:, None] == seg_rows[None, :]
    for layer_id in range(L):
        weight = mats_b[layer_id]
        normed = low(layer_norm(state, vector_b[4 * layer_id], vector_b[4 * layer_id + 1]))
        projected = low(low_back(matmul(normed, weight[:, :3 * D])))
        attended = attention(projected, same_segment)
        state = state + low_back(matmul(attended, weight[:, 3 * D:4 * D]))
        second = low(layer_norm(state, vector_b[4 * layer_id + 2], vector_b[4 * layer_id + 3]))
        hidden = low(jax.nn.gelu(low_back(matmul(second, weight[:, 4 * D:4 * D + MLP]))))
        state = state + low_back(matmul(hidden, weight[:, 4 * D + MLP:].T))
    return layer_norm(state, vector_b[4 * L], vector_b[4 * L + 1])

def forward(masters, patches, pos_index, segments, rows, labels, valid_mask, image_total):
    embed_b, vector_b, mats_b, rff_b, read_b = [low(weight) for weight in masters]

    def one_block(carry, pieces):
        return (carry, jax.checkpoint(block_forward)(embed_b, vector_b, mats_b, pieces[0], pieces[1], pieces[2]))
    blocks = (patches.reshape(-1, BLOCK, PATCH), pos_index.reshape(-1, BLOCK), segments.reshape(-1, BLOCK))
    _, final_rows = lax.scan(one_block, jnp.float32(0.0), blocks)
    features = low(final_rows.reshape(-1, D)[rows])
    phases = low_back(matmul(features, rff_b))
    lifted = low(jnp.cos(phases))
    logits = low_back(matmul(lifted, read_b))
    target = (labels[:, None] == jnp.arange(CLASSES)[None, :]).astype(jnp.float32)
    error = logits - target
    ridge_sum = jnp.sum(masters[4] * masters[4])
    return jnp.sum(valid_mask[:, None] * error * error) + l2_weight * image_total * ridge_sum

def adamw(weight, first, second, average, grad, rate, decay):
    first = beta_first * first + (1.0 - beta_first) * grad
    second = beta_second * second + (1.0 - beta_second) * grad * grad
    ahead = first / (1.0 - beta_first ** STEP)
    behind = second / (1.0 - beta_second ** STEP)
    weight = weight - rate * (ahead / (jnp.sqrt(behind) + adam_eps) + decay * weight)
    average = ema_rate * average + (1.0 - ema_rate) * weight
    return (weight, first, second, average, weight.astype(jnp.bfloat16))

def reference(patches, pos_index, segments, cls_row, labels, img_count, embed_w, embed_m, embed_v, embed_e, vector_w, vector_m, vector_v, vector_e, mats_w, mats_m, mats_v, mats_e, rff_w, rff_m, rff_v, rff_e, read_w, read_m, read_v, read_e):
    slot_ids = jnp.arange(IMAGES)
    valid_mask = (slot_ids % IMG_SEQ < img_count[slot_ids // IMG_SEQ]).astype(jnp.float32)
    rows = cls_row + slot_ids // IMG_DEV * TOK_DEV
    image_total = jnp.sum(img_count).astype(jnp.float32)
    masters = (embed_w, vector_w, mats_w, rff_w, read_w)
    patch_float = patches.astype(jnp.float32)

    def objective(params):
        return forward(params, patch_float, pos_index, segments, rows, labels, valid_mask, image_total)
    loss_sum, pull = jax.vjp(objective, masters)
    grads = [grad / image_total for grad in pull(jnp.ones_like(loss_sum))[0]]
    clip_norm = jnp.sqrt(sum((jnp.sum(grad * grad) for grad in grads)))
    factor = jnp.minimum(1.0, clip_bound / clip_norm)
    embed_out = adamw(embed_w, embed_m, embed_v, embed_e, grads[0] * factor, rate_matrix, weight_decay)
    vector_out = adamw(vector_w, vector_m, vector_v, vector_e, grads[1] * factor, rate_vector, 0.0)
    mats_out = adamw(mats_w, mats_m, mats_v, mats_e, grads[2] * factor, rate_matrix, weight_decay)
    rff_out = adamw(rff_w, rff_m, rff_v, rff_e, grads[3] * factor, rate_matrix, weight_decay)
    read_out = adamw(read_w, read_m, read_v, read_e, grads[4] * factor, rate_matrix, weight_decay)
    return (loss_sum, image_total, clip_norm, embed_out[0], embed_out[1], embed_out[2], embed_out[3], embed_out[4], vector_out[0], vector_out[1], vector_out[2], vector_out[3], vector_out[4], mats_out[0], mats_out[1], mats_out[2], mats_out[3], mats_out[4], rff_out[0], rff_out[1], rff_out[2], rff_out[3], rff_out[4], read_out[0], read_out[1], read_out[2], read_out[3], read_out[4])
```

```python
import math
import jax
import jax.numpy as jnp
from jax import lax
from jax.experimental import pallas as pl
from jax.experimental.pallas import tpu as pltpu
from jax.sharding import PartitionSpec as P

D = 384
HEADS = 6
HD = 64
MLP = 1536
SEQ = 256
norm_eps = 1e-06
GELU_A = 0.7978845608028654
GELU_B = 0.044715
f32 = jnp.float32
bf16 = jnp.bfloat16


def nn(a, b):
    return lax.dot_general(a, b, (((1,), (0,)), ((), ())), preferred_element_type=f32)


def nt(a, b):
    return lax.dot_general(a, b, (((1,), (1,)), ((), ())), preferred_element_type=f32)


def tn(a, b):
    return lax.dot_general(a, b, (((0,), (0,)), ((), ())), preferred_element_type=f32)


def unit(rows):
    centred = rows - jnp.mean(rows, axis=-1, keepdims=True)
    inverse = lax.rsqrt(jnp.mean(centred * centred, axis=-1, keepdims=True) + norm_eps)
    return centred * inverse, inverse


def unit_back(u, inverse, gain, grad):
    scaled = grad * gain
    return inverse * (
        scaled
        - jnp.mean(scaled, axis=-1, keepdims=True)
        - u * jnp.mean(scaled * u, axis=-1, keepdims=True)
    )


def gelu_parts(x):
    x2 = x * x
    t = jnp.tanh(GELU_A * x * (1.0 + GELU_B * x2))
    half = 0.5 * (1.0 + t)
    return half, t, x2


def gelu_value(x):
    half, _, _ = gelu_parts(x)
    return x * half


def gelu_both(x):
    half, t, x2 = gelu_parts(x)
    slope = half + 0.5 * x * (1.0 - t * t) * (GELU_A * (1.0 + 3.0 * GELU_B * x2))
    return x * half, slope


def layer_rows(x, wa_ref, wu_ref, wd_ref, gains, seg_col, seg_row):
    g1, b1, g2, b2 = (gains[i : i + 1, :] for i in range(4))
    u, _ = unit(x)
    normed = (u * g1 + b1).astype(bf16)
    qkv = nt(normed, wa_ref[: 3 * D, :]).astype(bf16)
    heads = []
    rows = x.shape[0]
    for s in range(rows // SEQ):
        r = slice(s * SEQ, (s + 1) * SEQ)
        same = seg_col[r, :] == seg_row[:, r]
        outs = []
        for h in range(HEADS):
            q = qkv[r, h * HD : (h + 1) * HD]
            k = qkv[r, D + h * HD : D + (h + 1) * HD]
            v = qkv[r, 2 * D + h * HD : 2 * D + (h + 1) * HD]
            sc = jnp.where(same, nt(q, k) * HD ** (-0.5), -1e30)
            e = jnp.exp(sc - jnp.max(sc, axis=-1, keepdims=True))
            p = (e * (1.0 / jnp.sum(e, axis=-1, keepdims=True))).astype(bf16)
            outs.append(nn(p, v))
        heads.append(jnp.concatenate(outs, axis=1))
    att = jnp.concatenate(heads, axis=0).astype(bf16)
    x1 = x + nt(att, wa_ref[3 * D :, :])
    u2, _ = unit(x1)
    second = (u2 * g2 + b2).astype(bf16)
    hidden = gelu_value(nt(second, wu_ref[...])).astype(bf16)
    out = x1 + nn(hidden, wd_ref[...])
    return qkv, att, x1, out


def fwd_kernel(x_ref, wa_ref, wu_ref, wd_ref, g_ref, sc_ref, sr_ref, qkv_ref, att_ref, x1_ref, out_ref):
    qkv, att, x1, out = layer_rows(x_ref[...], wa_ref, wu_ref, wd_ref, g_ref[...], sc_ref[...], sr_ref[0])
    qkv_ref[...] = qkv
    att_ref[...] = att
    x1_ref[...] = x1
    out_ref[...] = out


def first_kernel(p_ref, pos_ref, e_ref, wa_ref, wu_ref, wd_ref, g_ref, sc_ref, sr_ref, in_ref, x_ref, qkv_ref, att_ref, x1_ref, out_ref):
    pos = pos_ref[...]
    patch = jnp.where(pos != 0, p_ref[...].astype(f32), 0.0).astype(bf16)
    lanes = e_ref.shape[1] - p_ref.shape[1]
    table = (pos == lax.broadcasted_iota(jnp.int32, (pos.shape[0], lanes), 1)).astype(f32).astype(bf16)
    full = jnp.concatenate([patch, table], axis=1)
    in_ref[...] = full
    x = nt(full, e_ref[...])
    x_ref[...] = x
    qkv, att, x1, out = layer_rows(x, wa_ref, wu_ref, wd_ref, g_ref[...], sc_ref[...], sr_ref[0])
    qkv_ref[...] = qkv
    att_ref[...] = att
    x1_ref[...] = x1
    out_ref[...] = out


def rows_spec(r, width):
    return pl.BlockSpec((r, width), lambda i: (i, 0))


def whole_spec(shape):
    return pl.BlockSpec(shape, lambda *i: (0,) * len(shape))


def third_spec(block):
    return pl.BlockSpec((4 * D, D), lambda *i: (block, 0))


def params(mb=56, n=1):
    return pltpu.CompilerParams(dimension_semantics=("arbitrary",) * n, vmem_limit_bytes=mb << 20)


def layer_forward(x, w, layer, gains, seg, step_rows=512):
    rows = x.shape[0]
    steps = rows // step_rows
    return pl.pallas_call(
        fwd_kernel,
        grid=(steps,),
        in_specs=[
            rows_spec(step_rows, D),
            *(third_spec(3 * layer + i) for i in range(3)),
            whole_spec(gains.shape),
            rows_spec(step_rows, 1),
            pl.BlockSpec((1, 1, step_rows), lambda i: (i, 0, 0)),
        ],
        out_specs=[rows_spec(step_rows, 3 * D), rows_spec(step_rows, D), rows_spec(step_rows, D), rows_spec(step_rows, D)],
        out_shape=[
            jax.ShapeDtypeStruct((rows, 3 * D), bf16),
            jax.ShapeDtypeStruct((rows, D), bf16),
            jax.ShapeDtypeStruct((rows, D), f32),
            jax.ShapeDtypeStruct((rows, D), f32),
        ],
        compiler_params=params(),
        name="layer_fwd",
    )(x, w, w, w, gains, seg[:, None], seg.reshape(steps, 1, step_rows))


def first_forward(patches, pos, e, w, layer, gains, seg, step_rows=512):
    rows, patch = patches.shape
    lanes = e.shape[1]
    steps = rows // step_rows
    return pl.pallas_call(
        first_kernel,
        grid=(steps,),
        in_specs=[
            rows_spec(step_rows, patch),
            rows_spec(step_rows, 1),
            whole_spec(e.shape),
            *(third_spec(3 * layer + i) for i in range(3)),
            whole_spec(gains.shape),
            rows_spec(step_rows, 1),
            pl.BlockSpec((1, 1, step_rows), lambda i: (i, 0, 0)),
        ],
        out_specs=[rows_spec(step_rows, lanes), rows_spec(step_rows, D), rows_spec(step_rows, 3 * D), rows_spec(step_rows, D), rows_spec(step_rows, D), rows_spec(step_rows, D)],
        out_shape=[
            jax.ShapeDtypeStruct((rows, lanes), bf16),
            jax.ShapeDtypeStruct((rows, D), f32),
            jax.ShapeDtypeStruct((rows, 3 * D), bf16),
            jax.ShapeDtypeStruct((rows, D), bf16),
            jax.ShapeDtypeStruct((rows, D), f32),
            jax.ShapeDtypeStruct((rows, D), f32),
        ],
        compiler_params=params(),
        name="first_fwd",
    )(patches, pos[:, None], e, w, w, w, gains, seg[:, None], seg.reshape(steps, 1, step_rows))


def last_fwd_kernel(cls_ref, x_ref, wa_ref, wu_ref, wd_ref, g_ref, sk_ref, sq_ref, kv_ref, xc_ref, q_ref, att_ref, x1_ref, out_ref, feat_ref):
    g1, b1, g2, b2, g3, b3 = (g_ref[i : i + 1, :] for i in range(6))
    u, _ = unit(x_ref[...])
    normed = (u * g1 + b1).astype(bf16)
    kv = nt(normed, wa_ref[D : 3 * D, :]).astype(bf16)
    kv_ref[...] = kv
    slots = xc_ref.shape[0]
    for i in range(slots):
        xc_ref[i : i + 1, :] = x_ref[pl.ds(cls_ref[i], 1), :]
    xc = xc_ref[...]
    uc, _ = unit(xc)
    q = nt((uc * g1 + b1).astype(bf16), wa_ref[:D, :]).astype(bf16)
    q_ref[...] = q
    same = sq_ref[...] == sk_ref[...]
    outs = []
    for h in range(HEADS):
        c = slice(h * HD, (h + 1) * HD)
        sc = jnp.where(same, nt(q[:, c], kv[:, c]) * HD ** (-0.5), -1e30)
        e = jnp.exp(sc - jnp.max(sc, axis=-1, keepdims=True))
        p = (e * (1.0 / jnp.sum(e, axis=-1, keepdims=True))).astype(bf16)
        outs.append(nn(p, kv[:, D + h * HD : D + (h + 1) * HD]))
    att = jnp.concatenate(outs, axis=1).astype(bf16)
    att_ref[...] = att
    x1 = xc + nt(att, wa_ref[3 * D :, :])
    x1_ref[...] = x1
    u2, _ = unit(x1)
    second = (u2 * g2 + b2).astype(bf16)
    hidden = gelu_value(nt(second, wu_ref[...])).astype(bf16)
    out = x1 + nn(hidden, wd_ref[...])
    out_ref[...] = out
    u3, _ = unit(out)
    feat_ref[...] = (u3 * g3 + b3).astype(bf16)


def smem_spec():
    return pl.BlockSpec(memory_space=pltpu.SMEM)


def vmem_spec():
    return pl.BlockSpec(memory_space=pltpu.VMEM)


def last_forward(cls, x, w, layer, gains, seg, seg_cls):
    rows, slots = x.shape[0], cls.shape[0]
    return pl.pallas_call(
        last_fwd_kernel,
        grid=(1,),
        in_specs=[smem_spec(), whole_spec(x.shape), *(third_spec(3 * layer + i) for i in range(3)), *[vmem_spec()] * 3],
        out_specs=[vmem_spec()] * 7,
        out_shape=[
            jax.ShapeDtypeStruct((rows, 2 * D), bf16),
            jax.ShapeDtypeStruct((slots, D), f32),
            jax.ShapeDtypeStruct((slots, D), bf16),
            jax.ShapeDtypeStruct((slots, D), bf16),
            jax.ShapeDtypeStruct((slots, D), f32),
            jax.ShapeDtypeStruct((slots, D), f32),
            jax.ShapeDtypeStruct((slots, D), bf16),
        ],
        compiler_params=params(),
        name="last_fwd",
    )(cls, x, w, w, w, gains, seg[None, :], seg_cls[:, None])


def last_bwd_kernel(cls_ref, df_ref, x_ref, wa_ref, wu_ref, wd_ref, g_ref, sk_ref, sq_ref, kv_ref, xc_ref, q_ref, att_ref, x1_ref, xo_ref, dx_ref, dw_ref, dv_ref, dn_ref):
    g1, b1, g2, b2, g3, b3 = (g_ref[i : i + 1, :] for i in range(6))
    slots = xc_ref.shape[0]
    df = df_ref[...]
    u3, i3 = unit(xo_ref[...])
    dxo = unit_back(u3, i3, g3, df)
    dg3 = jnp.sum(df * u3, axis=0, keepdims=True)
    db3 = jnp.sum(df, axis=0, keepdims=True)
    branch = dxo.astype(bf16)
    u2, i2 = unit(x1_ref[...])
    second = (u2 * g2 + b2).astype(bf16)
    value, slope = gelu_both(nt(second, wu_ref[...]))
    dpre = (nt(branch, wd_ref[...]) * slope).astype(bf16)
    dw_ref[4 * D + MLP :, :] = tn(value.astype(bf16), branch).astype(bf16)
    dw_ref[4 * D : 4 * D + MLP, :] = tn(dpre, second).astype(bf16)
    dsecond = nn(dpre, wu_ref[...])
    dg2 = jnp.sum(dsecond * u2, axis=0, keepdims=True)
    db2 = jnp.sum(dsecond, axis=0, keepdims=True)
    dx1 = dxo + unit_back(u2, i2, g2, dsecond)
    ab = dx1.astype(bf16)
    datt = nn(ab, wa_ref[3 * D :, :]).astype(bf16)
    dw_ref[3 * D : 4 * D, :] = tn(ab, att_ref[...]).astype(bf16)
    same = sq_ref[...] == sk_ref[...]
    q, kv = q_ref[...], kv_ref[...]
    dqs, dks, dvs = [], [], []
    for h in range(HEADS):
        c = slice(h * HD, (h + 1) * HD)
        k, v = kv[:, c], kv[:, D + h * HD : D + (h + 1) * HD]
        sc = jnp.where(same, nt(q[:, c], k) * HD ** (-0.5), -1e30)
        e = jnp.exp(sc - jnp.max(sc, axis=-1, keepdims=True))
        p = e * (1.0 / jnp.sum(e, axis=-1, keepdims=True))
        dp = nt(datt[:, c], v)
        ds = (p * (dp - jnp.sum(dp * p, axis=-1, keepdims=True))).astype(bf16)
        dvs.append(tn(p.astype(bf16), datt[:, c]))
        dks.append(tn(ds, q[:, c]) * HD ** (-0.5))
        dqs.append(nn(ds, k) * HD ** (-0.5))
    dq = jnp.concatenate(dqs, axis=1).astype(bf16)
    dkv = jnp.concatenate(dks + dvs, axis=1).astype(bf16)
    u, i1 = unit(x_ref[...])
    normed = (u * g1 + b1).astype(bf16)
    dw_ref[D : 3 * D, :] = tn(dkv, normed).astype(bf16)
    uc, _ = unit(xc_ref[...])
    dw_ref[:D, :] = tn(dq, (uc * g1 + b1).astype(bf16)).astype(bf16)
    dn_ref[...] = nn(dkv, wa_ref[D : 3 * D, :])
    dnc = nn(dq, wa_ref[:D, :])
    for i in range(slots):
        at = pl.ds(cls_ref[i], 1)
        dn_ref[at, :] = dn_ref[at, :] + dnc[i : i + 1, :]
    dn = dn_ref[...]
    dg1 = jnp.sum(dn * u, axis=0, keepdims=True)
    db1 = jnp.sum(dn, axis=0, keepdims=True)
    dx_ref[...] = unit_back(u, i1, g1, dn)
    for i in range(slots):
        at = pl.ds(cls_ref[i], 1)
        dx_ref[at, :] = dx_ref[at, :] + dx1[i : i + 1, :]
    dv_ref[...] = jnp.concatenate([dg1, db1, dg2, db2, dg3, db3, jnp.zeros((2, D), f32)], axis=0)


def last_backward(cls, df, x, w, layer, gains, seg, seg_cls, kv, xc, q, att, x1, xo):
    rows = x.shape[0]
    return pl.pallas_call(
        last_bwd_kernel,
        grid=(1,),
        in_specs=[smem_spec(), vmem_spec(), whole_spec(x.shape), *(third_spec(3 * layer + i) for i in range(3)), *[vmem_spec()] * 9],
        out_specs=[vmem_spec()] * 3,
        out_shape=[
            jax.ShapeDtypeStruct((rows, D), f32),
            jax.ShapeDtypeStruct((12 * D, D), bf16),
            jax.ShapeDtypeStruct((8, D), f32),
        ],
        scratch_shapes=[pltpu.VMEM((rows, D), f32)],
        compiler_params=params(),
        name="last_bwd",
    )(cls, df, x, w, w, w, gains, seg[None, :], seg_cls[:, None], kv, xc, q, att, x1, xo)


def mlp_bwd_kernel(dxo_ref, x1_ref, wu_ref, wd_ref, g_ref, dx1_ref, dw_ref, dv_ref, acc_ref):
    step = pl.program_id(0)
    g2, b2 = g_ref[2:3, :], g_ref[3:4, :]
    dxo = dxo_ref[...]
    branch = dxo.astype(bf16)
    u2, i2 = unit(x1_ref[...])
    second = (u2 * g2 + b2).astype(bf16)
    value, slope = gelu_both(nt(second, wu_ref[...]))
    hidden = value.astype(bf16)
    dpre = (nt(branch, wd_ref[...]) * slope).astype(bf16)
    dsecond = nn(dpre, wu_ref[...])
    sums = jnp.concatenate([jnp.sum(dsecond * u2, axis=0, keepdims=True), jnp.sum(dsecond, axis=0, keepdims=True), jnp.zeros((6, D), f32)], axis=0)
    dx1_ref[...] = dxo + unit_back(u2, i2, g2, dsecond)
    last = pl.num_programs(0) - 1

    @pl.when(step == 0)
    def _():
        acc_ref[:MLP, :] = tn(dpre, second)
        acc_ref[MLP:, :] = tn(hidden, branch)
        dv_ref[...] = sums

    @pl.when(step > 0)
    def _():
        acc_ref[:MLP, :] += tn(dpre, second)
        acc_ref[MLP:, :] += tn(hidden, branch)
        dv_ref[...] += sums

    @pl.when(step == last)
    def _():
        dw_ref[...] = acc_ref[...].astype(bf16)


def mlp_backward(dxo, x1, w, layer, gains, step_rows=512):
    rows = x1.shape[0]
    steps = rows // step_rows
    return pl.pallas_call(
        mlp_bwd_kernel,
        grid=(steps,),
        in_specs=[rows_spec(step_rows, D), rows_spec(step_rows, D), third_spec(3 * layer + 1), third_spec(3 * layer + 2), whole_spec(gains.shape)],
        out_specs=[rows_spec(step_rows, D), whole_spec((2 * MLP, D)), whole_spec((8, D))],
        out_shape=[jax.ShapeDtypeStruct((rows, D), f32), jax.ShapeDtypeStruct((2 * MLP, D), bf16), jax.ShapeDtypeStruct((8, D), f32)],
        scratch_shapes=[pltpu.VMEM((2 * MLP, D), f32)],
        compiler_params=params(),
        name="mlp_bwd",
    )(dxo, x1, w, w, gains)


def att_bwd_kernel(dx1_ref, x_ref, qkv_ref, att_ref, w_ref, g_ref, sc_ref, sr_ref, dx_ref, dw_ref, dv_ref, acc_ref):
    step = pl.program_id(0)
    g1, b1 = g_ref[0:1, :], g_ref[1:2, :]
    dx1 = dx1_ref[...]
    ab = dx1.astype(bf16)
    datt = nn(ab, w_ref[3 * D : 4 * D, :]).astype(bf16)
    qkv = qkv_ref[...]
    parts = []
    for s in range(x_ref.shape[0] // SEQ):
        r = slice(s * SEQ, (s + 1) * SEQ)
        same = sc_ref[r, :] == sr_ref[0][:, r]
        dqs, dks, dvs = [], [], []
        for h in range(HEADS):
            q = qkv[r, h * HD : (h + 1) * HD]
            k = qkv[r, D + h * HD : D + (h + 1) * HD]
            v = qkv[r, 2 * D + h * HD : 2 * D + (h + 1) * HD]
            da = datt[r, h * HD : (h + 1) * HD]
            sc = jnp.where(same, nt(k, q) * HD ** (-0.5), -1e30)
            e = jnp.exp(sc - jnp.max(sc, axis=0, keepdims=True))
            p = e * (1.0 / jnp.sum(e, axis=0, keepdims=True))
            dp = nt(v, da)
            ds = (p * (dp - jnp.sum(dp * p, axis=0, keepdims=True))).astype(bf16)
            dvs.append(nn(p.astype(bf16), da))
            dks.append(nn(ds, q) * HD ** (-0.5))
            dqs.append(tn(ds, k) * HD ** (-0.5))
        parts.append(jnp.concatenate(dqs + dks + dvs, axis=1).astype(bf16))
    dqkv = jnp.concatenate(parts, axis=0)
    u, i1 = unit(x_ref[...])
    normed = (u * g1 + b1).astype(bf16)
    dn = nn(dqkv, w_ref[: 3 * D, :])
    sums = jnp.concatenate([jnp.sum(dn * u, axis=0, keepdims=True), jnp.sum(dn, axis=0, keepdims=True), jnp.zeros((6, D), f32)], axis=0)
    dx_ref[...] = dx1 + unit_back(u, i1, g1, dn)
    last = pl.num_programs(0) - 1

    @pl.when(step == 0)
    def _():
        acc_ref[: 3 * D, :] = tn(dqkv, normed)
        acc_ref[3 * D :, :] = tn(ab, att_ref[...])
        dv_ref[...] = sums

    @pl.when(step > 0)
    def _():
        acc_ref[: 3 * D, :] += tn(dqkv, normed)
        acc_ref[3 * D :, :] += tn(ab, att_ref[...])
        dv_ref[...] += sums

    @pl.when(step == last)
    def _():
        dw_ref[...] = acc_ref[...].astype(bf16)


def att_backward(dx1, x, qkv, att, w, layer, gains, seg, step_rows=512):
    rows = x.shape[0]
    steps = rows // step_rows
    return pl.pallas_call(
        att_bwd_kernel,
        grid=(steps,),
        in_specs=[
            rows_spec(step_rows, D),
            rows_spec(step_rows, D),
            rows_spec(step_rows, 3 * D),
            rows_spec(step_rows, D),
            third_spec(3 * layer),
            whole_spec(gains.shape),
            rows_spec(step_rows, 1),
            pl.BlockSpec((1, 1, step_rows), lambda i: (i, 0, 0)),
        ],
        out_specs=[rows_spec(step_rows, D), whole_spec((4 * D, D)), whole_spec((8, D))],
        out_shape=[jax.ShapeDtypeStruct((rows, D), f32), jax.ShapeDtypeStruct((4 * D, D), bf16), jax.ShapeDtypeStruct((8, D), f32)],
        scratch_shapes=[pltpu.VMEM((4 * D, D), f32)],
        compiler_params=params(),
        name="att_bwd",
    )(dx1, x, qkv, att, w, gains, seg[:, None], seg.reshape(steps, 1, step_rows))


POS = 197
CLASSES = 1000
L = 3
IMG_SEQ = 6
STEP = 10
PART = 4 * D
WIDE = 3 * PART
clip_bound = 0.02
l2_weight = 0.1
beta_first = 0.5
beta_second = 0.5
adam_eps = 1e-08
weight_decay = 0.05
rate_matrix = 0.05
rate_vector = 0.5
ema_rate = 0.5
ALL = ("dp", "narrow")


def bits_of(size):
    return size.bit_length() - 1


def swap(rows, axis, mask):
    return lax.ppermute(rows, axis, [(i, i ^ mask) for i in range(lax.axis_size(axis))])


def add_low(left, right):
    return (left.astype(f32) + right.astype(f32)).astype(bf16)


def halve(rows, dim, axis, bit):
    half = rows.shape[dim] // 2
    mine = (lax.axis_index(axis) >> bit) & 1
    keep = lax.dynamic_slice_in_dim(rows, mine * half, half, dim)
    send = lax.dynamic_slice_in_dim(rows, (1 - mine) * half, half, dim)
    return add_low(keep, swap(send, axis, 1 << bit))


def sum_narrow(rows, dim):
    for bit in range(bits_of(lax.axis_size("narrow"))):
        rows = halve(rows, dim, "narrow", bit)
    return rows


def sum_dp(rows):
    for bit in range(bits_of(lax.axis_size("dp"))):
        rows = rows.reshape(rows.shape[0] // 2, 2, *rows.shape[1:])
        rows = halve(rows, 1, "dp", bit)
        rows = rows.reshape(rows.shape[0], *rows.shape[2:])
    return rows[0]


def join_narrow(piece):
    every = lax.all_gather(piece, "narrow", axis=0, tiled=False)
    size = every.shape[0]
    bits = bits_of(size)
    order = [int(format(i, "b").zfill(bits)[::-1], 2) for i in range(size)]
    return [every[i] for i in order]


def total_of(scalars):
    tile = jnp.zeros((8, 128), f32)
    for i, value in enumerate(scalars):
        tile = tile.at[0, i].set(value)
    world = lax.axis_size("dp") * lax.axis_size("narrow")
    every = lax.all_to_all(jnp.broadcast_to(tile[None], (world, 8, 128)), ALL, 0, 0)
    row = jnp.sum(every, axis=0)[0]
    return [row[i] for i in range(len(scalars))]


def adamw(weight, first, second, average, grad, rate, decay):
    first = beta_first * first + (1.0 - beta_first) * grad
    second = beta_second * second + (1.0 - beta_second) * grad * grad
    ahead = first / (1.0 - beta_first**STEP)
    behind = second / (1.0 - beta_second**STEP)
    weight = weight - rate * (ahead / (jnp.sqrt(behind) + adam_eps) + decay * weight)
    average = ema_rate * average + (1.0 - ema_rate) * weight
    return (weight, first, second, average, weight.astype(bf16))


def square_sum(arrays):
    return sum(jnp.sum(a.astype(f32) * a.astype(f32)) for a in arrays)


def shards(
    patches,
    pos_index,
    segments,
    cls_row,
    labels,
    img_count,
    embed_w,
    embed_m,
    embed_v,
    embed_e,
    vector_w,
    vector_m,
    vector_v,
    vector_e,
    mats_w,
    mats_m,
    mats_v,
    mats_e,
    rff_w,
    rff_m,
    rff_v,
    rff_e,
    read_w,
    read_m,
    read_v,
    read_e,
):
    n_dp, n_narrow = lax.axis_size("dp"), lax.axis_size("narrow")
    me_dp, me_narrow = lax.axis_index("dp"), lax.axis_index("narrow")
    own_dim = embed_w.shape[1]
    own_wide = mats_w.shape[2]
    group = math.gcd(own_wide, PART)
    groups = WIDE // group
    slots = cls_row.shape[0]
    table_rows = -(-(embed_w.shape[0] + vector_w.shape[0]) // 256) * 256
    chunk = table_rows // n_narrow

    image_total = total_of([jnp.sum(img_count).astype(f32)])[0]
    slot_ids = jnp.arange(slots)
    valid = (slot_ids % IMG_SEQ < jnp.repeat(img_count, IMG_SEQ, total_repeat_length=slots)).astype(jnp.int32)
    facts = lax.all_gather(jnp.stack([labels, valid]), "narrow", axis=0)
    group_labels = facts[:, 0].reshape(-1)
    group_valid = facts[:, 1].reshape(-1).astype(f32)[:, None]

    table = jnp.concatenate([embed_w.T, vector_w.T], axis=1).astype(bf16)
    table = jnp.pad(table, ((0, 0), (0, table_rows - table.shape[1])))
    table = lax.dynamic_slice_in_dim(table, me_narrow * chunk, chunk, 1)
    table = lax.all_gather(table, ALL, axis=0)
    table = table.reshape(n_dp, n_narrow, own_dim, chunk).transpose(0, 2, 1, 3).reshape(D, table_rows)
    quarter = own_wide // n_narrow
    mats_own = lax.dynamic_slice_in_dim(jnp.swapaxes(mats_w, 1, 2), me_narrow * quarter, quarter, 1)
    mats = lax.all_gather(mats_own.astype(bf16), ALL, axis=1, tiled=True).reshape(L * WIDE, D)
    first_vec = embed_w.shape[0]
    gains = table[:, first_vec : first_vec + vector_w.shape[0]].T.astype(f32)

    pad = -slots % 16
    cls = jnp.concatenate([cls_row, jnp.broadcast_to(cls_row[-1:], (pad,))])
    seg_cls = segments[cls]
    inputs, x0, qkv0, att0, mid0, x1 = first_forward(patches, pos_index, table, mats, 0, gains[0:4], segments)
    states = [(x0, qkv0, att0, mid0)]
    for layer in range(1, L - 1):
        qkv, att, mid, x2 = layer_forward(x1, mats, layer, gains[4 * layer : 4 * layer + 4], segments)
        states.append((x1, qkv, att, mid))
        x1 = x2
    last_gains = gains[4 * L - 4 :]
    kept = last_forward(cls, x1, mats, L - 1, last_gains, segments, seg_cls)
    features = kept[-1][:slots]

    rff_low = rff_w.astype(bf16)
    read_low = read_w.T.astype(bf16)
    group_rows = lax.all_gather(features, "narrow", axis=0, tiled=True)
    phases = nn(group_rows, rff_low)
    lifted = jnp.cos(phases).astype(bf16)
    partial = lax.all_gather(nt(lifted, read_low).astype(bf16), "narrow", axis=0)
    logits = jnp.sum(partial.astype(f32), axis=0)
    error = logits - (group_labels[:, None] == jnp.arange(CLASSES)[None, :]).astype(f32)
    error_sum = jnp.sum(group_valid * error * error)
    grad_logits = (2.0 * group_valid * error).astype(bf16)
    grad_phases = (-jnp.sin(phases) * nn(grad_logits, read_low)).astype(bf16)
    grad_pieces = nt(grad_phases, rff_low).reshape(n_narrow, slots, D)
    grad_features = jnp.sum(lax.all_to_all(grad_pieces, "narrow", 0, 0), axis=0)
    grad_features = jnp.pad(grad_features, ((0, pad), (0, 0)))

    own_logits = lax.dynamic_slice_in_dim(grad_logits, me_narrow * slots, slots, 0)
    every = lax.all_gather(jnp.concatenate([features, own_logits], axis=1), ALL, axis=0, tiled=True)
    all_features, all_logits = every[:, :D], every[:, D:]
    all_phases = nn(all_features, rff_low)
    all_lifted = jnp.cos(all_phases).astype(bf16)
    all_grad = (-jnp.sin(all_phases) * nn(all_logits, read_low)).astype(bf16)
    grad_read = tn(all_logits, all_lifted).T
    grad_rff = tn(all_features, all_grad)

    xs, cls_kept = x1, kept[:-1]
    grad_state, grad_last, vec_last = last_backward(cls, grad_features, xs, mats, L - 1, last_gains, segments, seg_cls, *cls_kept)
    sums = [None] * L
    sums[L - 1] = sum_dp(sum_narrow(grad_last.reshape(groups, group, D), 1).reshape(n_dp, -1, D))
    vecs = [vec_last[:6]]
    for layer in reversed(range(L - 1)):
        x, qkv, att, mid = states[layer]
        lg = gains[4 * layer : 4 * layer + 4]
        grad_mid, grad_mlp, vec_mlp = mlp_backward(grad_state, mid, mats, layer, lg)
        mlp_sum = sum_narrow(grad_mlp.reshape(-1, group, D), 1)
        grad_state, grad_att, vec_att = att_backward(grad_mid, x, qkv, att, mats, layer, lg, segments)
        att_sum = sum_narrow(grad_att.reshape(-1, group, D), 1)
        sums[layer] = sum_dp(jnp.concatenate([att_sum, mlp_sum]).reshape(n_dp, -1, D))
        vecs = [vec_att[:2], vec_mlp[:2]] + vecs
    vec = jnp.concatenate(vecs).T
    grad_table = tn(grad_state.astype(bf16), inputs)
    grad_table = grad_table + jnp.pad(vec, ((0, 0), (first_vec, table_rows - first_vec - vec.shape[1])))
    table_sum = sum_narrow(grad_table.astype(bf16), 1).reshape(n_dp, own_dim, chunk)
    table_sum = sum_dp(table_sum)

    scale = 1.0 / image_total
    read_step = grad_read * scale + 2.0 * l2_weight * read_w
    rff_step = grad_rff * scale
    first_dp = (me_dp == 0).astype(f32)
    first_narrow = (me_narrow == 0).astype(f32)
    local = square_sum([*sums, table_sum]) * (scale * scale)
    local = local + first_dp * square_sum([read_step, rff_step])
    ridge = first_dp * jnp.sum(read_w * read_w)
    total_square, error_total, ridge_total = total_of([local, first_narrow * error_sum, ridge])
    loss_sum = error_total + l2_weight * image_total * ridge_total
    clip_norm = jnp.sqrt(total_square)
    factor = jnp.minimum(1.0, clip_bound / clip_norm)

    rows = jnp.stack([s.reshape(-1, group // n_narrow, D) for s in sums])
    rows = jnp.stack(join_narrow(rows), axis=2).reshape(L, own_wide, D)
    grad_mats = jnp.swapaxes(rows, 1, 2).astype(f32) * scale
    lanes = jnp.concatenate(join_narrow(table_sum), axis=1).astype(f32) * scale
    grad_embed = lanes[:, :first_vec].T
    grad_vector = lanes[:, first_vec : first_vec + vector_w.shape[0]].T

    outs = [loss_sum, image_total, clip_norm]
    outs += adamw(embed_w, embed_m, embed_v, embed_e, grad_embed * factor, rate_matrix, weight_decay)
    outs += adamw(vector_w, vector_m, vector_v, vector_e, grad_vector * factor, rate_vector, 0.0)
    outs += adamw(mats_w, mats_m, mats_v, mats_e, grad_mats * factor, rate_matrix, weight_decay)
    outs += adamw(rff_w, rff_m, rff_v, rff_e, rff_step * factor, rate_matrix, weight_decay)
    outs += adamw(read_w, read_m, read_v, read_e, read_step * factor, rate_matrix, weight_decay)
    return tuple(outs)


def solution(mesh):
    rows = P(ALL)
    table, mats, rff, read = P(None, "dp"), P(None, None, "dp"), P(None, "narrow"), P("narrow", None)
    ins = (P(ALL, None),) + (rows,) * 5 + (table,) * 8 + (mats,) * 4 + (rff,) * 4 + (read,) * 4
    outs = (P(),) * 3 + (table,) * 10 + (mats,) * 5 + (rff,) * 5 + (read,) * 5
    return jax.shard_map(shards, mesh=mesh, in_specs=ins, out_specs=outs, check_vma=False)
```

```python
import functools
import math
import jax
import jax.numpy as jnp
from jax import lax
from jax.experimental import pallas as pl
from jax.experimental.pallas import tpu as pltpu
from jax.sharding import PartitionSpec as P

D = 384
HEADS = 6
HD = 64
MLP = 1536
SEQ = 256
norm_eps = 1e-06
GELU_A = 0.7978845608028654
GELU_B = 0.044715
f32 = jnp.float32
bf16 = jnp.bfloat16


def nn(a, b):
    return lax.dot_general(a, b, (((1,), (0,)), ((), ())), preferred_element_type=f32)


def nt(a, b):
    return lax.dot_general(a, b, (((1,), (1,)), ((), ())), preferred_element_type=f32)


def tn(a, b):
    return lax.dot_general(a, b, (((0,), (0,)), ((), ())), preferred_element_type=f32)


def unit(rows):
    centred = rows - jnp.mean(rows, axis=-1, keepdims=True)
    inverse = lax.rsqrt(jnp.mean(centred * centred, axis=-1, keepdims=True) + norm_eps)
    return centred * inverse, inverse


def unit_back(u, inverse, gain, grad):
    scaled = grad * gain
    return inverse * (
        scaled
        - jnp.mean(scaled, axis=-1, keepdims=True)
        - u * jnp.mean(scaled * u, axis=-1, keepdims=True)
    )


def gelu_parts(x):
    x2 = x * x
    t = jnp.tanh(GELU_A * x * (1.0 + GELU_B * x2))
    half = 0.5 * (1.0 + t)
    return half, t, x2


def gelu_value(x):
    half, _, _ = gelu_parts(x)
    return x * half


def gelu_both(x):
    half, t, x2 = gelu_parts(x)
    slope = half + 0.5 * x * (1.0 - t * t) * (GELU_A * (1.0 + 3.0 * GELU_B * x2))
    return x * half, slope


def layer_rows(x, wa_ref, wu_ref, wd_ref, gains, seg_col, seg_row):
    g1, b1, g2, b2 = (gains[i : i + 1, :] for i in range(4))
    u, _ = unit(x)
    normed = (u * g1 + b1).astype(bf16)
    qkv = nt(normed, wa_ref[: 3 * D, :]).astype(bf16)
    heads = []
    rows = x.shape[0]
    for s in range(rows // SEQ):
        r = slice(s * SEQ, (s + 1) * SEQ)
        same = seg_col[r, :] == seg_row[:, r]
        outs = []
        for h in range(HEADS):
            q = qkv[r, h * HD : (h + 1) * HD]
            k = qkv[r, D + h * HD : D + (h + 1) * HD]
            v = qkv[r, 2 * D + h * HD : 2 * D + (h + 1) * HD]
            sc = jnp.where(same, nt(q, k) * HD ** (-0.5), -1e30)
            e = jnp.exp(sc - jnp.max(sc, axis=-1, keepdims=True))
            p = (e * (1.0 / jnp.sum(e, axis=-1, keepdims=True))).astype(bf16)
            outs.append(nn(p, v))
        heads.append(jnp.concatenate(outs, axis=1))
    att = jnp.concatenate(heads, axis=0).astype(bf16)
    x1 = x + nt(att, wa_ref[3 * D :, :])
    u2, _ = unit(x1)
    second = (u2 * g2 + b2).astype(bf16)
    hidden = gelu_value(nt(second, wu_ref[...])).astype(bf16)
    out = x1 + nn(hidden, wd_ref[...])
    return qkv, att, x1, out


def fwd_kernel(x_ref, wa_ref, wu_ref, wd_ref, g_ref, sc_ref, sr_ref, qkv_ref, att_ref, x1_ref, out_ref):
    qkv, att, x1, out = layer_rows(x_ref[...], wa_ref, wu_ref, wd_ref, g_ref[...], sc_ref[...], sr_ref[0])
    qkv_ref[...] = qkv
    att_ref[...] = att
    x1_ref[...] = x1
    out_ref[...] = out


def first_kernel(p_ref, pos_ref, e_ref, wa_ref, wu_ref, wd_ref, g_ref, sc_ref, sr_ref, in_ref, x_ref, qkv_ref, att_ref, x1_ref, out_ref):
    pos = pos_ref[...]
    patch = jnp.where(pos != 0, p_ref[...].astype(f32), 0.0).astype(bf16)
    lanes = e_ref.shape[1] - p_ref.shape[1]
    table = (pos == lax.broadcasted_iota(jnp.int32, (pos.shape[0], lanes), 1)).astype(f32).astype(bf16)
    full = jnp.concatenate([patch, table], axis=1)
    in_ref[...] = full
    x = nt(full, e_ref[...])
    x_ref[...] = x
    qkv, att, x1, out = layer_rows(x, wa_ref, wu_ref, wd_ref, g_ref[...], sc_ref[...], sr_ref[0])
    qkv_ref[...] = qkv
    att_ref[...] = att
    x1_ref[...] = x1
    out_ref[...] = out


def rows_spec(r, width):
    return pl.BlockSpec((r, width), lambda i: (i, 0))


def whole_spec(shape):
    return pl.BlockSpec(shape, lambda *i: (0,) * len(shape))


def third_spec(block):
    return pl.BlockSpec((4 * D, D), lambda *i: (block, 0))


def params(mb=56, n=1):
    return pltpu.CompilerParams(dimension_semantics=("arbitrary",) * n, vmem_limit_bytes=mb << 20)


def lasting(us):
    return pl.CostEstimate(flops=int(us * 1e9), bytes_accessed=int(us * 2e6), transcendentals=0)


def layer_forward(x, w, layer, gains, seg, step_rows=512):
    rows = x.shape[0]
    steps = rows // step_rows
    return pl.pallas_call(
        fwd_kernel,
        grid=(steps,),
        in_specs=[
            rows_spec(step_rows, D),
            *(third_spec(3 * layer + i) for i in range(3)),
            whole_spec(gains.shape),
            rows_spec(step_rows, 1),
            pl.BlockSpec((1, 1, step_rows), lambda i: (i, 0, 0)),
        ],
        out_specs=[rows_spec(step_rows, 3 * D), rows_spec(step_rows, D), rows_spec(step_rows, D), rows_spec(step_rows, D)],
        out_shape=[
            jax.ShapeDtypeStruct((rows, 3 * D), bf16),
            jax.ShapeDtypeStruct((rows, D), bf16),
            jax.ShapeDtypeStruct((rows, D), f32),
            jax.ShapeDtypeStruct((rows, D), f32),
        ],
        compiler_params=params(),
        cost_estimate=lasting(17),
        name="layer_fwd",
    )(x, w, w, w, gains, seg[:, None], seg.reshape(steps, 1, step_rows))


def first_forward(patches, pos, e, w, layer, gains, seg, step_rows=512):
    rows, patch = patches.shape
    lanes = e.shape[1]
    steps = rows // step_rows
    return pl.pallas_call(
        first_kernel,
        grid=(steps,),
        in_specs=[
            rows_spec(step_rows, patch),
            rows_spec(step_rows, 1),
            whole_spec(e.shape),
            *(third_spec(3 * layer + i) for i in range(3)),
            whole_spec(gains.shape),
            rows_spec(step_rows, 1),
            pl.BlockSpec((1, 1, step_rows), lambda i: (i, 0, 0)),
        ],
        out_specs=[rows_spec(step_rows, lanes), rows_spec(step_rows, D), rows_spec(step_rows, 3 * D), rows_spec(step_rows, D), rows_spec(step_rows, D), rows_spec(step_rows, D)],
        out_shape=[
            jax.ShapeDtypeStruct((rows, lanes), bf16),
            jax.ShapeDtypeStruct((rows, D), f32),
            jax.ShapeDtypeStruct((rows, 3 * D), bf16),
            jax.ShapeDtypeStruct((rows, D), bf16),
            jax.ShapeDtypeStruct((rows, D), f32),
            jax.ShapeDtypeStruct((rows, D), f32),
        ],
        compiler_params=params(),
        cost_estimate=lasting(18),
        name="first_fwd",
    )(patches, pos[:, None], e, w, w, w, gains, seg[:, None], seg.reshape(steps, 1, step_rows))


def last_fwd_kernel(cls_ref, x_ref, wa_ref, wu_ref, wd_ref, g_ref, sk_ref, sq_ref, kv_ref, xc_ref, q_ref, att_ref, x1_ref, out_ref, feat_ref):
    g1, b1, g2, b2, g3, b3 = (g_ref[i : i + 1, :] for i in range(6))
    u, _ = unit(x_ref[...])
    normed = (u * g1 + b1).astype(bf16)
    kv = nt(normed, wa_ref[D : 3 * D, :]).astype(bf16)
    kv_ref[...] = kv
    slots = xc_ref.shape[0]
    for i in range(slots):
        xc_ref[i : i + 1, :] = x_ref[pl.ds(cls_ref[i], 1), :]
    xc = xc_ref[...]
    uc, _ = unit(xc)
    q = nt((uc * g1 + b1).astype(bf16), wa_ref[:D, :]).astype(bf16)
    q_ref[...] = q
    same = sq_ref[...] == sk_ref[...]
    outs = []
    for h in range(HEADS):
        c = slice(h * HD, (h + 1) * HD)
        sc = jnp.where(same, nt(q[:, c], kv[:, c]) * HD ** (-0.5), -1e30)
        e = jnp.exp(sc - jnp.max(sc, axis=-1, keepdims=True))
        p = (e * (1.0 / jnp.sum(e, axis=-1, keepdims=True))).astype(bf16)
        outs.append(nn(p, kv[:, D + h * HD : D + (h + 1) * HD]))
    att = jnp.concatenate(outs, axis=1).astype(bf16)
    att_ref[...] = att
    x1 = xc + nt(att, wa_ref[3 * D :, :])
    x1_ref[...] = x1
    u2, _ = unit(x1)
    second = (u2 * g2 + b2).astype(bf16)
    hidden = gelu_value(nt(second, wu_ref[...])).astype(bf16)
    out = x1 + nn(hidden, wd_ref[...])
    out_ref[...] = out
    u3, _ = unit(out)
    feat_ref[...] = (u3 * g3 + b3).astype(bf16)


def put_halves(core_ref, acc_ref, keep_ref, send_ref):
    half = keep_ref.shape[1]
    mine = core_ref[0] * half
    other = (1 - core_ref[0]) * half
    for i in range(keep_ref.shape[0]):
        base = i * 2 * half
        keep_ref[i] = acc_ref[pl.ds(base + mine, half), :].astype(bf16)
        send_ref[i] = acc_ref[pl.ds(base + other, half), :].astype(bf16)


def smem_spec():
    return pl.BlockSpec(memory_space=pltpu.SMEM)


def vmem_spec():
    return pl.BlockSpec(memory_space=pltpu.VMEM)


def last_forward(cls, x, w, layer, gains, seg, seg_cls):
    rows, slots = x.shape[0], cls.shape[0]
    return pl.pallas_call(
        last_fwd_kernel,
        grid=(1,),
        in_specs=[smem_spec(), whole_spec(x.shape), *(third_spec(3 * layer + i) for i in range(3)), *[vmem_spec()] * 3],
        out_specs=[vmem_spec()] * 7,
        out_shape=[
            jax.ShapeDtypeStruct((rows, 2 * D), bf16),
            jax.ShapeDtypeStruct((slots, D), f32),
            jax.ShapeDtypeStruct((slots, D), bf16),
            jax.ShapeDtypeStruct((slots, D), bf16),
            jax.ShapeDtypeStruct((slots, D), f32),
            jax.ShapeDtypeStruct((slots, D), f32),
            jax.ShapeDtypeStruct((slots, D), bf16),
        ],
        compiler_params=params(),
        cost_estimate=lasting(9),
        name="last_fwd",
    )(cls, x, w, w, w, gains, seg[None, :], seg_cls[:, None])


def last_bwd_kernel(cls_ref, core_ref, df_ref, x_ref, wa_ref, wu_ref, wd_ref, g_ref, sk_ref, sq_ref, kv_ref, xc_ref, q_ref, att_ref, x1_ref, xo_ref, dx_ref, keep_ref, send_ref, dv_ref, dn_ref, dw_ref):
    g1, b1, g2, b2, g3, b3 = (g_ref[i : i + 1, :] for i in range(6))
    slots = xc_ref.shape[0]
    df = df_ref[...]
    u3, i3 = unit(xo_ref[...])
    dxo = unit_back(u3, i3, g3, df)
    dg3 = jnp.sum(df * u3, axis=0, keepdims=True)
    db3 = jnp.sum(df, axis=0, keepdims=True)
    branch = dxo.astype(bf16)
    u2, i2 = unit(x1_ref[...])
    second = (u2 * g2 + b2).astype(bf16)
    value, slope = gelu_both(nt(second, wu_ref[...]))
    dpre = (nt(branch, wd_ref[...]) * slope).astype(bf16)
    dw_ref[4 * D + MLP :, :] = tn(value.astype(bf16), branch)
    dw_ref[4 * D : 4 * D + MLP, :] = tn(dpre, second)
    dsecond = nn(dpre, wu_ref[...])
    dg2 = jnp.sum(dsecond * u2, axis=0, keepdims=True)
    db2 = jnp.sum(dsecond, axis=0, keepdims=True)
    dx1 = dxo + unit_back(u2, i2, g2, dsecond)
    ab = dx1.astype(bf16)
    datt = nn(ab, wa_ref[3 * D :, :]).astype(bf16)
    dw_ref[3 * D : 4 * D, :] = tn(ab, att_ref[...])
    same = sq_ref[...] == sk_ref[...]
    q, kv = q_ref[...], kv_ref[...]
    dqs, dks, dvs = [], [], []
    for h in range(HEADS):
        c = slice(h * HD, (h + 1) * HD)
        k, v = kv[:, c], kv[:, D + h * HD : D + (h + 1) * HD]
        sc = jnp.where(same, nt(q[:, c], k) * HD ** (-0.5), -1e30)
        e = jnp.exp(sc - jnp.max(sc, axis=-1, keepdims=True))
        p = e * (1.0 / jnp.sum(e, axis=-1, keepdims=True))
        dp = nt(datt[:, c], v)
        ds = (p * (dp - jnp.sum(dp * p, axis=-1, keepdims=True))).astype(bf16)
        dvs.append(tn(p.astype(bf16), datt[:, c]))
        dks.append(tn(ds, q[:, c]) * HD ** (-0.5))
        dqs.append(nn(ds, k) * HD ** (-0.5))
    dq = jnp.concatenate(dqs, axis=1).astype(bf16)
    dkv = jnp.concatenate(dks + dvs, axis=1).astype(bf16)
    u, i1 = unit(x_ref[...])
    normed = (u * g1 + b1).astype(bf16)
    dw_ref[D : 3 * D, :] = tn(dkv, normed)
    uc, _ = unit(xc_ref[...])
    dw_ref[:D, :] = tn(dq, (uc * g1 + b1).astype(bf16))
    dn_ref[...] = nn(dkv, wa_ref[D : 3 * D, :])
    dnc = nn(dq, wa_ref[:D, :])
    for i in range(slots):
        at = pl.ds(cls_ref[i], 1)
        dn_ref[at, :] = dn_ref[at, :] + dnc[i : i + 1, :]
    dn = dn_ref[...]
    dg1 = jnp.sum(dn * u, axis=0, keepdims=True)
    db1 = jnp.sum(dn, axis=0, keepdims=True)
    dx_ref[...] = unit_back(u, i1, g1, dn)
    for i in range(slots):
        at = pl.ds(cls_ref[i], 1)
        dx_ref[at, :] = dx_ref[at, :] + dx1[i : i + 1, :]
    dv_ref[...] = jnp.concatenate([dg1, db1, dg2, db2, dg3, db3, jnp.zeros((2, D), f32)], axis=0)
    put_halves(core_ref, dw_ref, keep_ref, send_ref)


def last_backward(cls, core, wide, df, x, w, layer, gains, seg, seg_cls, kv, xc, q, att, x1, xo):
    rows = x.shape[0]
    return pl.pallas_call(
        last_bwd_kernel,
        grid=(1,),
        in_specs=[smem_spec(), smem_spec(), vmem_spec(), whole_spec(x.shape), *(third_spec(3 * layer + i) for i in range(3)), *[vmem_spec()] * 9],
        out_specs=[vmem_spec()] * 4,
        out_shape=[
            jax.ShapeDtypeStruct((rows, D), f32),
            *[jax.ShapeDtypeStruct((12 * D // wide, wide // 2, D), bf16)] * 2,
            jax.ShapeDtypeStruct((8, D), f32),
        ],
        scratch_shapes=[pltpu.VMEM((rows, D), f32), pltpu.VMEM((12 * D, D), f32)],
        compiler_params=params(),
        cost_estimate=lasting(15),
        name="last_bwd",
    )(cls, core, df, x, w, w, w, gains, seg[None, :], seg_cls[:, None], kv, xc, q, att, x1, xo)


def mlp_bwd_kernel(core_ref, dxo_ref, x1_ref, att_ref, wu_ref, wd_ref, g_ref, dx1_ref, keep_ref, send_ref, dv_ref, acc_ref):
    step = pl.program_id(0)
    g2, b2 = g_ref[2:3, :], g_ref[3:4, :]
    dxo = dxo_ref[...]
    branch = dxo.astype(bf16)
    u2, i2 = unit(x1_ref[...])
    second = (u2 * g2 + b2).astype(bf16)
    value, slope = gelu_both(nt(second, wu_ref[...]))
    hidden = value.astype(bf16)
    dpre = (nt(branch, wd_ref[...]) * slope).astype(bf16)
    dsecond = nn(dpre, wu_ref[...])
    sums = jnp.concatenate([jnp.sum(dsecond * u2, axis=0, keepdims=True), jnp.sum(dsecond, axis=0, keepdims=True), jnp.zeros((6, D), f32)], axis=0)
    dx1 = dxo + unit_back(u2, i2, g2, dsecond)
    dx1_ref[...] = dx1
    ab = dx1.astype(bf16)
    last = pl.num_programs(0) - 1

    @pl.when(step == 0)
    def _():
        acc_ref[:D, :] = tn(ab, att_ref[...])
        acc_ref[D : D + MLP, :] = tn(dpre, second)
        acc_ref[D + MLP :, :] = tn(hidden, branch)
        dv_ref[...] = sums

    @pl.when(step > 0)
    def _():
        acc_ref[:D, :] += tn(ab, att_ref[...])
        acc_ref[D : D + MLP, :] += tn(dpre, second)
        acc_ref[D + MLP :, :] += tn(hidden, branch)
        dv_ref[...] += sums

    @pl.when(step == last)
    def _():
        put_halves(core_ref, acc_ref, keep_ref, send_ref)


def mlp_backward(core, wide, dxo, x1, att, w, layer, gains, step_rows=512):
    rows = x1.shape[0]
    steps = rows // step_rows
    return pl.pallas_call(
        mlp_bwd_kernel,
        grid=(steps,),
        in_specs=[smem_spec(), *[rows_spec(step_rows, D)] * 3, third_spec(3 * layer + 1), third_spec(3 * layer + 2), whole_spec(gains.shape)],
        out_specs=[rows_spec(step_rows, D), *[whole_spec((9 * D // wide, wide // 2, D))] * 2, whole_spec((8, D))],
        out_shape=[jax.ShapeDtypeStruct((rows, D), f32), *[jax.ShapeDtypeStruct((9 * D // wide, wide // 2, D), bf16)] * 2, jax.ShapeDtypeStruct((8, D), f32)],
        scratch_shapes=[pltpu.VMEM((9 * D, D), f32)],
        compiler_params=params(),
        cost_estimate=lasting(16),
        name="mlp_bwd",
    )(core, dxo, x1, att, w, w, gains)


def att_bwd_kernel(first_vec, *refs):
    core_ref, dx1_ref, x_ref, qkv_ref, w_ref, g_ref, sc_ref, sr_ref, *refs = refs
    if first_vec:
        in_ref, vec_ref, keep_ref, send_ref, tkeep_ref, tsend_ref, acc_ref, dv_ref, table_ref = refs
    else:
        dx_ref, keep_ref, send_ref, dv_ref, acc_ref = refs
    step = pl.program_id(0)
    g1, b1 = g_ref[0:1, :], g_ref[1:2, :]
    dx1 = dx1_ref[...]
    ab = dx1.astype(bf16)
    datt = nn(ab, w_ref[3 * D : 4 * D, :]).astype(bf16)
    qkv = qkv_ref[...]
    parts = []
    for s in range(x_ref.shape[0] // SEQ):
        r = slice(s * SEQ, (s + 1) * SEQ)
        same = sc_ref[r, :] == sr_ref[0][:, r]
        dqs, dks, dvs = [], [], []
        for h in range(HEADS):
            q = qkv[r, h * HD : (h + 1) * HD]
            k = qkv[r, D + h * HD : D + (h + 1) * HD]
            v = qkv[r, 2 * D + h * HD : 2 * D + (h + 1) * HD]
            da = datt[r, h * HD : (h + 1) * HD]
            sc = jnp.where(same, nt(k, q) * HD ** (-0.5), -1e30)
            e = jnp.exp(sc - jnp.max(sc, axis=0, keepdims=True))
            p = e * (1.0 / jnp.sum(e, axis=0, keepdims=True))
            dp = nt(v, da)
            ds = (p * (dp - jnp.sum(dp * p, axis=0, keepdims=True))).astype(bf16)
            dvs.append(nn(p.astype(bf16), da))
            dks.append(nn(ds, q) * HD ** (-0.5))
            dqs.append(tn(ds, k) * HD ** (-0.5))
        parts.append(jnp.concatenate(dqs + dks + dvs, axis=1).astype(bf16))
    dqkv = jnp.concatenate(parts, axis=0)
    u, i1 = unit(x_ref[...])
    normed = (u * g1 + b1).astype(bf16)
    dn = nn(dqkv, w_ref[: 3 * D, :])
    sums = jnp.concatenate([jnp.sum(dn * u, axis=0, keepdims=True), jnp.sum(dn, axis=0, keepdims=True), jnp.zeros((6, D), f32)], axis=0)
    dx = dx1 + unit_back(u, i1, g1, dn)
    if first_vec:
        grad_table = tn(dx.astype(bf16), in_ref[...])
    else:
        dx_ref[...] = dx
    last = pl.num_programs(0) - 1

    @pl.when(step == 0)
    def _():
        acc_ref[...] = tn(dqkv, normed)
        if first_vec:
            table_ref[...] = grad_table
        dv_ref[...] = sums

    @pl.when(step > 0)
    def _():
        acc_ref[...] += tn(dqkv, normed)
        if first_vec:
            table_ref[...] += grad_table
        dv_ref[...] += sums

    @pl.when(step == last)
    def _():
        put_halves(core_ref, acc_ref, keep_ref, send_ref)
        if first_vec:
            rows, lanes = vec_ref.shape[0], table_ref.shape[1]
            vec = vec_ref[...] + jnp.concatenate([dv_ref[...], jnp.zeros((rows - 8, D), f32)], axis=0)
            at = lax.broadcasted_iota(jnp.int32, (rows, lanes), 1) - first_vec
            pick = (at == lax.broadcasted_iota(jnp.int32, (rows, lanes), 0)).astype(f32).astype(bf16)
            table_ref[...] += tn(vec.astype(bf16), pick)
            half = lanes // 2
            mine = pl.multiple_of(core_ref[0] * half, 128)
            other = pl.multiple_of((1 - core_ref[0]) * half, 128)
            tkeep_ref[...] = table_ref[:, pl.ds(mine, half)].astype(bf16)
            tsend_ref[...] = table_ref[:, pl.ds(other, half)].astype(bf16)


def att_backward(core, wide, dx1, x, qkv, w, layer, gains, seg, table=None, step_rows=512):
    rows = x.shape[0]
    steps = rows // step_rows
    parts = [jax.ShapeDtypeStruct((3 * D // wide, wide // 2, D), bf16)] * 2
    whole = [whole_spec(p.shape) for p in parts]
    acc = pltpu.VMEM((3 * D, D), f32)
    if table is None:
        first_vec, more, more_specs = 0, (), []
        out_specs = [rows_spec(step_rows, D), *whole, whole_spec((8, D))]
        out_shape = [jax.ShapeDtypeStruct((rows, D), f32), *parts, jax.ShapeDtypeStruct((8, D), f32)]
        scratch = [acc]
    else:
        first_vec, inputs, vec = table
        lanes = inputs.shape[1]
        more, more_specs = (inputs, vec), [rows_spec(step_rows, lanes), whole_spec(vec.shape)]
        out_shape = [*parts, *[jax.ShapeDtypeStruct((D, lanes // 2), bf16)] * 2]
        out_specs = [whole_spec(p.shape) for p in out_shape]
        scratch = [acc, pltpu.VMEM((8, D), f32), pltpu.VMEM((D, lanes), f32)]
    return pl.pallas_call(
        functools.partial(att_bwd_kernel, first_vec),
        grid=(steps,),
        in_specs=[
            smem_spec(),
            rows_spec(step_rows, D),
            rows_spec(step_rows, D),
            rows_spec(step_rows, 3 * D),
            third_spec(3 * layer),
            whole_spec(gains.shape),
            rows_spec(step_rows, 1),
            pl.BlockSpec((1, 1, step_rows), lambda i: (i, 0, 0)),
            *more_specs,
        ],
        out_specs=out_specs,
        out_shape=out_shape,
        scratch_shapes=scratch,
        compiler_params=params(),
        cost_estimate=lasting(18),
        name="att_bwd",
    )(core, dx1, x, qkv, w, gains, seg[:, None], seg.reshape(steps, 1, step_rows), *more)


HALF_PI = (1.5703125, 0.000483751296996, 7.54978995489e-08, 5.1266913e-12)


def sin_cos(x):
    k = jnp.round(x * 0.6366197723675814)
    r = x
    for part in HALF_PI:
        r = r - k * part
    r = jnp.clip(r, -1.0, 1.0)
    r2 = r * r
    s = r + r * r2 * (-1.6666654611e-1 + r2 * (8.3321608736e-3 + r2 * -1.9515295891e-4))
    c = 1.0 - 0.5 * r2 + r2 * r2 * (4.166664568298827e-2 + r2 * (-1.388731625493765e-3 + r2 * 2.443315711809948e-5))
    n = k.astype(jnp.int32)
    odd = (n & 1) == 1
    sin_v = jnp.where(odd, c, s)
    cos_v = jnp.where(odd, s, c)
    sin_v = jnp.where((n & 2) == 2, -sin_v, sin_v)
    cos_v = jnp.where(((n + 1) & 2) == 2, -cos_v, cos_v)
    return sin_v, cos_v


def head_kernel(several, s_ref, all_ref, rff_ref, read_ref, w_ref, gread_ref, grff_ref, sums_ref, sin_ref, cos_ref):
    features = all_ref[:, :D]
    logits = all_ref[:, D:]
    phases = nn(features, rff_ref[...])
    large = jnp.max(jnp.abs(phases)) > 5e4

    @pl.when(large)
    def _():
        sin_ref[...] = jnp.sin(phases)
        cos_ref[...] = jnp.cos(phases)

    @pl.when(jnp.logical_not(large))
    def _():
        sin_ref[...], cos_ref[...] = sin_cos(phases)

    lifted = cos_ref[...].astype(bf16)
    back = (-sin_ref[...] * nn(logits, read_ref[...])).astype(bf16)
    blocks = pl.num_programs(1)
    gread = tn(logits, lifted)
    grff = tn(features, back)
    if several:
        block = pl.program_id(1)

        @pl.when(block == 0)
        def _():
            gread_ref[...] = gread
            grff_ref[...] = grff

        @pl.when(block > 0)
        def _():
            gread_ref[...] += gread
            grff_ref[...] += grff

        @pl.when(block == blocks - 1)
        def _():
            head_finish(s_ref, w_ref, gread_ref[...], grff_ref[...], gread_ref, grff_ref, sums_ref)
    else:
        head_finish(s_ref, w_ref, gread, grff, gread_ref, grff_ref, sums_ref)


def head_finish(s_ref, w_ref, gread, grff, gread_ref, grff_ref, sums_ref):
    step = pl.program_id(0)
    w = w_ref[...]
    gread = gread * s_ref[0] + 2.0 * l2_weight * w
    grff = grff * s_ref[0]
    gread_ref[...] = gread
    grff_ref[...] = grff
    total = jnp.sum(jnp.sum(gread * gread, axis=0, keepdims=True)) + jnp.sum(jnp.sum(grff * grff, axis=0, keepdims=True))
    ridge = jnp.sum(jnp.sum(w * w, axis=0, keepdims=True))
    row = lax.broadcasted_iota(jnp.int32, (8, 128), 0)
    tile = jnp.where(row == 0, total, jnp.where(row == 1, ridge, 0.0))

    @pl.when(step == 0)
    def _():
        sums_ref[...] = tile

    @pl.when(step > 0)
    def _():
        sums_ref[...] += tile


def head_backward(scale, every, rff, read, w, cols=256):
    n, classes = every.shape[0], read.shape[0]
    width = rff.shape[1]
    cols = min(cols, width)
    rows = math.gcd(n, 768)
    col = lambda r: pl.BlockSpec((r, cols), lambda i, j: (0, i))
    return pl.pallas_call(
        functools.partial(head_kernel, n > rows),
        grid=(width // cols, n // rows),
        in_specs=[smem_spec(), pl.BlockSpec((rows, every.shape[1]), lambda i, j: (j, 0)), col(D), col(classes), col(classes)],
        out_specs=[col(classes), col(D), whole_spec((8, 128))],
        out_shape=[jax.ShapeDtypeStruct((classes, width), f32), jax.ShapeDtypeStruct((D, width), f32), jax.ShapeDtypeStruct((8, 128), f32)],
        scratch_shapes=[pltpu.VMEM((rows, cols), f32)] * 2,
        compiler_params=params(56, 2),
        cost_estimate=lasting(12),
        name="head_bwd",
    )(scale, every, rff, read, w)


POS = 197
CLASSES = 1000
L = 3
IMG_SEQ = 6
STEP = 10
PART = 4 * D
WIDE = 3 * PART
clip_bound = 0.02
l2_weight = 0.1
beta_first = 0.5
beta_second = 0.5
adam_eps = 1e-08
weight_decay = 0.05
rate_matrix = 0.05
rate_vector = 0.5
ema_rate = 0.5
DP = ("dph", "dpl")
NARROW = ("ny", "nc")
ALL = DP + NARROW


def swap(rows, axis, mask):
    return lax.ppermute(rows, axis, [(i, i ^ mask) for i in range(lax.axis_size(axis))])


def add_up(terms):
    return sum(t.astype(f32) for t in terms)


def bits_of(size):
    return size.bit_length() - 1


class Slab:
    def __init__(self, terms):
        self.terms = terms

    def hop(self, dim, axis, bit=0):
        half = self.terms[0].shape[dim] // 2
        mine = (lax.axis_index(axis) >> bit) & 1
        send = add_up([lax.dynamic_slice_in_dim(t, (1 - mine) * half, half, dim) for t in self.terms])
        self.terms = [lax.dynamic_slice_in_dim(t, mine * half, half, dim) for t in self.terms]
        return swap(send.astype(bf16), axis, 1 << bit)

    def hops_y(self, dim):
        bits = bits_of(lax.axis_size("ny"))
        for bit in range(bits - 1):
            self.terms.append(self.hop(dim, "ny", bit))
        return self.hop(dim, "ny", bits - 1)

    def hop_x(self):
        self.terms = [t.reshape(t.shape[0] // 2, 2, *t.shape[1:]) for t in self.terms]
        got = self.hop(1, "dpl")
        self.terms = [t.reshape(t.shape[0], *t.shape[2:]) for t in self.terms]
        return got.reshape(got.shape[0], *got.shape[2:])

    def low(self):
        return add_up(self.terms).astype(bf16)


def spread(rows):
    return lax.all_to_all(rows, "dph", 0, 0)


def join_narrow(piece):
    every = lax.all_gather(piece, NARROW, axis=0, tiled=False)
    cores, ys = lax.axis_size("nc"), lax.axis_size("ny")
    bits = bits_of(ys)
    flip = [int(format(i, "b").zfill(bits)[::-1], 2) for i in range(ys)]
    return [every[flip[y] * cores + core] for core in range(cores) for y in range(ys)]


def total_of(scalars):
    lane = lax.broadcasted_iota(jnp.int32, (8, 128), 1)
    tile = jnp.zeros((8, 128), f32)
    for i, value in enumerate(scalars):
        tile = jnp.where(lane == i, value, tile)
    world = lax.axis_size(ALL)
    every = lax.all_to_all(jnp.broadcast_to(tile[None], (world, 8, 128)), ALL, 0, 0)
    row = jnp.sum(every, axis=0)[0]
    return [row[i] for i in range(len(scalars))]


def adamw(weight, first, second, average, grad, rate, decay):
    first = beta_first * first + (1.0 - beta_first) * grad
    second = beta_second * second + (1.0 - beta_second) * grad * grad
    ahead = first / (1.0 - beta_first**STEP)
    behind = second / (1.0 - beta_second**STEP)
    weight = weight - rate * (ahead / (jnp.sqrt(behind) + adam_eps) + decay * weight)
    average = ema_rate * average + (1.0 - ema_rate) * weight
    return (weight, first, second, average, weight.astype(bf16))


def square_sum(arrays):
    return sum(jnp.sum(a.astype(f32) * a.astype(f32)) for a in arrays)


def shards(
    patches,
    pos_index,
    segments,
    cls_row,
    labels,
    img_count,
    embed_w,
    embed_m,
    embed_v,
    embed_e,
    vector_w,
    vector_m,
    vector_v,
    vector_e,
    mats_w,
    mats_m,
    mats_v,
    mats_e,
    rff_w,
    rff_m,
    rff_v,
    rff_e,
    read_w,
    read_m,
    read_v,
    read_e,
):
    n_dp, n_narrow = lax.axis_size(DP), lax.axis_size(NARROW)
    me_dp, me_narrow = lax.axis_index(DP), lax.axis_index(NARROW)
    own_dim = embed_w.shape[1]
    own_wide = mats_w.shape[2]
    core = lax.axis_index("nc").astype(jnp.int32).reshape(1)
    slots = cls_row.shape[0]
    table_rows = -(-(embed_w.shape[0] + vector_w.shape[0]) // 256) * 256
    chunk = table_rows // n_narrow

    image_total = total_of([jnp.sum(img_count).astype(f32)])[0]
    slot_ids = jnp.arange(slots)
    valid = (slot_ids % IMG_SEQ < jnp.repeat(img_count, IMG_SEQ, total_repeat_length=slots)).astype(jnp.int32)
    facts = lax.all_gather(jnp.stack([labels, valid]), NARROW, axis=0)
    group_labels = facts[:, 0].reshape(-1)
    group_valid = facts[:, 1].reshape(-1).astype(f32)[:, None]

    table = jnp.concatenate([embed_w.T, vector_w.T], axis=1).astype(bf16)
    table = jnp.pad(table, ((0, 0), (0, table_rows - table.shape[1])))
    table = lax.dynamic_slice_in_dim(table, me_narrow * chunk, chunk, 1)
    table = lax.all_gather(table, ALL, axis=0)
    table = table.reshape(n_dp, n_narrow, own_dim, chunk).transpose(0, 2, 1, 3).reshape(D, table_rows)
    quarter = own_wide // n_narrow
    mats_own = lax.dynamic_slice_in_dim(jnp.swapaxes(mats_w, 1, 2), me_narrow * quarter, quarter, 1)
    mats = lax.all_gather(mats_own.astype(bf16), ALL, axis=1, tiled=True).reshape(L * WIDE, D)
    first_vec = embed_w.shape[0]
    gains = table[:, first_vec : first_vec + vector_w.shape[0]].T.astype(f32)

    pad = -slots % 16
    cls = jnp.concatenate([cls_row, jnp.broadcast_to(cls_row[-1:], (pad,))])
    seg_cls = segments[cls]
    inputs, x0, qkv0, att0, mid0, x1 = first_forward(patches, pos_index, table, mats, 0, gains[0:4], segments)
    states = [(x0, qkv0, att0, mid0)]
    for layer in range(1, L - 1):
        qkv, att, mid, x2 = layer_forward(x1, mats, layer, gains[4 * layer : 4 * layer + 4], segments)
        states.append((x1, qkv, att, mid))
        x1 = x2
    last_gains = gains[4 * L - 4 :]
    kept = last_forward(cls, x1, mats, L - 1, last_gains, segments, seg_cls)
    features = kept[-1][:slots]

    rff_low = rff_w.astype(bf16)
    read_low = read_w.T.astype(bf16)
    group_rows = lax.all_gather(features, NARROW, axis=0, tiled=True)
    phases = nn(group_rows, rff_low)
    lifted = jnp.cos(phases).astype(bf16)
    partial = lax.all_gather(nt(lifted, read_low).astype(bf16), NARROW, axis=0)
    logits = jnp.sum(partial.astype(f32), axis=0)
    error = logits - (group_labels[:, None] == jnp.arange(CLASSES)[None, :]).astype(f32)
    error_sum = jnp.sum(group_valid * error * error)
    grad_logits = (2.0 * group_valid * error).astype(bf16)
    grad_phases = (-jnp.sin(phases) * nn(grad_logits, read_low)).astype(bf16)
    grad_pieces = nt(grad_phases, rff_low).reshape(n_narrow, slots, D)
    grad_features = jnp.sum(lax.all_to_all(grad_pieces, NARROW, 0, 0), axis=0)
    grad_features = jnp.pad(grad_features, ((0, pad), (0, 0)))

    own_logits = lax.dynamic_slice_in_dim(grad_logits, me_narrow * slots, slots, 0)
    every = lax.all_gather(jnp.concatenate([features, own_logits], axis=1), ALL, axis=0, tiled=True)
    scale = 1.0 / image_total

    tie = lax.optimization_barrier
    state, keep, send, vec = last_backward(cls, core, own_wide, grad_features, x1, mats, L - 1, last_gains, segments, seg_cls, *kept[:-1])
    vecs = [vec[:6]]
    whole = Slab([keep])
    done = {}
    flight = {(L - 1, "c"): (whole, swap(send, "nc", 1))}
    parts = {}

    def land(outs):
        keys = list(flight)
        outs, got = tie((outs, [flight[k][1] for k in keys]))
        for (name, at), g in zip(keys, got):
            slab = flight.pop((name, at))[0]
            slab.terms.append(g)
            if at == "c":
                flight[(name, "y")] = (slab, slab.hops_y(2 if name == "table" else 1))
            elif at == "y":
                flight[(name, "x")] = (slab, slab.hop_x())
            else:
                parts[name] = slab.low()
                if name == L - 1:
                    done[name] = spread(parts[name])
                elif name == (1, "a"):
                    done[1] = spread(jnp.concatenate([parts[(1, "a")], parts[(1, "m")]]))
        return outs

    for layer in reversed(range(L - 1)):
        x, qkv, att, mid = states[layer]
        lg = gains[4 * layer : 4 * layer + 4]
        outs = mlp_backward(core, own_wide, state, mid, att, mats, layer, lg)
        grad_mid, keep, send, vec_mlp = land(outs)
        flight[((layer, "m"), "c")] = (Slab([keep]), swap(send, "nc", 1))
        if layer:
            outs = att_backward(core, own_wide, grad_mid, x, qkv, mats, layer, lg, segments)
            state, keep, send, vec_att = land(outs)
            vecs = [vec_att[:2], vec_mlp[:2]] + vecs
        else:
            vec = jnp.concatenate([jnp.zeros((2, D), f32), vec_mlp[:2]] + vecs)
            vec = jnp.pad(vec, ((0, -vec.shape[0] % 16), (0, 0)))
            outs = att_backward(core, own_wide, grad_mid, x, qkv, mats, layer, lg, segments, (first_vec, inputs, vec))
            keep, send, tkeep, tsend = land(outs)
            tkeep = tkeep.reshape(n_dp, own_dim, -1)
            flight[("table", "c")] = (Slab([tkeep]), swap(tsend.reshape(tkeep.shape), "nc", 1))
        flight[((layer, "a"), "c")] = (Slab([keep]), swap(send, "nc", 1))
    read_step, rff_step, head_sums = land(head_backward(scale.reshape(1), every, rff_low, read_low, read_w.T))
    while flight:
        land(())
    side = parts["table"].reshape(n_dp // 2, -1, D)
    both = spread(jnp.concatenate([jnp.concatenate([parts[(0, "a")], parts[(0, "m")]]), side], axis=1))
    cut = own_wide // n_narrow
    sums = jnp.concatenate([add_up(list(both)), *(add_up(list(done[i])) for i in range(1, L))])

    first_dp = (me_dp == 0).astype(f32)
    first_narrow = (me_narrow == 0).astype(f32)
    local = square_sum([sums]) * (scale * scale)
    local = local + first_dp * head_sums[0, 0]
    ridge = first_dp * head_sums[1, 0]
    total_square, error_total, ridge_total = total_of([local, first_narrow * error_sum, ridge])
    loss_sum = error_total + l2_weight * image_total * ridge_total
    clip_norm = jnp.sqrt(total_square)
    factor = jnp.minimum(1.0, clip_bound / clip_norm)

    shares = join_narrow(sums.astype(bf16))
    starts = [0, cut + side.shape[1], 2 * cut + side.shape[1]]
    rows = jnp.stack([jnp.concatenate([s[a : a + cut] for s in shares]) for a in starts])
    grad_mats = jnp.swapaxes(rows, 1, 2).astype(f32) * scale
    lanes = jnp.concatenate([s[cut : starts[1]].reshape(own_dim, chunk) for s in shares], axis=1).astype(f32) * scale
    grad_embed = lanes[:, :first_vec].T
    grad_vector = lanes[:, first_vec : first_vec + vector_w.shape[0]].T

    outs = [loss_sum, image_total, clip_norm]
    outs += adamw(embed_w, embed_m, embed_v, embed_e, grad_embed * factor, rate_matrix, weight_decay)
    outs += adamw(vector_w, vector_m, vector_v, vector_e, grad_vector * factor, rate_vector, 0.0)
    outs += adamw(mats_w, mats_m, mats_v, mats_e, grad_mats * factor, rate_matrix, weight_decay)
    outs += adamw(rff_w, rff_m, rff_v, rff_e, rff_step * factor, rate_matrix, weight_decay)
    outs += adamw(read_w, read_m, read_v, read_e, read_step.T * factor, rate_matrix, weight_decay)
    return tuple(outs)


def solution(mesh):
    n_dp, n_narrow = mesh.shape["dp"], mesh.shape["narrow"]
    fine = jax.sharding.Mesh(mesh.devices.reshape(n_dp // 2, 2, n_narrow // 2, 2), ALL)
    rows = P(ALL)
    table, mats, rff, read = P(None, DP), P(None, None, DP), P(None, NARROW), P(NARROW, None)
    ins = (P(ALL, None),) + (rows,) * 5 + (table,) * 8 + (mats,) * 4 + (rff,) * 4 + (read,) * 4
    outs = (P(),) * 3 + (table,) * 10 + (mats,) * 5 + (rff,) * 5 + (read,) * 5
    return jax.shard_map(shards, mesh=fine, in_specs=ins, out_specs=outs, check_vma=False)
```

```python
import functools
import math
import jax
import jax.numpy as jnp
from jax import lax
from jax.experimental import pallas as pl
from jax.experimental.pallas import tpu as pltpu
from jax.sharding import PartitionSpec as P

D = 384
HEADS = 6
HD = 64
MLP = 1536
SEQ = 256
norm_eps = 1e-06
EXP_SCALE = 1.4426950408889634 * HD ** (-0.5)
GELU_A = 0.7978845608028654
GELU_B = 0.044715
f32 = jnp.float32
bf16 = jnp.bfloat16


def nn(a, b):
    return lax.dot_general(a, b, (((1,), (0,)), ((), ())), preferred_element_type=f32)


def nt(a, b):
    return lax.dot_general(a, b, (((1,), (1,)), ((), ())), preferred_element_type=f32)


def tn(a, b):
    return lax.dot_general(a, b, (((0,), (0,)), ((), ())), preferred_element_type=f32)


def unit(rows):
    centred = rows - jnp.mean(rows, axis=-1, keepdims=True)
    inverse = lax.rsqrt(jnp.mean(centred * centred, axis=-1, keepdims=True) + norm_eps)
    return centred * inverse, inverse


def unit_back(u, inverse, gain, grad):
    scaled = grad * gain
    return inverse * (
        scaled
        - jnp.mean(scaled, axis=-1, keepdims=True)
        - u * jnp.mean(scaled * u, axis=-1, keepdims=True)
    )


def gelu_parts(x):
    x2 = x * x
    t = jnp.tanh(GELU_A * x * (1.0 + GELU_B * x2))
    half = 0.5 * (1.0 + t)
    return half, t, x2


def gelu_value(x):
    half, _, _ = gelu_parts(x)
    return x * half


def gelu_both(x):
    half, t, x2 = gelu_parts(x)
    slope = half + 0.5 * x * (1.0 - t * t) * (GELU_A * (1.0 + 3.0 * GELU_B * x2))
    return x * half, slope


def layer_rows(x, wa_ref, wu_ref, wd_ref, gains, seg_col, seg_row):
    g1, b1, g2, b2 = (gains[i : i + 1, :] for i in range(4))
    u, _ = unit(x)
    normed = (u * g1 + b1).astype(bf16)
    qkv = nt(normed, wa_ref[: 3 * D, :]).astype(bf16)
    heads = []
    rows = x.shape[0]
    for s in range(rows // SEQ):
        r = slice(s * SEQ, (s + 1) * SEQ)
        same = seg_col[r, :] == seg_row[:, r]
        outs = []
        for h in range(HEADS):
            q = qkv[r, h * HD : (h + 1) * HD]
            k = qkv[r, D + h * HD : D + (h + 1) * HD]
            v = qkv[r, 2 * D + h * HD : 2 * D + (h + 1) * HD]
            sc = jnp.where(same, nt(q, k), -1e30)
            e = jnp.exp2((sc - jnp.max(sc, axis=-1, keepdims=True)) * EXP_SCALE)
            p = (e * (1.0 / jnp.sum(e, axis=-1, keepdims=True))).astype(bf16)
            outs.append(nn(p, v))
        heads.append(jnp.concatenate(outs, axis=1))
    att = jnp.concatenate(heads, axis=0).astype(bf16)
    x1 = x + nt(att, wa_ref[3 * D :, :])
    u2, _ = unit(x1)
    second = (u2 * g2 + b2).astype(bf16)
    hidden = gelu_value(nt(second, wu_ref[...])).astype(bf16)
    out = x1 + nn(hidden, wd_ref[...])
    return qkv, att, x1, out


def fwd_kernel(x_ref, wa_ref, wu_ref, wd_ref, g_ref, sc_ref, sr_ref, qkv_ref, att_ref, x1_ref, out_ref):
    qkv, att, x1, out = layer_rows(x_ref[...], wa_ref, wu_ref, wd_ref, g_ref[...], sc_ref[...], sr_ref[0])
    qkv_ref[...] = qkv
    att_ref[...] = att
    x1_ref[...] = x1
    out_ref[...] = out


def first_kernel(p_ref, pos_ref, e_ref, wa_ref, wu_ref, wd_ref, g_ref, sc_ref, sr_ref, in_ref, x_ref, qkv_ref, att_ref, x1_ref, out_ref):
    pos = pos_ref[...]
    patch = jnp.where(pos != 0, p_ref[...].astype(f32), 0.0).astype(bf16)
    lanes = e_ref.shape[1] - p_ref.shape[1]
    table = (pos == lax.broadcasted_iota(jnp.int32, (pos.shape[0], lanes), 1)).astype(f32).astype(bf16)
    full = jnp.concatenate([patch, table], axis=1)
    in_ref[...] = full
    x = nt(full, e_ref[...])
    x_ref[...] = x
    qkv, att, x1, out = layer_rows(x, wa_ref, wu_ref, wd_ref, g_ref[...], sc_ref[...], sr_ref[0])
    qkv_ref[...] = qkv
    att_ref[...] = att
    x1_ref[...] = x1
    out_ref[...] = out


def join_kernel(plan, n_in, flag_ref, *refs):
    for src, dst in plan(flag_ref[0], refs[:n_in], refs[n_in:]):
        dst[...] = src[...]


def join(plan, flag, ins, shapes):
    return pl.pallas_call(
        functools.partial(join_kernel, plan, len(ins)),
        in_specs=[smem_spec()] + [vmem_spec()] * len(ins),
        out_specs=[vmem_spec()] * len(shapes),
        out_shape=[jax.ShapeDtypeStruct(s, bf16) for s in shapes],
        compiler_params=pltpu.CompilerParams(vmem_limit_bytes=24 << 20),
        cost_estimate=lasting(1),
        name="join",
    )(flag, *ins)


def joined_kernel(core_ref, h_ref, hg_ref, t_ref, tg_ref, p_ref, pos_ref, g_ref, sc_ref, sr_ref, in_ref, x_ref, qkv_ref, att_ref, x1_ref, out_ref, wo_ref, w_ref, tab_ref, sems, out_sem):
    step = pl.program_id(0)
    cells, piece = h_ref.shape[0], h_ref.shape[1]
    core = core_ref[0]
    copies = []
    for src, at in ((h_ref, core), (hg_ref, 1 - core)):
        for i in range(cells):
            copies.append((src.at[i], w_ref.at[pl.ds(pl.multiple_of((2 * i + at) * piece, 16), piece)]))
    for src, at in ((t_ref, core), (tg_ref, 1 - core)):
        for y in range(t_ref.shape[1]):
            copies.append((src.at[:, y], tab_ref.at[2 * y + at]))
    copies = [pltpu.make_async_copy(a, b, sems.at[i]) for i, (a, b) in enumerate(copies)]
    result = pltpu.make_async_copy(w_ref, wo_ref, out_sem)

    @pl.when(step == 0)
    def _():
        for c in copies:
            c.start()
        for c in copies:
            c.wait()
        result.start()

    pos = pos_ref[...]
    patch = jnp.where(pos != 0, p_ref[...].astype(f32), 0.0).astype(bf16)
    lanes = in_ref.shape[1] - p_ref.shape[1]
    onehot = (pos == lax.broadcasted_iota(jnp.int32, (pos.shape[0], lanes), 1)).astype(f32).astype(bf16)
    full = jnp.concatenate([patch, onehot], axis=1)
    in_ref[...] = full
    width = tab_ref.shape[3]
    x = sum(nt(full[:, n * width : (n + 1) * width], tab_ref[n].reshape(D, width)) for n in range(tab_ref.shape[0]))
    x_ref[...] = x
    qkv, att, x1, out = layer_rows(x, w_ref.at[: 4 * D], w_ref.at[4 * D : 8 * D], w_ref.at[8 * D :], g_ref[...], sc_ref[...], sr_ref[0])
    qkv_ref[...] = qkv
    att_ref[...] = att
    x1_ref[...] = x1
    out_ref[...] = out

    @pl.when(step == pl.num_programs(0) - 1)
    def _():
        result.wait()


def joined_forward(core, half, half_got, table, table_got, patches, pos, gains, seg, step_rows=512):
    rows, patch = patches.shape
    lanes = 2 * table.shape[1] * table.shape[3]
    steps = rows // step_rows
    anywhere = pl.BlockSpec(memory_space=pl.ANY)
    return pl.pallas_call(
        joined_kernel,
        grid=(steps,),
        in_specs=[
            smem_spec(),
            *[anywhere] * 4,
            rows_spec(step_rows, patch),
            rows_spec(step_rows, 1),
            whole_spec(gains.shape),
            rows_spec(step_rows, 1),
            pl.BlockSpec((1, 1, step_rows), lambda i: (i, 0, 0)),
        ],
        out_specs=[rows_spec(step_rows, lanes), rows_spec(step_rows, D), rows_spec(step_rows, 3 * D), rows_spec(step_rows, D), rows_spec(step_rows, D), rows_spec(step_rows, D), anywhere],
        out_shape=[
            jax.ShapeDtypeStruct((rows, lanes), bf16),
            jax.ShapeDtypeStruct((rows, D), f32),
            jax.ShapeDtypeStruct((rows, 3 * D), bf16),
            jax.ShapeDtypeStruct((rows, D), bf16),
            jax.ShapeDtypeStruct((rows, D), f32),
            jax.ShapeDtypeStruct((rows, D), f32),
            jax.ShapeDtypeStruct((12 * D, D), bf16),
        ],
        scratch_shapes=[
            pltpu.VMEM((12 * D, D), bf16),
            pltpu.VMEM((2 * table.shape[1], *table.shape[:1], *table.shape[2:]), bf16),
            pltpu.SemaphoreType.DMA((2 * half.shape[0] + 2 * table.shape[1],)),
            pltpu.SemaphoreType.DMA(()),
        ],
        compiler_params=params(),
        cost_estimate=lasting(18),
        name="first_fwd",
    )(core, half, half_got, table, table_got, patches, pos[:, None], gains, seg[:, None], seg.reshape(steps, 1, step_rows))


def rows_spec(r, width):
    return pl.BlockSpec((r, width), lambda i: (i, 0))


def whole_spec(shape):
    return pl.BlockSpec(shape, lambda *i: (0,) * len(shape))


def third_spec(block):
    return pl.BlockSpec((4 * D, D), lambda *i: (block, 0))


def params(mb=56, n=1):
    return pltpu.CompilerParams(dimension_semantics=("arbitrary",) * n, vmem_limit_bytes=mb << 20)


def lasting(us):
    return pl.CostEstimate(flops=int(us * 1e9), bytes_accessed=int(us * 2e6), transcendentals=0)


def layer_forward(x, w, layer, gains, seg, step_rows=512):
    rows = x.shape[0]
    steps = rows // step_rows
    return pl.pallas_call(
        fwd_kernel,
        grid=(steps,),
        in_specs=[
            rows_spec(step_rows, D),
            *(third_spec(3 * layer + i) for i in range(3)),
            whole_spec(gains.shape),
            rows_spec(step_rows, 1),
            pl.BlockSpec((1, 1, step_rows), lambda i: (i, 0, 0)),
        ],
        out_specs=[rows_spec(step_rows, 3 * D), rows_spec(step_rows, D), rows_spec(step_rows, D), rows_spec(step_rows, D)],
        out_shape=[
            jax.ShapeDtypeStruct((rows, 3 * D), bf16),
            jax.ShapeDtypeStruct((rows, D), bf16),
            jax.ShapeDtypeStruct((rows, D), f32),
            jax.ShapeDtypeStruct((rows, D), f32),
        ],
        compiler_params=params(),
        cost_estimate=lasting(17),
        name="layer_fwd",
    )(x, w, w, w, gains, seg[:, None], seg.reshape(steps, 1, step_rows))


def first_forward(patches, pos, e, w, layer, gains, seg, step_rows=512):
    rows, patch = patches.shape
    lanes = e.shape[1]
    steps = rows // step_rows
    return pl.pallas_call(
        first_kernel,
        grid=(steps,),
        in_specs=[
            rows_spec(step_rows, patch),
            rows_spec(step_rows, 1),
            whole_spec(e.shape),
            *(third_spec(3 * layer + i) for i in range(3)),
            whole_spec(gains.shape),
            rows_spec(step_rows, 1),
            pl.BlockSpec((1, 1, step_rows), lambda i: (i, 0, 0)),
        ],
        out_specs=[rows_spec(step_rows, lanes), rows_spec(step_rows, D), rows_spec(step_rows, 3 * D), rows_spec(step_rows, D), rows_spec(step_rows, D), rows_spec(step_rows, D)],
        out_shape=[
            jax.ShapeDtypeStruct((rows, lanes), bf16),
            jax.ShapeDtypeStruct((rows, D), f32),
            jax.ShapeDtypeStruct((rows, 3 * D), bf16),
            jax.ShapeDtypeStruct((rows, D), bf16),
            jax.ShapeDtypeStruct((rows, D), f32),
            jax.ShapeDtypeStruct((rows, D), f32),
        ],
        compiler_params=params(),
        cost_estimate=lasting(18),
        name="first_fwd",
    )(patches, pos[:, None], e, w, w, w, gains, seg[:, None], seg.reshape(steps, 1, step_rows))


def last_fwd_kernel(cls_ref, x_ref, wa_ref, wu_ref, wd_ref, g_ref, sk_ref, sq_ref, kv_ref, xc_ref, q_ref, att_ref, x1_ref, out_ref, feat_ref):
    g1, b1, g2, b2, g3, b3 = (g_ref[i : i + 1, :] for i in range(6))
    u, _ = unit(x_ref[...])
    normed = (u * g1 + b1).astype(bf16)
    kv = nt(normed, wa_ref[D : 3 * D, :]).astype(bf16)
    kv_ref[...] = kv
    slots = xc_ref.shape[0]
    for i in range(slots):
        xc_ref[i : i + 1, :] = x_ref[pl.ds(cls_ref[i], 1), :]
    xc = xc_ref[...]
    uc, _ = unit(xc)
    q = nt((uc * g1 + b1).astype(bf16), wa_ref[:D, :]).astype(bf16)
    q_ref[...] = q
    same = sq_ref[...] == sk_ref[...]
    outs = []
    for h in range(HEADS):
        c = slice(h * HD, (h + 1) * HD)
        sc = jnp.where(same, nt(q[:, c], kv[:, c]) * HD ** (-0.5), -1e30)
        e = jnp.exp(sc - jnp.max(sc, axis=-1, keepdims=True))
        p = (e * (1.0 / jnp.sum(e, axis=-1, keepdims=True))).astype(bf16)
        outs.append(nn(p, kv[:, D + h * HD : D + (h + 1) * HD]))
    att = jnp.concatenate(outs, axis=1).astype(bf16)
    att_ref[...] = att
    x1 = xc + nt(att, wa_ref[3 * D :, :])
    x1_ref[...] = x1
    u2, _ = unit(x1)
    second = (u2 * g2 + b2).astype(bf16)
    hidden = gelu_value(nt(second, wu_ref[...])).astype(bf16)
    out = x1 + nn(hidden, wd_ref[...])
    out_ref[...] = out
    u3, _ = unit(out)
    feat_ref[...] = (u3 * g3 + b3).astype(bf16)


def put_halves(core_ref, acc_ref, keep_ref, send_ref):
    half = keep_ref.shape[1]
    mine = core_ref[0] * half
    other = (1 - core_ref[0]) * half
    for i in range(keep_ref.shape[0]):
        base = i * 2 * half
        keep_ref[i] = acc_ref[pl.ds(base + mine, half), :].astype(bf16)
        send_ref[i] = acc_ref[pl.ds(base + other, half), :].astype(bf16)


def smem_spec():
    return pl.BlockSpec(memory_space=pltpu.SMEM)


def vmem_spec():
    return pl.BlockSpec(memory_space=pltpu.VMEM)


def last_forward(cls, x, w, layer, gains, seg, seg_cls):
    rows, slots = x.shape[0], cls.shape[0]
    return pl.pallas_call(
        last_fwd_kernel,
        grid=(1,),
        in_specs=[smem_spec(), whole_spec(x.shape), *(third_spec(3 * layer + i) for i in range(3)), *[vmem_spec()] * 3],
        out_specs=[vmem_spec()] * 7,
        out_shape=[
            jax.ShapeDtypeStruct((rows, 2 * D), bf16),
            jax.ShapeDtypeStruct((slots, D), f32),
            jax.ShapeDtypeStruct((slots, D), bf16),
            jax.ShapeDtypeStruct((slots, D), bf16),
            jax.ShapeDtypeStruct((slots, D), f32),
            jax.ShapeDtypeStruct((slots, D), f32),
            jax.ShapeDtypeStruct((slots, D), bf16),
        ],
        compiler_params=params(),
        cost_estimate=lasting(9),
        name="last_fwd",
    )(cls, x, w, w, w, gains, seg[None, :], seg_cls[:, None])


def last_bwd_kernel(cls_ref, core_ref, df_ref, x_ref, wa_ref, wu_ref, wd_ref, g_ref, sk_ref, sq_ref, kv_ref, xc_ref, q_ref, att_ref, x1_ref, xo_ref, dx_ref, keep_ref, send_ref, dv_ref, dn_ref, dw_ref):
    g1, b1, g2, b2, g3, b3 = (g_ref[i : i + 1, :] for i in range(6))
    slots = xc_ref.shape[0]
    df = df_ref[...]
    u3, i3 = unit(xo_ref[...])
    dxo = unit_back(u3, i3, g3, df)
    dg3 = jnp.sum(df * u3, axis=0, keepdims=True)
    db3 = jnp.sum(df, axis=0, keepdims=True)
    branch = dxo.astype(bf16)
    u2, i2 = unit(x1_ref[...])
    second = (u2 * g2 + b2).astype(bf16)
    value, slope = gelu_both(nt(second, wu_ref[...]))
    dpre = (nt(branch, wd_ref[...]) * slope).astype(bf16)
    dw_ref[4 * D + MLP :, :] = tn(value.astype(bf16), branch)
    dw_ref[4 * D : 4 * D + MLP, :] = tn(dpre, second)
    dsecond = nn(dpre, wu_ref[...])
    dg2 = jnp.sum(dsecond * u2, axis=0, keepdims=True)
    db2 = jnp.sum(dsecond, axis=0, keepdims=True)
    dx1 = dxo + unit_back(u2, i2, g2, dsecond)
    ab = dx1.astype(bf16)
    datt = nn(ab, wa_ref[3 * D :, :]).astype(bf16)
    dw_ref[3 * D : 4 * D, :] = tn(ab, att_ref[...])
    same = sq_ref[...] == sk_ref[...]
    q, kv = q_ref[...], kv_ref[...]
    dqs, dks, dvs = [], [], []
    for h in range(HEADS):
        c = slice(h * HD, (h + 1) * HD)
        k, v = kv[:, c], kv[:, D + h * HD : D + (h + 1) * HD]
        sc = jnp.where(same, nt(q[:, c], k) * HD ** (-0.5), -1e30)
        e = jnp.exp(sc - jnp.max(sc, axis=-1, keepdims=True))
        p = e * (1.0 / jnp.sum(e, axis=-1, keepdims=True))
        dp = nt(datt[:, c], v)
        ds = (p * (dp - jnp.sum(dp * p, axis=-1, keepdims=True))).astype(bf16)
        dvs.append(tn(p.astype(bf16), datt[:, c]))
        dks.append(tn(ds, q[:, c]) * HD ** (-0.5))
        dqs.append(nn(ds, k) * HD ** (-0.5))
    dq = jnp.concatenate(dqs, axis=1).astype(bf16)
    dkv = jnp.concatenate(dks + dvs, axis=1).astype(bf16)
    u, i1 = unit(x_ref[...])
    normed = (u * g1 + b1).astype(bf16)
    dw_ref[D : 3 * D, :] = tn(dkv, normed)
    uc, _ = unit(xc_ref[...])
    dw_ref[:D, :] = tn(dq, (uc * g1 + b1).astype(bf16))
    dn_ref[...] = nn(dkv, wa_ref[D : 3 * D, :])
    dnc = nn(dq, wa_ref[:D, :])
    for i in range(slots):
        at = pl.ds(cls_ref[i], 1)
        dn_ref[at, :] = dn_ref[at, :] + dnc[i : i + 1, :]
    dn = dn_ref[...]
    dg1 = jnp.sum(dn * u, axis=0, keepdims=True)
    db1 = jnp.sum(dn, axis=0, keepdims=True)
    dx_ref[...] = unit_back(u, i1, g1, dn)
    for i in range(slots):
        at = pl.ds(cls_ref[i], 1)
        dx_ref[at, :] = dx_ref[at, :] + dx1[i : i + 1, :]
    dv_ref[...] = jnp.concatenate([dg1, db1, dg2, db2, dg3, db3, jnp.zeros((2, D), f32)], axis=0)
    put_halves(core_ref, dw_ref, keep_ref, send_ref)


def last_backward(cls, core, wide, df, x, w, layer, gains, seg, seg_cls, kv, xc, q, att, x1, xo):
    rows = x.shape[0]
    return pl.pallas_call(
        last_bwd_kernel,
        grid=(1,),
        in_specs=[smem_spec(), smem_spec(), vmem_spec(), whole_spec(x.shape), *(third_spec(3 * layer + i) for i in range(3)), *[vmem_spec()] * 9],
        out_specs=[vmem_spec()] * 4,
        out_shape=[
            jax.ShapeDtypeStruct((rows, D), f32),
            *[jax.ShapeDtypeStruct((12 * D // wide, wide // 2, D), bf16)] * 2,
            jax.ShapeDtypeStruct((8, D), f32),
        ],
        scratch_shapes=[pltpu.VMEM((rows, D), f32), pltpu.VMEM((12 * D, D), f32)],
        compiler_params=params(),
        cost_estimate=lasting(15),
        name="last_bwd",
    )(cls, core, df, x, w, w, w, gains, seg[None, :], seg_cls[:, None], kv, xc, q, att, x1, xo)


def mlp_bwd_kernel(core_ref, dxo_ref, x1_ref, att_ref, wu_ref, wd_ref, g_ref, dx1_ref, keep_ref, send_ref, dv_ref, acc_ref):
    step = pl.program_id(0)
    g2, b2 = g_ref[2:3, :], g_ref[3:4, :]
    dxo = dxo_ref[...]
    branch = dxo.astype(bf16)
    u2, i2 = unit(x1_ref[...])
    second = (u2 * g2 + b2).astype(bf16)
    value, slope = gelu_both(nt(second, wu_ref[...]))
    hidden = value.astype(bf16)
    dpre = (nt(branch, wd_ref[...]) * slope).astype(bf16)
    dsecond = nn(dpre, wu_ref[...])
    sums = jnp.concatenate([jnp.sum(dsecond * u2, axis=0, keepdims=True), jnp.sum(dsecond, axis=0, keepdims=True), jnp.zeros((6, D), f32)], axis=0)
    dx1 = dxo + unit_back(u2, i2, g2, dsecond)
    dx1_ref[...] = dx1
    ab = dx1.astype(bf16)
    last = pl.num_programs(0) - 1

    @pl.when(step == 0)
    def _():
        acc_ref[:D, :] = tn(ab, att_ref[...])
        acc_ref[D : D + MLP, :] = tn(dpre, second)
        acc_ref[D + MLP :, :] = tn(hidden, branch)
        dv_ref[...] = sums

    @pl.when(step > 0)
    def _():
        acc_ref[:D, :] += tn(ab, att_ref[...])
        acc_ref[D : D + MLP, :] += tn(dpre, second)
        acc_ref[D + MLP :, :] += tn(hidden, branch)
        dv_ref[...] += sums

    @pl.when(step == last)
    def _():
        put_halves(core_ref, acc_ref, keep_ref, send_ref)


def mlp_backward(core, wide, dxo, x1, att, w, layer, gains, step_rows=512):
    rows = x1.shape[0]
    steps = rows // step_rows
    return pl.pallas_call(
        mlp_bwd_kernel,
        grid=(steps,),
        in_specs=[smem_spec(), *[rows_spec(step_rows, D)] * 3, third_spec(3 * layer + 1), third_spec(3 * layer + 2), whole_spec(gains.shape)],
        out_specs=[rows_spec(step_rows, D), *[whole_spec((9 * D // wide, wide // 2, D))] * 2, whole_spec((8, D))],
        out_shape=[jax.ShapeDtypeStruct((rows, D), f32), *[jax.ShapeDtypeStruct((9 * D // wide, wide // 2, D), bf16)] * 2, jax.ShapeDtypeStruct((8, D), f32)],
        scratch_shapes=[pltpu.VMEM((9 * D, D), f32)],
        compiler_params=params(),
        cost_estimate=lasting(16),
        name="mlp_bwd",
    )(core, dxo, x1, att, w, w, gains)


def att_bwd_kernel(first_vec, *refs):
    core_ref, dx1_ref, x_ref, qkv_ref, w_ref, g_ref, sc_ref, sr_ref, *refs = refs
    if first_vec:
        in_ref, vec_ref, keep_ref, send_ref, tkeep_ref, tsend_ref, acc_ref, dv_ref, table_ref = refs
    else:
        dx_ref, keep_ref, send_ref, dv_ref, acc_ref = refs
    step = pl.program_id(0)
    g1, b1 = g_ref[0:1, :], g_ref[1:2, :]
    dx1 = dx1_ref[...]
    ab = dx1.astype(bf16)
    datt = nn(ab, w_ref[3 * D : 4 * D, :]).astype(bf16)
    qkv = qkv_ref[...]
    parts = []
    for s in range(x_ref.shape[0] // SEQ):
        r = slice(s * SEQ, (s + 1) * SEQ)
        same = sc_ref[r, :] == sr_ref[0][:, r]
        dqs, dks, dvs = [], [], []
        for h in range(HEADS):
            q = qkv[r, h * HD : (h + 1) * HD]
            k = qkv[r, D + h * HD : D + (h + 1) * HD]
            v = qkv[r, 2 * D + h * HD : 2 * D + (h + 1) * HD]
            da = datt[r, h * HD : (h + 1) * HD]
            sc = jnp.where(same, nt(k, q), -1e30)
            e = jnp.exp2((sc - jnp.max(sc, axis=0, keepdims=True)) * EXP_SCALE)
            p = e * (1.0 / jnp.sum(e, axis=0, keepdims=True))
            dp = nt(v, da)
            ds = (p * (dp - jnp.sum(dp * p, axis=0, keepdims=True))).astype(bf16)
            dvs.append(nn(p.astype(bf16), da))
            dks.append(nn(ds, q) * HD ** (-0.5))
            dqs.append(tn(ds, k) * HD ** (-0.5))
        parts.append(jnp.concatenate(dqs + dks + dvs, axis=1).astype(bf16))
    dqkv = jnp.concatenate(parts, axis=0)
    u, i1 = unit(x_ref[...])
    normed = (u * g1 + b1).astype(bf16)
    dn = nn(dqkv, w_ref[: 3 * D, :])
    sums = jnp.concatenate([jnp.sum(dn * u, axis=0, keepdims=True), jnp.sum(dn, axis=0, keepdims=True), jnp.zeros((6, D), f32)], axis=0)
    dx = dx1 + unit_back(u, i1, g1, dn)
    if first_vec:
        grad_table = tn(dx.astype(bf16), in_ref[...])
    else:
        dx_ref[...] = dx
    last = pl.num_programs(0) - 1

    @pl.when(step == 0)
    def _():
        acc_ref[...] = tn(dqkv, normed)
        if first_vec:
            table_ref[...] = grad_table
        dv_ref[...] = sums

    @pl.when(step > 0)
    def _():
        acc_ref[...] += tn(dqkv, normed)
        if first_vec:
            table_ref[...] += grad_table
        dv_ref[...] += sums

    @pl.when(step == last)
    def _():
        put_halves(core_ref, acc_ref, keep_ref, send_ref)
        if first_vec:
            rows, lanes = vec_ref.shape[0], table_ref.shape[1]
            vec = vec_ref[...] + jnp.concatenate([dv_ref[...], jnp.zeros((rows - 8, D), f32)], axis=0)
            at = lax.broadcasted_iota(jnp.int32, (rows, lanes), 1) - first_vec
            pick = (at == lax.broadcasted_iota(jnp.int32, (rows, lanes), 0)).astype(f32).astype(bf16)
            table_ref[...] += tn(vec.astype(bf16), pick)
            half = lanes // 2
            mine = pl.multiple_of(core_ref[0] * half, 128)
            other = pl.multiple_of((1 - core_ref[0]) * half, 128)
            tkeep_ref[...] = table_ref[:, pl.ds(mine, half)].astype(bf16)
            tsend_ref[...] = table_ref[:, pl.ds(other, half)].astype(bf16)


def att_backward(core, wide, dx1, x, qkv, w, layer, gains, seg, table=None, step_rows=512):
    rows = x.shape[0]
    steps = rows // step_rows
    parts = [jax.ShapeDtypeStruct((3 * D // wide, wide // 2, D), bf16)] * 2
    whole = [whole_spec(p.shape) for p in parts]
    acc = pltpu.VMEM((3 * D, D), f32)
    if table is None:
        first_vec, more, more_specs = 0, (), []
        out_specs = [rows_spec(step_rows, D), *whole, whole_spec((8, D))]
        out_shape = [jax.ShapeDtypeStruct((rows, D), f32), *parts, jax.ShapeDtypeStruct((8, D), f32)]
        scratch = [acc]
    else:
        first_vec, inputs, vec = table
        lanes = inputs.shape[1]
        more, more_specs = (inputs, vec), [rows_spec(step_rows, lanes), whole_spec(vec.shape)]
        out_shape = [*parts, *[jax.ShapeDtypeStruct((D, lanes // 2), bf16)] * 2]
        out_specs = [whole_spec(p.shape) for p in out_shape]
        scratch = [acc, pltpu.VMEM((8, D), f32), pltpu.VMEM((D, lanes), f32)]
    return pl.pallas_call(
        functools.partial(att_bwd_kernel, first_vec),
        grid=(steps,),
        in_specs=[
            smem_spec(),
            rows_spec(step_rows, D),
            rows_spec(step_rows, D),
            rows_spec(step_rows, 3 * D),
            third_spec(3 * layer),
            whole_spec(gains.shape),
            rows_spec(step_rows, 1),
            pl.BlockSpec((1, 1, step_rows), lambda i: (i, 0, 0)),
            *more_specs,
        ],
        out_specs=out_specs,
        out_shape=out_shape,
        scratch_shapes=scratch,
        compiler_params=params(),
        cost_estimate=lasting(18),
        name="att_bwd",
    )(core, dx1, x, qkv, w, gains, seg[:, None], seg.reshape(steps, 1, step_rows), *more)


HALF_PI = (1.5703125, 0.000483751296996, 7.54978995489e-08, 5.1266913e-12)


def sin_cos(x):
    k = jnp.round(x * 0.6366197723675814)
    r = x
    for part in HALF_PI:
        r = r - k * part
    r = jnp.clip(r, -1.0, 1.0)
    r2 = r * r
    s = r + r * r2 * (-1.6666654611e-1 + r2 * (8.3321608736e-3 + r2 * -1.9515295891e-4))
    c = 1.0 - 0.5 * r2 + r2 * r2 * (4.166664568298827e-2 + r2 * (-1.388731625493765e-3 + r2 * 2.443315711809948e-5))
    n = k.astype(jnp.int32)
    odd = (n & 1) == 1
    sin_v = jnp.where(odd, c, s)
    cos_v = jnp.where(odd, s, c)
    sin_v = jnp.where((n & 2) == 2, -sin_v, sin_v)
    cos_v = jnp.where(((n + 1) & 2) == 2, -cos_v, cos_v)
    return sin_v, cos_v


def head_kernel(several, skip, s_ref, all_ref, rff_ref, read_ref, w_ref, *refs):
    gread_ref, grff_ref, sums_ref, sin_ref, cos_ref = refs[skip:]
    features = all_ref[:, :D]
    logits = all_ref[:, D:]
    phases = nn(features, rff_ref[...])
    large = jnp.max(jnp.abs(phases)) > 5e4

    @pl.when(large)
    def _():
        sin_ref[...] = jnp.sin(phases)
        cos_ref[...] = jnp.cos(phases)

    @pl.when(jnp.logical_not(large))
    def _():
        sin_ref[...], cos_ref[...] = sin_cos(phases)

    lifted = cos_ref[...].astype(bf16)
    back = (-sin_ref[...] * nn(logits, read_ref[...])).astype(bf16)
    blocks = pl.num_programs(1)
    gread = tn(logits, lifted)
    grff = tn(features, back)
    if several:
        block = pl.program_id(1)

        @pl.when(block == 0)
        def _():
            gread_ref[...] = gread
            grff_ref[...] = grff

        @pl.when(block > 0)
        def _():
            gread_ref[...] += gread
            grff_ref[...] += grff

        @pl.when(block == blocks - 1)
        def _():
            head_finish(s_ref, w_ref, gread_ref[...], grff_ref[...], gread_ref, grff_ref, sums_ref)
    else:
        head_finish(s_ref, w_ref, gread, grff, gread_ref, grff_ref, sums_ref)


def head_finish(s_ref, w_ref, gread, grff, gread_ref, grff_ref, sums_ref):
    step = pl.program_id(0)
    w = w_ref[...]
    gread = gread * s_ref[0] + 2.0 * l2_weight * w
    grff = grff * s_ref[0]
    gread_ref[...] = gread
    grff_ref[...] = grff
    total = jnp.sum(jnp.sum(gread * gread, axis=0, keepdims=True)) + jnp.sum(jnp.sum(grff * grff, axis=0, keepdims=True))
    ridge = jnp.sum(jnp.sum(w * w, axis=0, keepdims=True))
    row = lax.broadcasted_iota(jnp.int32, (8, 128), 0)
    tile = jnp.where(row == 0, total, jnp.where(row == 1, ridge, 0.0))

    @pl.when(step == 0)
    def _():
        sums_ref[...] = tile

    @pl.when(step > 0)
    def _():
        sums_ref[...] += tile


def head_backward(scale, every, rff, read, w, part, parts, before=None, cols=256):
    n, classes = every.shape[0], read.shape[0]
    width = rff.shape[1]
    cols = min(cols, width // parts)
    rows = math.gcd(n, 768)
    steps = width // cols // parts
    base = part * steps
    col = lambda r: pl.BlockSpec((r, cols), lambda i, j: (0, base + i))
    more = () if before is None else before[:2]
    out = pl.pallas_call(
        functools.partial(head_kernel, n > rows, len(more)),
        grid=(steps, n // rows),
        in_specs=[smem_spec(), pl.BlockSpec((rows, every.shape[1]), lambda i, j: (j, 0)), col(D), col(classes), col(classes)] + [pl.BlockSpec(memory_space=pl.ANY)] * len(more),
        out_specs=[col(classes), col(D), whole_spec((8, 128))],
        out_shape=[jax.ShapeDtypeStruct((classes, width), f32), jax.ShapeDtypeStruct((D, width), f32), jax.ShapeDtypeStruct((8, 128), f32)],
        scratch_shapes=[pltpu.VMEM((rows, cols), f32)] * 2,
        input_output_aliases={5 + i: i for i in range(len(more))},
        compiler_params=params(56, 2),
        cost_estimate=lasting(8),
        name="head_bwd",
    )(scale, every, rff, read, w, *more)
    return out if before is None else [*out[:2], before[2], out[2]]


def step_rows_of(refs, outs, factor, rate, decay):
    w_ref, m_ref, v_ref, e_ref, g_ref = refs
    out = adamw(w_ref[...], m_ref[...], v_ref[...], e_ref[...], g_ref[...].astype(f32) * factor, rate, decay)
    for o_ref, value in zip(outs, out):
        o_ref[...] = value


def optimizer_kernel(counts, f_ref, *refs):
    step = pl.program_id(0)
    ins, outs = refs[: 5 * len(counts)], refs[5 * len(counts) :]
    low = 0
    for i, count in enumerate(counts):

        @pl.when((step >= low) & (step < low + count))
        def _(i=i):
            step_rows_of(ins[5 * i : 5 * i + 5], outs[5 * i : 5 * i + 5], f_ref[i], rate_matrix, weight_decay)

        low += count


def optimizer(factors, groups, us):
    counts = [g[0][0].shape[0] // g[1] for g in groups]
    specs, out_specs, out_shape, args = [], [], [], []
    low = 0
    for (arrays, rows), count in zip(groups, counts):
        width = arrays[0].shape[1]
        spec = pl.BlockSpec((rows, width), lambda i, low=low, count=count: (jnp.clip(i - low, 0, count - 1), 0))
        specs += [spec] * 5
        out_specs += [spec] * 5
        out_shape += [jax.ShapeDtypeStruct(arrays[0].shape, f32)] * 4 + [jax.ShapeDtypeStruct(arrays[0].shape, bf16)]
        args += arrays
        low += count
    out = pl.pallas_call(
        functools.partial(optimizer_kernel, counts),
        grid=(low,),
        in_specs=[smem_spec(), *specs],
        out_specs=out_specs,
        out_shape=out_shape,
        compiler_params=params(48),
        cost_estimate=lasting(us),
        name="optimizer",
    )(factors, *args)
    return [out[5 * i : 5 * i + 5] for i in range(len(groups))]


POS = 197
CLASSES = 1000
L = 3
IMG_SEQ = 6
STEP = 10
PART = 4 * D
WIDE = 3 * PART
clip_bound = 0.02
l2_weight = 0.1
beta_first = 0.5
beta_second = 0.5
adam_eps = 1e-08
weight_decay = 0.05
rate_matrix = 0.05
rate_vector = 0.5
ema_rate = 0.5
DP = ("dph", "dpl")
NARROW = ("ny", "nc")
ALL = DP + NARROW


def swap(rows, axis, mask):
    return lax.ppermute(rows, axis, [(i, i ^ mask) for i in range(lax.axis_size(axis))])


def add_up(terms):
    return sum(t.astype(f32) for t in terms)


def bits_of(size):
    return size.bit_length() - 1


class Slab:
    def __init__(self, terms):
        self.terms = terms

    def hop(self, dim, axis, bit=0):
        half = self.terms[0].shape[dim] // 2
        mine = (lax.axis_index(axis) >> bit) & 1
        send = add_up([lax.dynamic_slice_in_dim(t, (1 - mine) * half, half, dim) for t in self.terms])
        self.terms = [lax.dynamic_slice_in_dim(t, mine * half, half, dim) for t in self.terms]
        return swap(send.astype(bf16), axis, 1 << bit)

    def hops_y(self, dim):
        bits = bits_of(lax.axis_size("ny"))
        for bit in range(bits - 1):
            self.terms.append(self.hop(dim, "ny", bit))
        return self.hop(dim, "ny", bits - 1)

    def hop_x(self):
        self.terms = [t.reshape(t.shape[0] // 2, 2, *t.shape[1:]) for t in self.terms]
        got = self.hop(1, "dpl")
        self.terms = [t.reshape(t.shape[0], *t.shape[2:]) for t in self.terms]
        return got.reshape(got.shape[0], *got.shape[2:])

    def low(self):
        return add_up(self.terms).astype(bf16)


def spread(rows):
    return lax.all_to_all(rows, "dph", 0, 0)


def join_narrow(piece):
    every = lax.all_gather(piece, NARROW, axis=0, tiled=False)
    cores, ys = lax.axis_size("nc"), lax.axis_size("ny")
    bits = bits_of(ys)
    flip = [int(format(i, "b").zfill(bits)[::-1], 2) for i in range(ys)]
    return [every[flip[y] * cores + core] for core in range(cores) for y in range(ys)]


def total_of(scalars):
    lane = lax.broadcasted_iota(jnp.int32, (8, 128), 1)
    tile = jnp.zeros((8, 128), f32)
    for i, value in enumerate(scalars):
        tile = jnp.where(lane == i, value, tile)
    world = lax.axis_size(ALL)
    every = lax.all_to_all(jnp.broadcast_to(tile[None], (world, 8, 128)), ALL, 0, 0)
    row = jnp.sum(every, axis=0)[0]
    return [row[i] for i in range(len(scalars))]


def adamw(weight, first, second, average, grad, rate, decay):
    first = beta_first * first + (1.0 - beta_first) * grad
    second = beta_second * second + (1.0 - beta_second) * grad * grad
    ahead = first / (1.0 - beta_first**STEP)
    behind = second / (1.0 - beta_second**STEP)
    weight = weight - rate * (ahead / (jnp.sqrt(behind) + adam_eps) + decay * weight)
    average = ema_rate * average + (1.0 - ema_rate) * weight
    return (weight, first, second, average, weight.astype(bf16))


def square_sum(arrays):
    return sum(jnp.sum(a.astype(f32) * a.astype(f32)) for a in arrays)


def shards(
    patches,
    pos_index,
    segments,
    cls_row,
    labels,
    img_count,
    embed_w,
    embed_m,
    embed_v,
    embed_e,
    vector_w,
    vector_m,
    vector_v,
    vector_e,
    mats_w,
    mats_m,
    mats_v,
    mats_e,
    rff_w,
    rff_m,
    rff_v,
    rff_e,
    read_w,
    read_m,
    read_v,
    read_e,
):
    n_dp, n_narrow = lax.axis_size(DP), lax.axis_size(NARROW)
    me_dp, me_narrow = lax.axis_index(DP), lax.axis_index(NARROW)
    own_dim = embed_w.shape[1]
    own_wide = mats_w.shape[2]
    core = lax.axis_index("nc").astype(jnp.int32).reshape(1)
    slots = cls_row.shape[0]
    table_rows = -(-(embed_w.shape[0] + vector_w.shape[0]) // 256) * 256
    chunk = table_rows // n_narrow

    tie = lax.optimization_barrier

    def small_facts():
        total = total_of([jnp.sum(img_count).astype(f32)])[0]
        slot_ids = jnp.arange(slots)
        valid = (slot_ids % IMG_SEQ < jnp.repeat(img_count, IMG_SEQ, total_repeat_length=slots)).astype(jnp.int32)
        return total, lax.all_gather(jnp.stack([labels, valid]), NARROW, axis=0)

    def low_head():
        pad = -slots % 16
        cls = jnp.concatenate([cls_row, jnp.broadcast_to(cls_row[-1:], (pad,))])
        return rff_w.astype(bf16), read_w.T.astype(bf16), cls, segments[cls]

    table = jnp.concatenate([embed_w.T, vector_w.T], axis=1).astype(bf16)
    table = jnp.pad(table, ((0, 0), (0, table_rows - table.shape[1])))
    table = lax.dynamic_slice_in_dim(table, me_narrow * chunk, chunk, 1)
    quarter = own_wide // n_narrow
    mats_own = lax.dynamic_slice_in_dim(jnp.swapaxes(mats_w, 1, 2), me_narrow * quarter, quarter, 1).astype(bf16)
    first_vec, vectors = embed_w.shape[0], vector_w.shape[0]
    rest = lax.all_gather(mats_own[1:], ALL, axis=1, tiled=True).reshape((L - 1) * WIDE, D)
    dph, dpl, ny = (lax.axis_size(a) for a in ("dph", "dpl", "ny"))

    if (dph, dpl, ny) == (4, 2, 2) and quarter % 16 == 0 and own_dim % 16 == 0 and chunk % 128 == 0:
        cut = quarter // 32 * 16

        def flag(axis, bit=0):
            return ((lax.axis_index(axis) >> bit) & 1).astype(jnp.int32).reshape(1)

        def both(src, got, dst, put):
            return lambda f, i, o: [(i[src], put(o[dst], f)), (i[got], put(o[dst], 1 - f))]

        def plan_of(*moves):
            return lambda f, i, o: [c for move in moves for c in move(f, i, o)]

        a, e = mats_own[:1], table[None]
        ga, ge = swap(a, "dph", 2), swap(e, "dph", 2)
        ahead = lambda o, f: o.at[:, f]
        a, e = join(plan_of(both(0, 1, 0, ahead), both(2, 3, 1, ahead)), flag("dph", 1), (a, ga, e, ge), ((1, 2, quarter, D), (1, 2, own_dim, chunk)))
        a, e = a.reshape(2, quarter, D), e.reshape(2, own_dim, chunk)
        (ga, ge), (image_total, facts) = tie(((swap(a, "dph", 1), swap(e, "dph", 1)), small_facts()))

        def split(f, i, o):
            out = []
            for src, at in ((i[0], f), (i[1], 1 - f)):
                out += [(src.at[:, :cut], o[0].at[:, at]), (src.at[:, cut:], o[1].at[:, at])]
            return out + [(i[2], o[2].at[:, f]), (i[3], o[2].at[:, 1 - f])]

        p, q, e = join(split, flag("dph"), (a, ga, e, ge), ((2, 2, cut, D), (2, 2, quarter - cut, D), (2, 2, own_dim, chunk)))
        p, q, e = (t.reshape(4, *t.shape[2:]) for t in (p, q, e))
        gp, gq, ge = swap(p, "dpl", 1), swap(q, "ny", 1), swap(e, "dpl", 1)
        (p,) = join(both(0, 1, 0, ahead), flag("dpl"), (p, gp), ((4, 2, cut, D),))
        (q,) = join(both(0, 1, 0, ahead), flag("ny"), (q, gq), ((4, 2, quarter - cut, D),))
        (e,) = join(both(0, 1, 0, ahead), flag("dpl"), (e, ge), ((4, 2, own_dim, chunk),))
        (gp, gq, ge), low_parts = tie(((swap(p, "ny", 1), swap(q, "dpl", 1), swap(e, "ny", 1)), low_head()))

        def last(f, i, o):
            fx, fy = f
            return [
                (i[0], o[0].at[:, :, fy, :cut]),
                (i[1], o[0].at[:, :, 1 - fy, :cut]),
                (i[2], o[0].at[:, fx, :, cut:]),
                (i[3], o[0].at[:, 1 - fx, :, cut:]),
                (i[4], o[1].at[:, :, fy]),
                (i[5], o[1].at[:, :, 1 - fy]),
            ]

        half, e = join(
            lambda f, i, o: last((f & 1, f >> 1), i, o),
            flag("dpl") + 2 * flag("ny"),
            (p, gp, q, gq, e, ge),
            ((4, 2, 2, quarter, D), (4, 2, 2, own_dim, chunk)),
        )
        half, e = half.reshape(n_dp * ny, quarter, D), e.reshape(n_dp, ny, own_dim, chunk)
        got, ge = swap(half, "nc", 1), swap(e, "nc", 1)
        holder, lane = first_vec // chunk, first_vec % chunk
        piece = jnp.where(core[0] == holder % 2, e[:, holder // 2], ge[:, holder // 2])
        gains = piece[:, :, lane : lane + vectors].reshape(D, vectors).T.astype(f32)
        outs = joined_forward(core, half, got, e, ge, patches, pos_index, gains[0:4], segments)
        inputs, x0, qkv0, att0, mid0, x1, mats0 = outs
    else:
        image_total, facts = small_facts()
        low_parts = low_head()
        table = lax.all_gather(table, ALL, axis=0)
        table = table.reshape(n_dp, n_narrow, own_dim, chunk).transpose(0, 2, 1, 3).reshape(D, table_rows)
        mats0 = lax.all_gather(mats_own[0], ALL, axis=0, tiled=True)
        gains = table[:, first_vec : first_vec + vectors].T.astype(f32)
        inputs, x0, qkv0, att0, mid0, x1 = first_forward(patches, pos_index, table, mats0, 0, gains[0:4], segments)
    rff_low, read_low, cls, seg_cls = low_parts
    group_labels = facts[:, 0].reshape(-1)
    group_valid = facts[:, 1].reshape(-1).astype(f32)[:, None]
    pad = cls.shape[0] - slots
    weights = [(mats0, 0)] + [(rest, i) for i in range(L - 1)]

    states = [(x0, qkv0, att0, mid0)]
    for layer in range(1, L - 1):
        qkv, att, mid, x2 = layer_forward(x1, *weights[layer], gains[4 * layer : 4 * layer + 4], segments)
        states.append((x1, qkv, att, mid))
        x1 = x2
    last_gains = gains[4 * L - 4 :]
    kept = last_forward(cls, x1, *weights[-1], last_gains, segments, seg_cls)
    features = kept[-1][:slots]

    group_rows = lax.all_gather(features, NARROW, axis=0, tiled=True)
    phases = nn(group_rows, rff_low)
    lifted = jnp.cos(phases).astype(bf16)
    partial = lax.all_gather(nt(lifted, read_low).astype(bf16), NARROW, axis=0)
    logits = jnp.sum(partial.astype(f32), axis=0)
    error = logits - (group_labels[:, None] == jnp.arange(CLASSES)[None, :]).astype(f32)
    error_sum = jnp.sum(group_valid * error * error)
    grad_logits = (2.0 * group_valid * error).astype(bf16)
    grad_phases = (-jnp.sin(phases) * nn(grad_logits, read_low)).astype(bf16)
    grad_pieces = nt(grad_phases, rff_low).reshape(n_narrow, slots, D)
    grad_features = jnp.sum(lax.all_to_all(grad_pieces, NARROW, 0, 0), axis=0)
    grad_features = jnp.pad(grad_features, ((0, pad), (0, 0)))

    own_logits = lax.dynamic_slice_in_dim(grad_logits, me_narrow * slots, slots, 0)
    every = lax.all_gather(jnp.concatenate([features, own_logits], axis=1), ALL, axis=0, tiled=True)
    scale = 1.0 / image_total

    state, keep, send, vec = last_backward(cls, core, own_wide, grad_features, x1, *weights[-1], last_gains, segments, seg_cls, *kept[:-1])
    vecs = [vec[:6]]
    whole = Slab([keep])
    done = {}
    flight = {(L - 1, "c"): (whole, swap(send, "nc", 1))}
    parts = {}

    def start(name, at, slab, dim=1, sent=None):
        if at == "c":
            flight[(name, at)] = (slab, swap(sent, "nc", 1))
        elif at == "y":
            flight[(name, at)] = (slab, slab.hops_y(dim))
        else:
            flight[(name, at)] = (slab, slab.hop_x())

    def land(outs, only=None):
        keys = [k for k in flight if only is None or k == only]
        outs, got = tie((outs, [flight[k][1] for k in keys]))
        for (name, at), g in zip(keys, got):
            slab = flight.pop((name, at))[0]
            if at == "z":
                done[name] = g
                continue
            slab.terms.append(g)
            if at == "c":
                start(name, "y", slab, 2 if name == "table" else 1)
            elif at == "y":
                start(name, "x", slab)
            else:
                parts[name] = slab.low()
                upper = [L - 1, *((i, kind) for i in range(1, L - 1) for kind in "am")]
                if name in upper and all(u in parts for u in upper):
                    pieces = [parts[L - 1]] + [jnp.concatenate([parts[(i, "a")], parts[(i, "m")]]) for i in range(1, L - 1)]
                    flight[("upper", "z")] = (None, spread(jnp.concatenate(pieces, axis=1)))
        return outs

    for layer in reversed(range(L - 1)):
        x, qkv, att, mid = states[layer]
        lg = gains[4 * layer : 4 * layer + 4]
        outs = mlp_backward(core, own_wide, state, mid, att, *weights[layer], lg)
        grad_mid, keep, send, vec_mlp = land(outs)
        start((layer, "m"), "c", Slab([keep]), sent=send)
        if layer:
            outs = att_backward(core, own_wide, grad_mid, x, qkv, *weights[layer], lg, segments)
            state, keep, send, vec_att = land(outs)
            start((layer, "a"), "c", Slab([keep]), sent=send)
            vecs = [vec_att[:2], vec_mlp[:2]] + vecs
        else:
            vec = jnp.concatenate([jnp.zeros((2, D), f32), vec_mlp[:2]] + vecs)
            vec = jnp.pad(vec, ((0, -vec.shape[0] % 16), (0, 0)))
            outs = att_backward(core, own_wide, grad_mid, x, qkv, *weights[layer], lg, segments, (first_vec, inputs, vec))
            keep, send, tkeep, tsend = land(outs)
            tkeep = tkeep.reshape(n_dp, own_dim, -1)
            start("table", "c", Slab([tkeep]), sent=tsend.reshape(tkeep.shape))
            start((layer, "a"), "c", Slab([keep]), sent=send)
    head_in = (scale.reshape(1), every, rff_low, read_low, read_w.T)
    head = land(head_backward(*head_in, 0, 2))
    read_step, rff_step, sums0, sums1 = land(head_backward(*head_in, 1, 2, head))
    head_sums = sums0 + sums1
    while flight:
        land(())
    side = parts["table"].reshape(n_dp // 2, -1, D)
    both = spread(jnp.concatenate([jnp.concatenate([parts[(0, "a")], parts[(0, "m")]]), side], axis=1))
    cut = own_wide // n_narrow
    sums = jnp.concatenate([add_up(list(both)), add_up(list(done["upper"]))])

    first_dp = (me_dp == 0).astype(f32)
    first_narrow = (me_narrow == 0).astype(f32)
    local = square_sum([sums]) * (scale * scale)
    local = local + first_dp * head_sums[0, 0]
    ridge = first_dp * head_sums[1, 0]
    total_square, error_total, ridge_total = total_of([local, first_narrow * error_sum, ridge])
    loss_sum = error_total + l2_weight * image_total * ridge_total
    clip_norm = jnp.sqrt(total_square)
    factor = jnp.minimum(1.0, clip_bound / clip_norm)

    shares = join_narrow(sums.astype(bf16))
    low = cut + side.shape[1]
    starts = [0, *(low + i * cut for i in range(1, L - 1)), low]
    rows = jnp.stack([jnp.concatenate([s[a : a + cut] for s in shares]) for a in starts])
    grad_mats = rows
    lanes = jnp.concatenate([s[cut:low].reshape(own_dim, chunk) for s in shares], axis=1)
    grad_embed = lanes[:, :first_vec]
    grad_vector = lanes[:, first_vec : first_vec + vectors].T.astype(f32)

    def flat(*arrays):
        turned = [jnp.swapaxes(a, -1, -2) for a in arrays]
        return [t.reshape(-1, t.shape[-1]) for t in turned]

    def back(arrays, shape):
        return [jnp.swapaxes(a.reshape(shape), -1, -2) for a in arrays]

    two = jnp.stack([factor, factor])
    of_read, of_rff = optimizer(
        two,
        [
            ([*flat(read_w, read_m, read_v, read_e), read_step], 200),
            ([rff_w, rff_m, rff_v, rff_e, rff_step], 128),
        ],
        16,
    )
    tail = jnp.stack([factor * scale, factor * scale])
    of_mats, of_embed = optimizer(
        tail,
        [
            ([*flat(mats_w, mats_m, mats_v, mats_e), grad_mats.reshape(-1, D)], math.gcd(L * own_wide, 216)),
            ([*flat(embed_w, embed_m, embed_v, embed_e), grad_embed], own_dim),
        ],
        11,
    )
    outs = [loss_sum, image_total, clip_norm]
    outs += back(of_embed, (own_dim, first_vec))
    outs += adamw(vector_w, vector_m, vector_v, vector_e, grad_vector * (factor * scale), rate_vector, 0.0)
    outs += back(of_mats, (L, own_wide, D))
    outs += of_rff
    outs += back(of_read, read_step.shape)
    return tuple(outs)


def solution(mesh):
    n_dp, n_narrow = mesh.shape["dp"], mesh.shape["narrow"]
    fine = jax.sharding.Mesh(mesh.devices.reshape(n_dp // 2, 2, n_narrow // 2, 2), ALL)
    rows = P(ALL)
    table, mats, rff, read = P(None, DP), P(None, None, DP), P(None, NARROW), P(NARROW, None)
    ins = (P(ALL, None),) + (rows,) * 5 + (table,) * 8 + (mats,) * 4 + (rff,) * 4 + (read,) * 4
    outs = (P(),) * 3 + (table,) * 10 + (mats,) * 5 + (rff,) * 5 + (read,) * 5
    return jax.shard_map(shards, mesh=fine, in_specs=ins, out_specs=outs, check_vma=False)
```

```python
import functools
import math
import jax
import jax.numpy as jnp
from jax import lax
from jax.experimental import pallas as pl
from jax.experimental.pallas import tpu as pltpu
from jax.sharding import PartitionSpec as P

D = 384
HEADS = 6
HD = 64
MLP = 1536
SEQ = 256
norm_eps = 1e-06
EXP_SCALE = 1.4426950408889634 * HD ** (-0.5)
GELU_A = 0.7978845608028654
GELU_B = 0.044715
f32 = jnp.float32
bf16 = jnp.bfloat16


def nn(a, b):
    return lax.dot_general(a, b, (((1,), (0,)), ((), ())), preferred_element_type=f32)


def nt(a, b):
    return lax.dot_general(a, b, (((1,), (1,)), ((), ())), preferred_element_type=f32)


def tn(a, b):
    return lax.dot_general(a, b, (((0,), (0,)), ((), ())), preferred_element_type=f32)


def unit(rows):
    centred = rows - jnp.mean(rows, axis=-1, keepdims=True)
    inverse = lax.rsqrt(jnp.mean(centred * centred, axis=-1, keepdims=True) + norm_eps)
    return centred * inverse, inverse


def unit_back(u, inverse, gain, grad):
    scaled = grad * gain
    return inverse * (
        scaled
        - jnp.mean(scaled, axis=-1, keepdims=True)
        - u * jnp.mean(scaled * u, axis=-1, keepdims=True)
    )


def gelu_parts(x):
    x2 = x * x
    t = jnp.tanh(GELU_A * x * (1.0 + GELU_B * x2))
    half = 0.5 * (1.0 + t)
    return half, t, x2


def gelu_value(x):
    half, _, _ = gelu_parts(x)
    return x * half


def gelu_both(x):
    half, t, x2 = gelu_parts(x)
    slope = half + 0.5 * x * (1.0 - t * t) * (GELU_A * (1.0 + 3.0 * GELU_B * x2))
    return x * half, slope


def layer_rows(x, wa_ref, wu_ref, wd_ref, gains, seg_col, seg_row):
    g1, b1, g2, b2 = (gains[i : i + 1, :] for i in range(4))
    u, _ = unit(x)
    normed = (u * g1 + b1).astype(bf16)
    qkv = nt(normed, wa_ref[: 3 * D, :]).astype(bf16)
    heads = []
    rows = x.shape[0]
    for s in range(rows // SEQ):
        r = slice(s * SEQ, (s + 1) * SEQ)
        same = seg_col[r, :] == seg_row[:, r]
        outs = []
        for h in range(HEADS):
            q = qkv[r, h * HD : (h + 1) * HD]
            k = qkv[r, D + h * HD : D + (h + 1) * HD]
            v = qkv[r, 2 * D + h * HD : 2 * D + (h + 1) * HD]
            sc = jnp.where(same, nt(q, k), -1e30)
            e = jnp.exp2((sc - jnp.max(sc, axis=-1, keepdims=True)) * EXP_SCALE)
            p = (e * (1.0 / jnp.sum(e, axis=-1, keepdims=True))).astype(bf16)
            outs.append(nn(p, v))
        heads.append(jnp.concatenate(outs, axis=1))
    att = jnp.concatenate(heads, axis=0).astype(bf16)
    x1 = x + nt(att, wa_ref[3 * D :, :])
    u2, _ = unit(x1)
    second = (u2 * g2 + b2).astype(bf16)
    hidden = gelu_value(nt(second, wu_ref[...])).astype(bf16)
    out = x1 + nn(hidden, wd_ref[...])
    return qkv, att, x1, out


def fwd_kernel(x_ref, wa_ref, wu_ref, wd_ref, g_ref, sc_ref, sr_ref, qkv_ref, att_ref, x1_ref, out_ref):
    qkv, att, x1, out = layer_rows(x_ref[...], wa_ref, wu_ref, wd_ref, g_ref[...], sc_ref[...], sr_ref[0])
    qkv_ref[...] = qkv
    att_ref[...] = att
    x1_ref[...] = x1
    out_ref[...] = out


def first_kernel(p_ref, pos_ref, e_ref, wa_ref, wu_ref, wd_ref, g_ref, sc_ref, sr_ref, in_ref, x_ref, qkv_ref, att_ref, x1_ref, out_ref):
    pos = pos_ref[...]
    patch = jnp.where(pos != 0, p_ref[...].astype(f32), 0.0).astype(bf16)
    lanes = e_ref.shape[1] - p_ref.shape[1]
    table = (pos == lax.broadcasted_iota(jnp.int32, (pos.shape[0], lanes), 1)).astype(f32).astype(bf16)
    full = jnp.concatenate([patch, table], axis=1)
    in_ref[...] = full
    x = nt(full, e_ref[...])
    x_ref[...] = x
    qkv, att, x1, out = layer_rows(x, wa_ref, wu_ref, wd_ref, g_ref[...], sc_ref[...], sr_ref[0])
    qkv_ref[...] = qkv
    att_ref[...] = att
    x1_ref[...] = x1
    out_ref[...] = out


def join_kernel(plan, n_in, flag_ref, *refs):
    for src, dst in plan(flag_ref[0], refs[:n_in], refs[n_in:]):
        dst[...] = src[...]


def join(plan, flag, ins, shapes):
    return pl.pallas_call(
        functools.partial(join_kernel, plan, len(ins)),
        in_specs=[smem_spec()] + [vmem_spec()] * len(ins),
        out_specs=[vmem_spec()] * len(shapes),
        out_shape=[jax.ShapeDtypeStruct(s, bf16) for s in shapes],
        compiler_params=pltpu.CompilerParams(vmem_limit_bytes=24 << 20),
        cost_estimate=lasting(1),
        name="join",
    )(flag, *ins)


def joined_kernel(core_ref, h_ref, hg_ref, t_ref, tg_ref, p_ref, pos_ref, g_ref, sc_ref, sr_ref, in_ref, x_ref, qkv_ref, att_ref, x1_ref, out_ref, wo_ref, w_ref, tab_ref, sems, out_sem):
    step = pl.program_id(0)
    cells, piece = h_ref.shape[0], h_ref.shape[1]
    core = core_ref[0]
    copies = []
    for src, at in ((h_ref, core), (hg_ref, 1 - core)):
        for i in range(cells):
            copies.append((src.at[i], w_ref.at[pl.ds(pl.multiple_of((2 * i + at) * piece, 16), piece)]))
    for src, at in ((t_ref, core), (tg_ref, 1 - core)):
        for y in range(t_ref.shape[1]):
            copies.append((src.at[:, y], tab_ref.at[2 * y + at]))
    copies = [pltpu.make_async_copy(a, b, sems.at[i]) for i, (a, b) in enumerate(copies)]
    result = pltpu.make_async_copy(w_ref, wo_ref, out_sem)

    @pl.when(step == 0)
    def _():
        for c in copies:
            c.start()
        for c in copies:
            c.wait()
        result.start()

    pos = pos_ref[...]
    patch = jnp.where(pos != 0, p_ref[...].astype(f32), 0.0).astype(bf16)
    lanes = in_ref.shape[1] - p_ref.shape[1]
    onehot = (pos == lax.broadcasted_iota(jnp.int32, (pos.shape[0], lanes), 1)).astype(f32).astype(bf16)
    full = jnp.concatenate([patch, onehot], axis=1)
    in_ref[...] = full
    width = tab_ref.shape[3]
    x = sum(nt(full[:, n * width : (n + 1) * width], tab_ref[n].reshape(D, width)) for n in range(tab_ref.shape[0]))
    x_ref[...] = x
    qkv, att, x1, out = layer_rows(x, w_ref.at[: 4 * D], w_ref.at[4 * D : 8 * D], w_ref.at[8 * D :], g_ref[...], sc_ref[...], sr_ref[0])
    qkv_ref[...] = qkv
    att_ref[...] = att
    x1_ref[...] = x1
    out_ref[...] = out

    @pl.when(step == pl.num_programs(0) - 1)
    def _():
        result.wait()


def joined_forward(core, half, half_got, table, table_got, patches, pos, gains, seg, step_rows=512):
    rows, patch = patches.shape
    lanes = 2 * table.shape[1] * table.shape[3]
    steps = rows // step_rows
    anywhere = pl.BlockSpec(memory_space=pl.ANY)
    return pl.pallas_call(
        joined_kernel,
        grid=(steps,),
        in_specs=[
            smem_spec(),
            *[anywhere] * 4,
            rows_spec(step_rows, patch),
            rows_spec(step_rows, 1),
            whole_spec(gains.shape),
            rows_spec(step_rows, 1),
            pl.BlockSpec((1, 1, step_rows), lambda i: (i, 0, 0)),
        ],
        out_specs=[rows_spec(step_rows, lanes), rows_spec(step_rows, D), rows_spec(step_rows, 3 * D), rows_spec(step_rows, D), rows_spec(step_rows, D), rows_spec(step_rows, D), anywhere],
        out_shape=[
            jax.ShapeDtypeStruct((rows, lanes), bf16),
            jax.ShapeDtypeStruct((rows, D), f32),
            jax.ShapeDtypeStruct((rows, 3 * D), bf16),
            jax.ShapeDtypeStruct((rows, D), bf16),
            jax.ShapeDtypeStruct((rows, D), f32),
            jax.ShapeDtypeStruct((rows, D), f32),
            jax.ShapeDtypeStruct((12 * D, D), bf16),
        ],
        scratch_shapes=[
            pltpu.VMEM((12 * D, D), bf16),
            pltpu.VMEM((2 * table.shape[1], *table.shape[:1], *table.shape[2:]), bf16),
            pltpu.SemaphoreType.DMA((2 * half.shape[0] + 2 * table.shape[1],)),
            pltpu.SemaphoreType.DMA(()),
        ],
        compiler_params=params(),
        cost_estimate=lasting(18),
        name="first_fwd",
    )(core, half, half_got, table, table_got, patches, pos[:, None], gains, seg[:, None], seg.reshape(steps, 1, step_rows))


def rows_spec(r, width):
    return pl.BlockSpec((r, width), lambda i: (i, 0))


def whole_spec(shape):
    return pl.BlockSpec(shape, lambda *i: (0,) * len(shape))


def third_spec(block):
    return pl.BlockSpec((4 * D, D), lambda *i: (block, 0))


def params(mb=56, n=1):
    return pltpu.CompilerParams(dimension_semantics=("arbitrary",) * n, vmem_limit_bytes=mb << 20)


def lasting(us):
    return pl.CostEstimate(flops=int(us * 1e9), bytes_accessed=int(us * 2e6), transcendentals=0)


def layer_forward(x, w, layer, gains, seg, step_rows=512):
    rows = x.shape[0]
    steps = rows // step_rows
    return pl.pallas_call(
        fwd_kernel,
        grid=(steps,),
        in_specs=[
            rows_spec(step_rows, D),
            *(third_spec(3 * layer + i) for i in range(3)),
            whole_spec(gains.shape),
            rows_spec(step_rows, 1),
            pl.BlockSpec((1, 1, step_rows), lambda i: (i, 0, 0)),
        ],
        out_specs=[rows_spec(step_rows, 3 * D), rows_spec(step_rows, D), rows_spec(step_rows, D), rows_spec(step_rows, D)],
        out_shape=[
            jax.ShapeDtypeStruct((rows, 3 * D), bf16),
            jax.ShapeDtypeStruct((rows, D), bf16),
            jax.ShapeDtypeStruct((rows, D), f32),
            jax.ShapeDtypeStruct((rows, D), f32),
        ],
        compiler_params=params(),
        cost_estimate=lasting(17),
        name="layer_fwd",
    )(x, w, w, w, gains, seg[:, None], seg.reshape(steps, 1, step_rows))


def first_forward(patches, pos, e, w, layer, gains, seg, step_rows=512):
    rows, patch = patches.shape
    lanes = e.shape[1]
    steps = rows // step_rows
    return pl.pallas_call(
        first_kernel,
        grid=(steps,),
        in_specs=[
            rows_spec(step_rows, patch),
            rows_spec(step_rows, 1),
            whole_spec(e.shape),
            *(third_spec(3 * layer + i) for i in range(3)),
            whole_spec(gains.shape),
            rows_spec(step_rows, 1),
            pl.BlockSpec((1, 1, step_rows), lambda i: (i, 0, 0)),
        ],
        out_specs=[rows_spec(step_rows, lanes), rows_spec(step_rows, D), rows_spec(step_rows, 3 * D), rows_spec(step_rows, D), rows_spec(step_rows, D), rows_spec(step_rows, D)],
        out_shape=[
            jax.ShapeDtypeStruct((rows, lanes), bf16),
            jax.ShapeDtypeStruct((rows, D), f32),
            jax.ShapeDtypeStruct((rows, 3 * D), bf16),
            jax.ShapeDtypeStruct((rows, D), bf16),
            jax.ShapeDtypeStruct((rows, D), f32),
            jax.ShapeDtypeStruct((rows, D), f32),
        ],
        compiler_params=params(),
        cost_estimate=lasting(18),
        name="first_fwd",
    )(patches, pos[:, None], e, w, w, w, gains, seg[:, None], seg.reshape(steps, 1, step_rows))


def last_fwd_kernel(cls_ref, x_ref, wa_ref, wu_ref, wd_ref, g_ref, sk_ref, sq_ref, kv_ref, xc_ref, q_ref, att_ref, x1_ref, out_ref, feat_ref):
    g1, b1, g2, b2, g3, b3 = (g_ref[i : i + 1, :] for i in range(6))
    u, _ = unit(x_ref[...])
    normed = (u * g1 + b1).astype(bf16)
    kv = nt(normed, wa_ref[D : 3 * D, :]).astype(bf16)
    kv_ref[...] = kv
    slots = xc_ref.shape[0]
    for i in range(slots):
        xc_ref[i : i + 1, :] = x_ref[pl.ds(cls_ref[i], 1), :]
    xc = xc_ref[...]
    uc, _ = unit(xc)
    q = nt((uc * g1 + b1).astype(bf16), wa_ref[:D, :]).astype(bf16)
    q_ref[...] = q
    same = sq_ref[...] == sk_ref[...]
    outs = []
    for h in range(HEADS):
        c = slice(h * HD, (h + 1) * HD)
        sc = jnp.where(same, nt(q[:, c], kv[:, c]) * HD ** (-0.5), -1e30)
        e = jnp.exp(sc - jnp.max(sc, axis=-1, keepdims=True))
        p = (e * (1.0 / jnp.sum(e, axis=-1, keepdims=True))).astype(bf16)
        outs.append(nn(p, kv[:, D + h * HD : D + (h + 1) * HD]))
    att = jnp.concatenate(outs, axis=1).astype(bf16)
    att_ref[...] = att
    x1 = xc + nt(att, wa_ref[3 * D :, :])
    x1_ref[...] = x1
    u2, _ = unit(x1)
    second = (u2 * g2 + b2).astype(bf16)
    hidden = gelu_value(nt(second, wu_ref[...])).astype(bf16)
    out = x1 + nn(hidden, wd_ref[...])
    out_ref[...] = out
    u3, _ = unit(out)
    feat_ref[...] = (u3 * g3 + b3).astype(bf16)


def put_halves(core_ref, acc_ref, keep_ref, send_ref):
    half = keep_ref.shape[1]
    mine = core_ref[0] * half
    other = (1 - core_ref[0]) * half
    for i in range(keep_ref.shape[0]):
        base = i * 2 * half
        keep_ref[i] = acc_ref[pl.ds(base + mine, half), :].astype(bf16)
        send_ref[i] = acc_ref[pl.ds(base + other, half), :].astype(bf16)


def smem_spec():
    return pl.BlockSpec(memory_space=pltpu.SMEM)


def vmem_spec():
    return pl.BlockSpec(memory_space=pltpu.VMEM)


def last_forward(cls, x, w, layer, gains, seg, seg_cls):
    rows, slots = x.shape[0], cls.shape[0]
    return pl.pallas_call(
        last_fwd_kernel,
        grid=(1,),
        in_specs=[smem_spec(), whole_spec(x.shape), *(third_spec(3 * layer + i) for i in range(3)), *[vmem_spec()] * 3],
        out_specs=[vmem_spec()] * 7,
        out_shape=[
            jax.ShapeDtypeStruct((rows, 2 * D), bf16),
            jax.ShapeDtypeStruct((slots, D), f32),
            jax.ShapeDtypeStruct((slots, D), bf16),
            jax.ShapeDtypeStruct((slots, D), bf16),
            jax.ShapeDtypeStruct((slots, D), f32),
            jax.ShapeDtypeStruct((slots, D), f32),
            jax.ShapeDtypeStruct((slots, D), bf16),
        ],
        compiler_params=params(),
        cost_estimate=lasting(9),
        name="last_fwd",
    )(cls, x, w, w, w, gains, seg[None, :], seg_cls[:, None])


def last_bwd_kernel(cls_ref, core_ref, df_ref, x_ref, wa_ref, wu_ref, wd_ref, g_ref, sk_ref, sq_ref, kv_ref, xc_ref, q_ref, att_ref, x1_ref, xo_ref, dx_ref, keep_ref, send_ref, dv_ref, dn_ref, dw_ref):
    g1, b1, g2, b2, g3, b3 = (g_ref[i : i + 1, :] for i in range(6))
    slots = xc_ref.shape[0]
    df = df_ref[...]
    u3, i3 = unit(xo_ref[...])
    dxo = unit_back(u3, i3, g3, df)
    dg3 = jnp.sum(df * u3, axis=0, keepdims=True)
    db3 = jnp.sum(df, axis=0, keepdims=True)
    branch = dxo.astype(bf16)
    u2, i2 = unit(x1_ref[...])
    second = (u2 * g2 + b2).astype(bf16)
    value, slope = gelu_both(nt(second, wu_ref[...]))
    dpre = (nt(branch, wd_ref[...]) * slope).astype(bf16)
    dw_ref[4 * D + MLP :, :] = tn(value.astype(bf16), branch)
    dw_ref[4 * D : 4 * D + MLP, :] = tn(dpre, second)
    dsecond = nn(dpre, wu_ref[...])
    dg2 = jnp.sum(dsecond * u2, axis=0, keepdims=True)
    db2 = jnp.sum(dsecond, axis=0, keepdims=True)
    dx1 = dxo + unit_back(u2, i2, g2, dsecond)
    ab = dx1.astype(bf16)
    datt = nn(ab, wa_ref[3 * D :, :]).astype(bf16)
    dw_ref[3 * D : 4 * D, :] = tn(ab, att_ref[...])
    same = sq_ref[...] == sk_ref[...]
    q, kv = q_ref[...], kv_ref[...]
    dqs, dks, dvs = [], [], []
    for h in range(HEADS):
        c = slice(h * HD, (h + 1) * HD)
        k, v = kv[:, c], kv[:, D + h * HD : D + (h + 1) * HD]
        sc = jnp.where(same, nt(q[:, c], k) * HD ** (-0.5), -1e30)
        e = jnp.exp(sc - jnp.max(sc, axis=-1, keepdims=True))
        p = e * (1.0 / jnp.sum(e, axis=-1, keepdims=True))
        dp = nt(datt[:, c], v)
        ds = (p * (dp - jnp.sum(dp * p, axis=-1, keepdims=True))).astype(bf16)
        dvs.append(tn(p.astype(bf16), datt[:, c]))
        dks.append(tn(ds, q[:, c]) * HD ** (-0.5))
        dqs.append(nn(ds, k) * HD ** (-0.5))
    dq = jnp.concatenate(dqs, axis=1).astype(bf16)
    dkv = jnp.concatenate(dks + dvs, axis=1).astype(bf16)
    u, i1 = unit(x_ref[...])
    normed = (u * g1 + b1).astype(bf16)
    dw_ref[D : 3 * D, :] = tn(dkv, normed)
    uc, _ = unit(xc_ref[...])
    dw_ref[:D, :] = tn(dq, (uc * g1 + b1).astype(bf16))
    dn_ref[...] = nn(dkv, wa_ref[D : 3 * D, :])
    dnc = nn(dq, wa_ref[:D, :])
    for i in range(slots):
        at = pl.ds(cls_ref[i], 1)
        dn_ref[at, :] = dn_ref[at, :] + dnc[i : i + 1, :]
    dn = dn_ref[...]
    dg1 = jnp.sum(dn * u, axis=0, keepdims=True)
    db1 = jnp.sum(dn, axis=0, keepdims=True)
    dx_ref[...] = unit_back(u, i1, g1, dn)
    for i in range(slots):
        at = pl.ds(cls_ref[i], 1)
        dx_ref[at, :] = dx_ref[at, :] + dx1[i : i + 1, :]
    dv_ref[...] = jnp.concatenate([dg1, db1, dg2, db2, dg3, db3, jnp.zeros((2, D), f32)], axis=0)
    put_halves(core_ref, dw_ref, keep_ref, send_ref)


def last_backward(cls, core, wide, df, x, w, layer, gains, seg, seg_cls, kv, xc, q, att, x1, xo):
    rows = x.shape[0]
    return pl.pallas_call(
        last_bwd_kernel,
        grid=(1,),
        in_specs=[smem_spec(), smem_spec(), vmem_spec(), whole_spec(x.shape), *(third_spec(3 * layer + i) for i in range(3)), *[vmem_spec()] * 9],
        out_specs=[vmem_spec()] * 4,
        out_shape=[
            jax.ShapeDtypeStruct((rows, D), f32),
            *[jax.ShapeDtypeStruct((12 * D // wide, wide // 2, D), bf16)] * 2,
            jax.ShapeDtypeStruct((8, D), f32),
        ],
        scratch_shapes=[pltpu.VMEM((rows, D), f32), pltpu.VMEM((12 * D, D), f32)],
        compiler_params=params(),
        cost_estimate=lasting(15),
        name="last_bwd",
    )(cls, core, df, x, w, w, w, gains, seg[None, :], seg_cls[:, None], kv, xc, q, att, x1, xo)


def mlp_bwd_kernel(core_ref, dxo_ref, x1_ref, att_ref, wu_ref, wd_ref, g_ref, dx1_ref, keep_ref, send_ref, dv_ref, acc_ref):
    step = pl.program_id(0)
    g2, b2 = g_ref[2:3, :], g_ref[3:4, :]
    dxo = dxo_ref[...]
    branch = dxo.astype(bf16)
    u2, i2 = unit(x1_ref[...])
    second = (u2 * g2 + b2).astype(bf16)
    value, slope = gelu_both(nt(second, wu_ref[...]))
    hidden = value.astype(bf16)
    dpre = (nt(branch, wd_ref[...]) * slope).astype(bf16)
    dsecond = nn(dpre, wu_ref[...])
    sums = jnp.concatenate([jnp.sum(dsecond * u2, axis=0, keepdims=True), jnp.sum(dsecond, axis=0, keepdims=True), jnp.zeros((6, D), f32)], axis=0)
    dx1 = dxo + unit_back(u2, i2, g2, dsecond)
    dx1_ref[...] = dx1
    ab = dx1.astype(bf16)
    last = pl.num_programs(0) - 1

    @pl.when(step == 0)
    def _():
        acc_ref[:D, :] = tn(ab, att_ref[...])
        acc_ref[D : D + MLP, :] = tn(dpre, second)
        acc_ref[D + MLP :, :] = tn(hidden, branch)
        dv_ref[...] = sums

    @pl.when(step > 0)
    def _():
        acc_ref[:D, :] += tn(ab, att_ref[...])
        acc_ref[D : D + MLP, :] += tn(dpre, second)
        acc_ref[D + MLP :, :] += tn(hidden, branch)
        dv_ref[...] += sums

    @pl.when(step == last)
    def _():
        put_halves(core_ref, acc_ref, keep_ref, send_ref)


def mlp_backward(core, wide, dxo, x1, att, w, layer, gains, step_rows=512):
    rows = x1.shape[0]
    steps = rows // step_rows
    return pl.pallas_call(
        mlp_bwd_kernel,
        grid=(steps,),
        in_specs=[smem_spec(), *[rows_spec(step_rows, D)] * 3, third_spec(3 * layer + 1), third_spec(3 * layer + 2), whole_spec(gains.shape)],
        out_specs=[rows_spec(step_rows, D), *[whole_spec((9 * D // wide, wide // 2, D))] * 2, whole_spec((8, D))],
        out_shape=[jax.ShapeDtypeStruct((rows, D), f32), *[jax.ShapeDtypeStruct((9 * D // wide, wide // 2, D), bf16)] * 2, jax.ShapeDtypeStruct((8, D), f32)],
        scratch_shapes=[pltpu.VMEM((9 * D, D), f32)],
        compiler_params=params(),
        cost_estimate=lasting(16),
        name="mlp_bwd",
    )(core, dxo, x1, att, w, w, gains)


def att_bwd_kernel(first_vec, *refs):
    core_ref, dx1_ref, x_ref, qkv_ref, w_ref, g_ref, sc_ref, sr_ref, *refs = refs
    if first_vec:
        in_ref, vec_ref, keep_ref, send_ref, tkeep_ref, tsend_ref, acc_ref, dv_ref, table_ref = refs
    else:
        dx_ref, keep_ref, send_ref, dv_ref, acc_ref = refs
    step = pl.program_id(0)
    g1, b1 = g_ref[0:1, :], g_ref[1:2, :]
    dx1 = dx1_ref[...]
    ab = dx1.astype(bf16)
    datt = nn(ab, w_ref[3 * D : 4 * D, :]).astype(bf16)
    qkv = qkv_ref[...]
    parts = []
    for s in range(x_ref.shape[0] // SEQ):
        r = slice(s * SEQ, (s + 1) * SEQ)
        same = sc_ref[r, :] == sr_ref[0][:, r]
        dqs, dks, dvs = [], [], []
        for h in range(HEADS):
            q = qkv[r, h * HD : (h + 1) * HD]
            k = qkv[r, D + h * HD : D + (h + 1) * HD]
            v = qkv[r, 2 * D + h * HD : 2 * D + (h + 1) * HD]
            da = datt[r, h * HD : (h + 1) * HD]
            sc = jnp.where(same, nt(k, q), -1e30)
            e = jnp.exp2((sc - jnp.max(sc, axis=0, keepdims=True)) * EXP_SCALE)
            p = e * (1.0 / jnp.sum(e, axis=0, keepdims=True))
            dp = nt(v, da)
            ds = (p * (dp - jnp.sum(dp * p, axis=0, keepdims=True))).astype(bf16)
            dvs.append(nn(p.astype(bf16), da))
            dks.append(nn(ds, q) * HD ** (-0.5))
            dqs.append(tn(ds, k) * HD ** (-0.5))
        parts.append(jnp.concatenate(dqs + dks + dvs, axis=1).astype(bf16))
    dqkv = jnp.concatenate(parts, axis=0)
    u, i1 = unit(x_ref[...])
    normed = (u * g1 + b1).astype(bf16)
    dn = nn(dqkv, w_ref[: 3 * D, :])
    sums = jnp.concatenate([jnp.sum(dn * u, axis=0, keepdims=True), jnp.sum(dn, axis=0, keepdims=True), jnp.zeros((6, D), f32)], axis=0)
    dx = dx1 + unit_back(u, i1, g1, dn)
    if first_vec:
        grad_table = tn(dx.astype(bf16), in_ref[...])
    else:
        dx_ref[...] = dx
    last = pl.num_programs(0) - 1

    @pl.when(step == 0)
    def _():
        acc_ref[...] = tn(dqkv, normed)
        if first_vec:
            table_ref[...] = grad_table
        dv_ref[...] = sums

    @pl.when(step > 0)
    def _():
        acc_ref[...] += tn(dqkv, normed)
        if first_vec:
            table_ref[...] += grad_table
        dv_ref[...] += sums

    @pl.when(step == last)
    def _():
        put_halves(core_ref, acc_ref, keep_ref, send_ref)
        if first_vec:
            rows, lanes = vec_ref.shape[0], table_ref.shape[1]
            vec = vec_ref[...] + jnp.concatenate([dv_ref[...], jnp.zeros((rows - 8, D), f32)], axis=0)
            at = lax.broadcasted_iota(jnp.int32, (rows, lanes), 1) - first_vec
            pick = (at == lax.broadcasted_iota(jnp.int32, (rows, lanes), 0)).astype(f32).astype(bf16)
            table_ref[...] += tn(vec.astype(bf16), pick)
            half = lanes // 2
            mine = pl.multiple_of(core_ref[0] * half, 128)
            other = pl.multiple_of((1 - core_ref[0]) * half, 128)
            if len(tkeep_ref.shape) == 2:
                tkeep_ref[...] = table_ref[:, pl.ds(mine, half)].astype(bf16)
                tsend_ref[...] = table_ref[:, pl.ds(other, half)].astype(bf16)
            else:
                put_cells(table_ref, mine, half, tkeep_ref)
                put_cells(table_ref, other, half, tsend_ref)


PACK = ((0, 0, 32, 0, 0), (0, 32, 16, 0, 1), (1, 0, 16, 16, 1), (1, 16, 32, 0, 2))


def put_cells(table_ref, base, half, out_ref):
    for d in range(D // 48):
        for y in range(half // 256):
            cell = d * (half // 256) + y
            for block, row, count, to_row, to_block in PACK:
                lane = pl.multiple_of(base + y * 256 + block * 128, 128)
                value = table_ref[d * 48 + row : d * 48 + row + count, pl.ds(lane, 128)]
                out_ref[cell, to_row : to_row + count, to_block * 128 : to_block * 128 + 128] = value.astype(bf16)


def att_backward(core, wide, dx1, x, qkv, w, layer, gains, seg, table=None, step_rows=512):
    rows = x.shape[0]
    steps = rows // step_rows
    parts = [jax.ShapeDtypeStruct((3 * D // wide, wide // 2, D), bf16)] * 2
    whole = [whole_spec(p.shape) for p in parts]
    acc = pltpu.VMEM((3 * D, D), f32)
    if table is None:
        first_vec, more, more_specs = 0, (), []
        out_specs = [rows_spec(step_rows, D), *whole, whole_spec((8, D))]
        out_shape = [jax.ShapeDtypeStruct((rows, D), f32), *parts, jax.ShapeDtypeStruct((8, D), f32)]
        scratch = [acc]
    else:
        first_vec, inputs, vec, packed = table
        lanes = inputs.shape[1]
        side = (D // 48 * (lanes // 512), 32, D) if packed else (D, lanes // 2)
        more, more_specs = (inputs, vec), [rows_spec(step_rows, lanes), whole_spec(vec.shape)]
        out_shape = [*parts, *[jax.ShapeDtypeStruct(side, bf16)] * 2]
        out_specs = [whole_spec(p.shape) for p in out_shape]
        scratch = [acc, pltpu.VMEM((8, D), f32), pltpu.VMEM((D, lanes), f32)]
    return pl.pallas_call(
        functools.partial(att_bwd_kernel, first_vec),
        grid=(steps,),
        in_specs=[
            smem_spec(),
            rows_spec(step_rows, D),
            rows_spec(step_rows, D),
            rows_spec(step_rows, 3 * D),
            third_spec(3 * layer),
            whole_spec(gains.shape),
            rows_spec(step_rows, 1),
            pl.BlockSpec((1, 1, step_rows), lambda i: (i, 0, 0)),
            *more_specs,
        ],
        out_specs=out_specs,
        out_shape=out_shape,
        scratch_shapes=scratch,
        compiler_params=params(),
        cost_estimate=lasting(18),
        name="att_bwd",
    )(core, dx1, x, qkv, w, gains, seg[:, None], seg.reshape(steps, 1, step_rows), *more)


HALF_PI = (1.5703125, 0.000483751296996, 7.54978995489e-08, 5.1266913e-12)


def sin_cos(x):
    k = jnp.round(x * 0.6366197723675814)
    r = x
    for part in HALF_PI:
        r = r - k * part
    r = jnp.clip(r, -1.0, 1.0)
    r2 = r * r
    s = r + r * r2 * (-1.6666654611e-1 + r2 * (8.3321608736e-3 + r2 * -1.9515295891e-4))
    c = 1.0 - 0.5 * r2 + r2 * r2 * (4.166664568298827e-2 + r2 * (-1.388731625493765e-3 + r2 * 2.443315711809948e-5))
    n = k.astype(jnp.int32)
    odd = (n & 1) == 1
    sin_v = jnp.where(odd, c, s)
    cos_v = jnp.where(odd, s, c)
    sin_v = jnp.where((n & 2) == 2, -sin_v, sin_v)
    cos_v = jnp.where(((n + 1) & 2) == 2, -cos_v, cos_v)
    return sin_v, cos_v


def head_kernel(several, skip, s_ref, all_ref, rff_ref, read_ref, w_ref, *refs):
    gread_ref, grff_ref, sums_ref, sin_ref, cos_ref = refs[skip:]
    features = all_ref[:, :D]
    logits = all_ref[:, D:]
    phases = nn(features, rff_ref[...])
    large = jnp.max(jnp.abs(phases)) > 5e4

    @pl.when(large)
    def _():
        sin_ref[...] = jnp.sin(phases)
        cos_ref[...] = jnp.cos(phases)

    @pl.when(jnp.logical_not(large))
    def _():
        sin_ref[...], cos_ref[...] = sin_cos(phases)

    lifted = cos_ref[...].astype(bf16)
    back = (-sin_ref[...] * nn(logits, read_ref[...])).astype(bf16)
    blocks = pl.num_programs(1)
    gread = tn(logits, lifted)
    grff = tn(features, back)
    if several:
        block = pl.program_id(1)

        @pl.when(block == 0)
        def _():
            gread_ref[...] = gread
            grff_ref[...] = grff

        @pl.when(block > 0)
        def _():
            gread_ref[...] += gread
            grff_ref[...] += grff

        @pl.when(block == blocks - 1)
        def _():
            head_finish(s_ref, w_ref, gread_ref[...], grff_ref[...], gread_ref, grff_ref, sums_ref)
    else:
        head_finish(s_ref, w_ref, gread, grff, gread_ref, grff_ref, sums_ref)


def head_finish(s_ref, w_ref, gread, grff, gread_ref, grff_ref, sums_ref):
    step = pl.program_id(0)
    w = w_ref[...]
    gread = gread * s_ref[0] + 2.0 * l2_weight * w
    grff = grff * s_ref[0]
    gread_ref[...] = gread
    grff_ref[...] = grff
    total = jnp.sum(jnp.sum(gread * gread, axis=0, keepdims=True)) + jnp.sum(jnp.sum(grff * grff, axis=0, keepdims=True))
    ridge = jnp.sum(jnp.sum(w * w, axis=0, keepdims=True))
    row = lax.broadcasted_iota(jnp.int32, (8, 128), 0)
    tile = jnp.where(row == 0, total, jnp.where(row == 1, ridge, 0.0))

    @pl.when(step == 0)
    def _():
        sums_ref[...] = tile

    @pl.when(step > 0)
    def _():
        sums_ref[...] += tile


def head_backward(scale, every, rff, read, w, part, parts, before=None, cols=256):
    n, classes = every.shape[0], read.shape[0]
    width = rff.shape[1]
    cols = min(cols, width // parts)
    rows = math.gcd(n, 768)
    steps = width // cols // parts
    base = part * steps
    col = lambda r: pl.BlockSpec((r, cols), lambda i, j: (0, base + i))
    more = () if before is None else before[:2]
    out = pl.pallas_call(
        functools.partial(head_kernel, n > rows, len(more)),
        grid=(steps, n // rows),
        in_specs=[smem_spec(), pl.BlockSpec((rows, every.shape[1]), lambda i, j: (j, 0)), col(D), col(classes), col(classes)] + [pl.BlockSpec(memory_space=pl.ANY)] * len(more),
        out_specs=[col(classes), col(D), whole_spec((8, 128))],
        out_shape=[jax.ShapeDtypeStruct((classes, width), f32), jax.ShapeDtypeStruct((D, width), f32), jax.ShapeDtypeStruct((8, 128), f32)],
        scratch_shapes=[pltpu.VMEM((rows, cols), f32)] * 2,
        input_output_aliases={5 + i: i for i in range(len(more))},
        compiler_params=params(56, 2),
        cost_estimate=lasting(8),
        name="head_bwd",
    )(scale, every, rff, read, w, *more)
    return out if before is None else [*out[:2], before[2], out[2]]


def optimizer_kernel(plan, f_ref, *refs):
    step = pl.program_id(0)
    ins, outs = refs[: 5 * len(plan)], refs[5 * len(plan) :]
    low = 0
    for i, count in enumerate(plan):

        @pl.when((step >= low) & (step < low + count))
        def _(i=i):
            *state, g_ref = ins[5 * i : 5 * i + 5]
            out = adamw(*(r[...] for r in state), g_ref[...].astype(f32) * f_ref[0], rate_matrix, weight_decay)
            for o_ref, value in zip(outs[5 * i : 5 * i + 5], out):
                o_ref[...] = value

        low += count


def optimizer(factor, groups, us):
    plan = [arrays[-1].shape[0] // rows for arrays, rows in groups]
    specs, out_specs, out_shape, args = [], [], [], []
    low = 0
    for (arrays, rows), count in zip(groups, plan):
        shape = arrays[-1].shape
        spec = pl.BlockSpec((rows, shape[1]), lambda i, low=low, count=count: (jnp.clip(i - low, 0, count - 1), 0))
        specs += [spec] * 5
        out_specs += [spec] * 5
        out_shape += [jax.ShapeDtypeStruct(shape, f32)] * 4 + [jax.ShapeDtypeStruct(shape, bf16)]
        args += arrays
        low += count
    out = pl.pallas_call(
        functools.partial(optimizer_kernel, plan),
        grid=(low,),
        in_specs=[smem_spec(), *specs],
        out_specs=out_specs,
        out_shape=out_shape,
        compiler_params=params(48),
        cost_estimate=lasting(us),
        name="optimizer",
    )(factor.reshape(1), *args)
    return [out[5 * i : 5 * i + 5] for i in range(len(groups))]


POS = 197
CLASSES = 1000
L = 3
IMG_SEQ = 6
STEP = 10
PART = 4 * D
WIDE = 3 * PART
clip_bound = 0.02
l2_weight = 0.1
beta_first = 0.5
beta_second = 0.5
adam_eps = 1e-08
weight_decay = 0.05
rate_matrix = 0.05
rate_vector = 0.5
ema_rate = 0.5
DP = ("dph", "dpl")
NARROW = ("ny", "nc")
ALL = DP + NARROW


def swap(rows, axis, mask):
    return lax.ppermute(rows, axis, [(i, i ^ mask) for i in range(lax.axis_size(axis))])


def add_up(terms):
    return sum(t.astype(f32) for t in terms)


def bits_of(size):
    return size.bit_length() - 1


def spread(cells, axes=DP):
    return lax.all_to_all(cells, axes, 0, 0)


def hop_y(cells):
    ny = lax.axis_size("ny")
    cells = cells.reshape(-1, ny, *cells.shape[1:])
    if ny > 2:
        return [lax.psum_scatter(cells, "ny", scatter_dimension=1, tiled=False)], None
    mine = lax.axis_index("ny")
    keep = lax.dynamic_index_in_dim(cells, mine, 1, keepdims=False)
    return [keep], swap(lax.dynamic_index_in_dim(cells, 1 - mine, 1, keepdims=False), "ny", 1)


def hop_x(rows):
    rows = rows.reshape(-1, 2, *rows.shape[1:])
    mine = lax.axis_index("dpl")
    keep = lax.dynamic_index_in_dim(rows, mine, 1, keepdims=False)
    return [keep], swap(lax.dynamic_index_in_dim(rows, 1 - mine, 1, keepdims=False), "dpl", 1)


def after(terms, got):
    return terms[0] if got is None else add_up([*terms, got]).astype(bf16)


def pair(keep, got, rows):
    return add_up([keep, got]).astype(bf16).reshape(-1, rows, D)


def unpacked(cell):
    left = jnp.concatenate([cell[:, :128], cell[:16, 128:256]])
    right = jnp.concatenate([cell[16:, 128:256], cell[:, 256:]])
    return jnp.concatenate([left, right], axis=1)


def join_narrow(piece):
    every = lax.all_gather(piece, NARROW, axis=0, tiled=False)
    cores, ys = lax.axis_size("nc"), lax.axis_size("ny")
    return [every[y * cores + core] for core in range(cores) for y in range(ys)]


def total_of(scalars):
    lane = lax.broadcasted_iota(jnp.int32, (8, 128), 1)
    tile = jnp.zeros((8, 128), f32)
    for i, value in enumerate(scalars):
        tile = jnp.where(lane == i, value, tile)
    world = lax.axis_size(ALL)
    every = lax.all_to_all(jnp.broadcast_to(tile[None], (world, 8, 128)), ALL, 0, 0)
    row = jnp.sum(every, axis=0)[0]
    return [row[i] for i in range(len(scalars))]


def adamw(weight, first, second, average, grad, rate, decay):
    first = beta_first * first + (1.0 - beta_first) * grad
    second = beta_second * second + (1.0 - beta_second) * grad * grad
    ahead = first / (1.0 - beta_first**STEP)
    behind = second / (1.0 - beta_second**STEP)
    weight = weight - rate * (ahead / (jnp.sqrt(behind) + adam_eps) + decay * weight)
    average = ema_rate * average + (1.0 - ema_rate) * weight
    return (weight, first, second, average, weight.astype(bf16))


def square_sum(arrays):
    return sum(jnp.sum(a.astype(f32) * a.astype(f32)) for a in arrays)


def shards(
    patches,
    pos_index,
    segments,
    cls_row,
    labels,
    img_count,
    embed_w,
    embed_m,
    embed_v,
    embed_e,
    vector_w,
    vector_m,
    vector_v,
    vector_e,
    mats_w,
    mats_m,
    mats_v,
    mats_e,
    rff_w,
    rff_m,
    rff_v,
    rff_e,
    read_w,
    read_m,
    read_v,
    read_e,
):
    n_dp, n_narrow = lax.axis_size(DP), lax.axis_size(NARROW)
    me_dp, me_narrow = lax.axis_index(DP), lax.axis_index(NARROW)
    own_dim = embed_w.shape[1]
    own_wide = mats_w.shape[2]
    core = lax.axis_index("nc").astype(jnp.int32).reshape(1)
    slots = cls_row.shape[0]
    table_rows = -(-(embed_w.shape[0] + vector_w.shape[0]) // 256) * 256
    chunk = table_rows // n_narrow

    tie = lax.optimization_barrier

    def small_facts():
        total = total_of([jnp.sum(img_count).astype(f32)])[0]
        slot_ids = jnp.arange(slots)
        valid = (slot_ids % IMG_SEQ < jnp.repeat(img_count, IMG_SEQ, total_repeat_length=slots)).astype(jnp.int32)
        return total, lax.all_gather(jnp.stack([labels, valid]), NARROW, axis=0)

    def low_head():
        pad = -slots % 16
        cls = jnp.concatenate([cls_row, jnp.broadcast_to(cls_row[-1:], (pad,))])
        return rff_w.astype(bf16), read_w.T.astype(bf16), cls, segments[cls]

    table = jnp.concatenate([embed_w.T, vector_w.T], axis=1).astype(bf16)
    table = jnp.pad(table, ((0, 0), (0, table_rows - table.shape[1])))
    table = lax.dynamic_slice_in_dim(table, me_narrow * chunk, chunk, 1)
    quarter = own_wide // n_narrow
    mats_own = lax.dynamic_slice_in_dim(jnp.swapaxes(mats_w, 1, 2), me_narrow * quarter, quarter, 1).astype(bf16)
    first_vec, vectors = embed_w.shape[0], vector_w.shape[0]
    rest = lax.all_gather(mats_own[1:], ALL, axis=1, tiled=True).reshape((L - 1) * WIDE, D)
    dph, dpl, ny = (lax.axis_size(a) for a in ("dph", "dpl", "ny"))

    if (dph, dpl, ny) == (4, 2, 2) and quarter % 16 == 0 and own_dim % 16 == 0 and chunk % 128 == 0:
        cut = quarter // 32 * 16

        def flag(axis, bit=0):
            return ((lax.axis_index(axis) >> bit) & 1).astype(jnp.int32).reshape(1)

        def both(src, got, dst, put):
            return lambda f, i, o: [(i[src], put(o[dst], f)), (i[got], put(o[dst], 1 - f))]

        def plan_of(*moves):
            return lambda f, i, o: [c for move in moves for c in move(f, i, o)]

        a, e = mats_own[:1], table[None]
        ga, ge = swap(a, "dph", 2), swap(e, "dph", 2)
        ahead = lambda o, f: o.at[:, f]
        a, e = join(plan_of(both(0, 1, 0, ahead), both(2, 3, 1, ahead)), flag("dph", 1), (a, ga, e, ge), ((1, 2, quarter, D), (1, 2, own_dim, chunk)))
        a, e = a.reshape(2, quarter, D), e.reshape(2, own_dim, chunk)
        (ga, ge), (image_total, facts) = tie(((swap(a, "dph", 1), swap(e, "dph", 1)), small_facts()))

        def split(f, i, o):
            out = []
            for src, at in ((i[0], f), (i[1], 1 - f)):
                out += [(src.at[:, :cut], o[0].at[:, at]), (src.at[:, cut:], o[1].at[:, at])]
            return out + [(i[2], o[2].at[:, f]), (i[3], o[2].at[:, 1 - f])]

        p, q, e = join(split, flag("dph"), (a, ga, e, ge), ((2, 2, cut, D), (2, 2, quarter - cut, D), (2, 2, own_dim, chunk)))
        p, q, e = (t.reshape(4, *t.shape[2:]) for t in (p, q, e))
        gp, gq, ge = swap(p, "dpl", 1), swap(q, "ny", 1), swap(e, "dpl", 1)
        (p,) = join(both(0, 1, 0, ahead), flag("dpl"), (p, gp), ((4, 2, cut, D),))
        (q,) = join(both(0, 1, 0, ahead), flag("ny"), (q, gq), ((4, 2, quarter - cut, D),))
        (e,) = join(both(0, 1, 0, ahead), flag("dpl"), (e, ge), ((4, 2, own_dim, chunk),))
        (gp, gq, ge), low_parts = tie(((swap(p, "ny", 1), swap(q, "dpl", 1), swap(e, "ny", 1)), low_head()))

        def last(f, i, o):
            fx, fy = f
            return [
                (i[0], o[0].at[:, :, fy, :cut]),
                (i[1], o[0].at[:, :, 1 - fy, :cut]),
                (i[2], o[0].at[:, fx, :, cut:]),
                (i[3], o[0].at[:, 1 - fx, :, cut:]),
                (i[4], o[1].at[:, :, fy]),
                (i[5], o[1].at[:, :, 1 - fy]),
            ]

        half, e = join(
            lambda f, i, o: last((f & 1, f >> 1), i, o),
            flag("dpl") + 2 * flag("ny"),
            (p, gp, q, gq, e, ge),
            ((4, 2, 2, quarter, D), (4, 2, 2, own_dim, chunk)),
        )
        half, e = half.reshape(n_dp * ny, quarter, D), e.reshape(n_dp, ny, own_dim, chunk)
        got, ge = swap(half, "nc", 1), swap(e, "nc", 1)
        holder, lane = first_vec // chunk, first_vec % chunk
        piece = jnp.where(core[0] == holder % 2, e[:, holder // 2], ge[:, holder // 2])
        gains = piece[:, :, lane : lane + vectors].reshape(D, vectors).T.astype(f32)
        outs = joined_forward(core, half, got, e, ge, patches, pos_index, gains[0:4], segments)
        inputs, x0, qkv0, att0, mid0, x1, mats0 = outs
    else:
        image_total, facts = small_facts()
        low_parts = low_head()
        table = lax.all_gather(table, ALL, axis=0)
        table = table.reshape(n_dp, n_narrow, own_dim, chunk).transpose(0, 2, 1, 3).reshape(D, table_rows)
        mats0 = lax.all_gather(mats_own[0], ALL, axis=0, tiled=True)
        gains = table[:, first_vec : first_vec + vectors].T.astype(f32)
        inputs, x0, qkv0, att0, mid0, x1 = first_forward(patches, pos_index, table, mats0, 0, gains[0:4], segments)
    rff_low, read_low, cls, seg_cls = low_parts
    group_labels = facts[:, 0].reshape(-1)
    group_valid = facts[:, 1].reshape(-1).astype(f32)[:, None]
    pad = cls.shape[0] - slots
    weights = [(mats0, 0)] + [(rest, i) for i in range(L - 1)]

    states = [(x0, qkv0, att0, mid0)]
    for layer in range(1, L - 1):
        qkv, att, mid, x2 = layer_forward(x1, *weights[layer], gains[4 * layer : 4 * layer + 4], segments)
        states.append((x1, qkv, att, mid))
        x1 = x2
    last_gains = gains[4 * L - 4 :]
    kept = last_forward(cls, x1, *weights[-1], last_gains, segments, seg_cls)
    features = kept[-1][:slots]

    group_rows = lax.all_gather(features, NARROW, axis=0, tiled=True)
    phases = nn(group_rows, rff_low)
    lifted = jnp.cos(phases).astype(bf16)
    partial = lax.all_gather(nt(lifted, read_low).astype(bf16), NARROW, axis=0)
    logits = jnp.sum(partial.astype(f32), axis=0)
    error = logits - (group_labels[:, None] == jnp.arange(CLASSES)[None, :]).astype(f32)
    error_sum = jnp.sum(group_valid * error * error)
    grad_logits = (2.0 * group_valid * error).astype(bf16)
    grad_phases = (-jnp.sin(phases) * nn(grad_logits, read_low)).astype(bf16)
    grad_pieces = nt(grad_phases, rff_low).reshape(n_narrow, slots, D)
    grad_features = jnp.sum(lax.all_to_all(grad_pieces, NARROW, 0, 0), axis=0)
    grad_features = jnp.pad(grad_features, ((0, pad), (0, 0)))

    own_logits = lax.dynamic_slice_in_dim(grad_logits, me_narrow * slots, slots, 0)
    own_rows, grad_features = tie((jnp.concatenate([features, own_logits], axis=1), grad_features))
    every = lax.all_gather(own_rows, ALL, axis=0, tiled=True)
    scale = 1.0 / image_total

    def flat(*arrays):
        turned = [jnp.swapaxes(a, -1, -2) for a in arrays]
        return [t.reshape(-1, t.shape[-1]) for t in turned]

    packed = own_dim == 48 and chunk == 256
    state, keep, send, vec = last_backward(cls, core, own_wide, grad_features, x1, *weights[-1], last_gains, segments, seg_cls, *kept[:-1])
    vecs = [vec[:6]]
    summed = {}
    above, got = [keep], [swap(send, "nc", 1)]
    for layer in reversed(range(L - 1)):
        x, qkv, att, mid = states[layer]
        lg = gains[4 * layer : 4 * layer + 4]
        outs = mlp_backward(core, own_wide, state, mid, att, *weights[layer], lg)
        (grad_mid, mkeep, send, vec_mlp), got, summed = tie((outs, got, summed))
        moving = hop_y(jnp.concatenate([pair(k, g, quarter) for k, g in zip(above, got)]))
        mgot = swap(send, "nc", 1)
        if layer:
            outs = att_backward(core, own_wide, grad_mid, x, qkv, *weights[layer], lg, segments)
            (state, akeep, send, vec_att), mgot, moving = tie((outs, mgot, moving))
            summed[layer + 1] = spread(after(*moving))
            vecs = [vec_att[:2], vec_mlp[:2]] + vecs
            above, got = [akeep, mkeep], [swap(send, "nc", 1), mgot]
        else:
            vec = jnp.concatenate([jnp.zeros((2, D), f32), vec_mlp[:2]] + vecs)
            vec = jnp.pad(vec, ((0, -vec.shape[0] % 16), (0, 0)))
            outs = att_backward(core, own_wide, grad_mid, x, qkv, *weights[layer], lg, segments, (first_vec, inputs, vec, packed))
            (akeep, send, tkeep, tsend), mgot, moving = tie((outs, mgot, moving))
            got = [swap(send, "nc", 1), swap(tsend, "nc", 1)]
            summed[1] = spread(after(*moving))
            mlp = hop_y(pair(mkeep, mgot, quarter))
    head_in = (scale.reshape(1), every, rff_low, read_low, read_w.T)
    head, got, mlp, summed = tie((head_backward(*head_in, 0, 2), got, mlp, summed))
    first = hop_y(pair(akeep, got[0], quarter))
    if packed:
        side = pair(tkeep, got[1], 32)
    else:
        side = add_up([tkeep, got[1]]).astype(bf16).reshape(n_dp, own_dim, ny, chunk).swapaxes(1, 2).reshape(n_dp * ny, -1, D)
    side = hop_y(side)
    mlp = hop_x(after(*mlp))
    (read_step, rff_step, sums0, sums1), first, side, mlp = tie((head_backward(*head_in, 1, 2, head), first, side, mlp))
    head_sums = sums0 + sums1
    side, first = hop_x(after(*side)), hop_x(after(*first))
    low = jnp.concatenate([after(*first), after(*mlp)])
    summed[0] = spread(jnp.concatenate([low, after(*side)], axis=1), "dph")
    side = side[0][0]
    sums = jnp.concatenate([add_up(list(summed[i])) for i in range(L)])

    first_dp = (me_dp == 0).astype(f32)
    first_narrow = (me_narrow == 0).astype(f32)
    local = square_sum([sums]) * (scale * scale)
    local = local + first_dp * head_sums[0, 0]
    ridge = first_dp * head_sums[1, 0]
    total_square, error_total, ridge_total = total_of([local, first_narrow * error_sum, ridge])
    loss_sum = error_total + l2_weight * image_total * ridge_total
    clip_norm = jnp.sqrt(total_square)
    factor = jnp.minimum(1.0, clip_bound / clip_norm)

    sums, factor = tie((sums, factor))
    shares = join_narrow(sums.astype(bf16))
    low = quarter + side.shape[1]
    starts = [0, *(low + i * quarter for i in range(L - 1))]
    rows = jnp.stack([jnp.concatenate([s[a : a + quarter] for s in shares]) for a in starts])
    grad_mats = rows
    tables = [s[quarter:low] for s in shares]
    lanes = jnp.concatenate([unpacked(t) if packed else t.reshape(own_dim, chunk) for t in tables], axis=1)
    grad_embed = lanes[:, :first_vec]
    grad_vector = lanes[:, first_vec : first_vec + vectors].T.astype(f32)

    def back(arrays, shape):
        return [jnp.swapaxes(a.reshape(shape), -1, -2) for a in arrays]

    of_read, of_rff = optimizer(
        factor,
        [([*flat(read_w, read_m, read_v, read_e), read_step], 200), ([rff_w, rff_m, rff_v, rff_e, rff_step], 128)],
        16,
    )
    of_mats, of_embed = optimizer(
        factor * scale,
        [
            ([*flat(mats_w, mats_m, mats_v, mats_e), grad_mats.reshape(-1, D)], math.gcd(L * own_wide, 432)),
            ([*flat(embed_w, embed_m, embed_v, embed_e), grad_embed], own_dim),
        ],
        11,
    )
    outs = [loss_sum, image_total, clip_norm]
    outs += back(of_embed, (own_dim, first_vec))
    outs += adamw(vector_w, vector_m, vector_v, vector_e, grad_vector * (factor * scale), rate_vector, 0.0)
    outs += back(of_mats, (L, own_wide, D))
    outs += of_rff
    outs += back(of_read, read_step.shape)
    return tuple(outs)


def solution(mesh):
    n_dp, n_narrow = mesh.shape["dp"], mesh.shape["narrow"]
    fine = jax.sharding.Mesh(mesh.devices.reshape(n_dp // 2, 2, n_narrow // 2, 2), ALL)
    rows = P(ALL)
    table, mats, rff, read = P(None, DP), P(None, None, DP), P(None, NARROW), P(NARROW, None)
    ins = (P(ALL, None),) + (rows,) * 5 + (table,) * 8 + (mats,) * 4 + (rff,) * 4 + (read,) * 4
    outs = (P(),) * 3 + (table,) * 10 + (mats,) * 5 + (rff,) * 5 + (read,) * 5
    return jax.shard_map(shards, mesh=fine, in_specs=ins, out_specs=outs, check_vma=False)
```

```python
import functools
import math
import jax
import jax.numpy as jnp
from jax import lax
from jax.experimental import pallas as pl
from jax.experimental.pallas import tpu as pltpu
from jax.sharding import PartitionSpec as P

D = 384
HEADS = 6
HD = 64
MLP = 1536
SEQ = 256
norm_eps = 1e-06
EXP_SCALE = 1.4426950408889634 * HD ** (-0.5)
GELU_A = 0.7978845608028654
GELU_B = 0.044715
f32 = jnp.float32
bf16 = jnp.bfloat16


def nn(a, b):
    return lax.dot_general(a, b, (((1,), (0,)), ((), ())), preferred_element_type=f32)


def nt(a, b):
    return lax.dot_general(a, b, (((1,), (1,)), ((), ())), preferred_element_type=f32)


def tn(a, b):
    return lax.dot_general(a, b, (((0,), (0,)), ((), ())), preferred_element_type=f32)


def unit(rows):
    centred = rows - jnp.mean(rows, axis=-1, keepdims=True)
    inverse = lax.rsqrt(jnp.mean(centred * centred, axis=-1, keepdims=True) + norm_eps)
    return centred * inverse, inverse


def unit_back(u, inverse, gain, grad):
    scaled = grad * gain
    return inverse * (
        scaled
        - jnp.mean(scaled, axis=-1, keepdims=True)
        - u * jnp.mean(scaled * u, axis=-1, keepdims=True)
    )


def gelu_parts(x):
    x2 = x * x
    t = jnp.tanh(GELU_A * x * (1.0 + GELU_B * x2))
    half = 0.5 * (1.0 + t)
    return half, t, x2


def gelu_value(x):
    half, _, _ = gelu_parts(x)
    return x * half


def gelu_both(x):
    half, t, x2 = gelu_parts(x)
    slope = half + 0.5 * x * (1.0 - t * t) * (GELU_A * (1.0 + 3.0 * GELU_B * x2))
    return x * half, slope


def layer_rows(x, wa_ref, wu_ref, wd_ref, gains, seg_col, seg_row):
    g1, b1, g2, b2 = (gains[i : i + 1, :] for i in range(4))
    u, _ = unit(x)
    normed = (u * g1 + b1).astype(bf16)
    qkv = nt(normed, wa_ref[: 3 * D, :]).astype(bf16)
    heads = []
    rows = x.shape[0]
    for s in range(rows // SEQ):
        r = slice(s * SEQ, (s + 1) * SEQ)
        same = seg_col[r, :] == seg_row[:, r]
        outs = []
        for h in range(HEADS):
            q = qkv[r, h * HD : (h + 1) * HD]
            k = qkv[r, D + h * HD : D + (h + 1) * HD]
            v = qkv[r, 2 * D + h * HD : 2 * D + (h + 1) * HD]
            sc = jnp.where(same, nt(q, k), -1e30)
            e = jnp.exp2((sc - jnp.max(sc, axis=-1, keepdims=True)) * EXP_SCALE)
            p = (e * (1.0 / jnp.sum(e, axis=-1, keepdims=True))).astype(bf16)
            outs.append(nn(p, v))
        heads.append(jnp.concatenate(outs, axis=1))
    att = jnp.concatenate(heads, axis=0).astype(bf16)
    x1 = x + nt(att, wa_ref[3 * D :, :])
    u2, _ = unit(x1)
    second = (u2 * g2 + b2).astype(bf16)
    hidden = gelu_value(nt(second, wu_ref[...])).astype(bf16)
    out = x1 + nn(hidden, wd_ref[...])
    return qkv, att, x1, out


def fwd_kernel(x_ref, wa_ref, wu_ref, wd_ref, g_ref, sc_ref, sr_ref, qkv_ref, att_ref, x1_ref, out_ref):
    qkv, att, x1, out = layer_rows(x_ref[...], wa_ref, wu_ref, wd_ref, g_ref[...], sc_ref[...], sr_ref[0])
    qkv_ref[...] = qkv
    att_ref[...] = att
    x1_ref[...] = x1
    out_ref[...] = out


def first_kernel(p_ref, pos_ref, e_ref, wa_ref, wu_ref, wd_ref, g_ref, sc_ref, sr_ref, in_ref, x_ref, qkv_ref, att_ref, x1_ref, out_ref):
    pos = pos_ref[...]
    patch = jnp.where(pos != 0, p_ref[...].astype(f32), 0.0).astype(bf16)
    lanes = e_ref.shape[1] - p_ref.shape[1]
    table = (pos == lax.broadcasted_iota(jnp.int32, (pos.shape[0], lanes), 1)).astype(f32).astype(bf16)
    full = jnp.concatenate([patch, table], axis=1)
    in_ref[...] = full
    x = nt(full, e_ref[...])
    x_ref[...] = x
    qkv, att, x1, out = layer_rows(x, wa_ref, wu_ref, wd_ref, g_ref[...], sc_ref[...], sr_ref[0])
    qkv_ref[...] = qkv
    att_ref[...] = att
    x1_ref[...] = x1
    out_ref[...] = out


def join_kernel(plan, n_in, flag_ref, *refs):
    for src, dst in plan(flag_ref[0], refs[:n_in], refs[n_in:]):
        dst[...] = src[...]


def join(plan, flag, ins, shapes):
    return pl.pallas_call(
        functools.partial(join_kernel, plan, len(ins)),
        in_specs=[smem_spec()] + [vmem_spec()] * len(ins),
        out_specs=[vmem_spec()] * len(shapes),
        out_shape=[jax.ShapeDtypeStruct(s, bf16) for s in shapes],
        compiler_params=pltpu.CompilerParams(vmem_limit_bytes=24 << 20),
        cost_estimate=lasting(1),
        name="join",
    )(flag, *ins)


def joined_kernel(core_ref, h_ref, hg_ref, t_ref, tg_ref, p_ref, pos_ref, g_ref, sc_ref, sr_ref, in_ref, x_ref, qkv_ref, att_ref, x1_ref, out_ref, wo_ref, w_ref, tab_ref, sems, out_sem):
    step = pl.program_id(0)
    cells, piece = h_ref.shape[0], h_ref.shape[1]
    core = core_ref[0]
    copies = []
    for src, at in ((h_ref, core), (hg_ref, 1 - core)):
        for i in range(cells):
            copies.append((src.at[i], w_ref.at[pl.ds(pl.multiple_of((2 * i + at) * piece, 16), piece)]))
    for src, at in ((t_ref, core), (tg_ref, 1 - core)):
        for y in range(t_ref.shape[1]):
            copies.append((src.at[:, y], tab_ref.at[2 * y + at]))
    copies = [pltpu.make_async_copy(a, b, sems.at[i]) for i, (a, b) in enumerate(copies)]
    result = pltpu.make_async_copy(w_ref, wo_ref, out_sem)

    @pl.when(step == 0)
    def _():
        for c in copies:
            c.start()
        for c in copies:
            c.wait()
        result.start()

    pos = pos_ref[...]
    patch = jnp.where(pos != 0, p_ref[...].astype(f32), 0.0).astype(bf16)
    lanes = in_ref.shape[1] - p_ref.shape[1]
    onehot = (pos == lax.broadcasted_iota(jnp.int32, (pos.shape[0], lanes), 1)).astype(f32).astype(bf16)
    full = jnp.concatenate([patch, onehot], axis=1)
    in_ref[...] = full
    width = tab_ref.shape[3]
    x = sum(nt(full[:, n * width : (n + 1) * width], tab_ref[n].reshape(D, width)) for n in range(tab_ref.shape[0]))
    x_ref[...] = x
    qkv, att, x1, out = layer_rows(x, w_ref.at[: 4 * D], w_ref.at[4 * D : 8 * D], w_ref.at[8 * D :], g_ref[...], sc_ref[...], sr_ref[0])
    qkv_ref[...] = qkv
    att_ref[...] = att
    x1_ref[...] = x1
    out_ref[...] = out

    @pl.when(step == pl.num_programs(0) - 1)
    def _():
        result.wait()


def joined_forward(core, half, half_got, table, table_got, patches, pos, gains, seg, step_rows=512):
    rows, patch = patches.shape
    lanes = 2 * table.shape[1] * table.shape[3]
    steps = rows // step_rows
    anywhere = pl.BlockSpec(memory_space=pl.ANY)
    return pl.pallas_call(
        joined_kernel,
        grid=(steps,),
        in_specs=[
            smem_spec(),
            *[anywhere] * 4,
            rows_spec(step_rows, patch),
            rows_spec(step_rows, 1),
            whole_spec(gains.shape),
            rows_spec(step_rows, 1),
            pl.BlockSpec((1, 1, step_rows), lambda i: (i, 0, 0)),
        ],
        out_specs=[rows_spec(step_rows, lanes), rows_spec(step_rows, D), rows_spec(step_rows, 3 * D), rows_spec(step_rows, D), rows_spec(step_rows, D), rows_spec(step_rows, D), anywhere],
        out_shape=[
            jax.ShapeDtypeStruct((rows, lanes), bf16),
            jax.ShapeDtypeStruct((rows, D), f32),
            jax.ShapeDtypeStruct((rows, 3 * D), bf16),
            jax.ShapeDtypeStruct((rows, D), bf16),
            jax.ShapeDtypeStruct((rows, D), f32),
            jax.ShapeDtypeStruct((rows, D), f32),
            jax.ShapeDtypeStruct((12 * D, D), bf16),
        ],
        scratch_shapes=[
            pltpu.VMEM((12 * D, D), bf16),
            pltpu.VMEM((2 * table.shape[1], *table.shape[:1], *table.shape[2:]), bf16),
            pltpu.SemaphoreType.DMA((2 * half.shape[0] + 2 * table.shape[1],)),
            pltpu.SemaphoreType.DMA(()),
        ],
        compiler_params=params(),
        cost_estimate=lasting(18),
        name="first_fwd",
    )(core, half, half_got, table, table_got, patches, pos[:, None], gains, seg[:, None], seg.reshape(steps, 1, step_rows))


def rows_spec(r, width):
    return pl.BlockSpec((r, width), lambda i: (i, 0))


def whole_spec(shape):
    return pl.BlockSpec(shape, lambda *i: (0,) * len(shape))


def third_spec(block):
    return pl.BlockSpec((4 * D, D), lambda *i: (block, 0))


def params(mb=56, n=1):
    return pltpu.CompilerParams(dimension_semantics=("arbitrary",) * n, vmem_limit_bytes=mb << 20)


def lasting(us):
    return pl.CostEstimate(flops=int(us * 1e9), bytes_accessed=int(us * 2e6), transcendentals=0)


def layer_forward(x, w, layer, gains, seg, step_rows=512):
    rows = x.shape[0]
    steps = rows // step_rows
    return pl.pallas_call(
        fwd_kernel,
        grid=(steps,),
        in_specs=[
            rows_spec(step_rows, D),
            *(third_spec(3 * layer + i) for i in range(3)),
            whole_spec(gains.shape),
            rows_spec(step_rows, 1),
            pl.BlockSpec((1, 1, step_rows), lambda i: (i, 0, 0)),
        ],
        out_specs=[rows_spec(step_rows, 3 * D), rows_spec(step_rows, D), rows_spec(step_rows, D), rows_spec(step_rows, D)],
        out_shape=[
            jax.ShapeDtypeStruct((rows, 3 * D), bf16),
            jax.ShapeDtypeStruct((rows, D), bf16),
            jax.ShapeDtypeStruct((rows, D), f32),
            jax.ShapeDtypeStruct((rows, D), f32),
        ],
        compiler_params=params(),
        cost_estimate=lasting(17),
        name="layer_fwd",
    )(x, w, w, w, gains, seg[:, None], seg.reshape(steps, 1, step_rows))


def first_forward(patches, pos, e, w, layer, gains, seg, step_rows=512):
    rows, patch = patches.shape
    lanes = e.shape[1]
    steps = rows // step_rows
    return pl.pallas_call(
        first_kernel,
        grid=(steps,),
        in_specs=[
            rows_spec(step_rows, patch),
            rows_spec(step_rows, 1),
            whole_spec(e.shape),
            *(third_spec(3 * layer + i) for i in range(3)),
            whole_spec(gains.shape),
            rows_spec(step_rows, 1),
            pl.BlockSpec((1, 1, step_rows), lambda i: (i, 0, 0)),
        ],
        out_specs=[rows_spec(step_rows, lanes), rows_spec(step_rows, D), rows_spec(step_rows, 3 * D), rows_spec(step_rows, D), rows_spec(step_rows, D), rows_spec(step_rows, D)],
        out_shape=[
            jax.ShapeDtypeStruct((rows, lanes), bf16),
            jax.ShapeDtypeStruct((rows, D), f32),
            jax.ShapeDtypeStruct((rows, 3 * D), bf16),
            jax.ShapeDtypeStruct((rows, D), bf16),
            jax.ShapeDtypeStruct((rows, D), f32),
            jax.ShapeDtypeStruct((rows, D), f32),
        ],
        compiler_params=params(),
        cost_estimate=lasting(18),
        name="first_fwd",
    )(patches, pos[:, None], e, w, w, w, gains, seg[:, None], seg.reshape(steps, 1, step_rows))


def last_fwd_kernel(cls_ref, x_ref, wa_ref, wu_ref, wd_ref, g_ref, sk_ref, sq_ref, kv_ref, xc_ref, q_ref, att_ref, x1_ref, out_ref, feat_ref):
    g1, b1, g2, b2, g3, b3 = (g_ref[i : i + 1, :] for i in range(6))
    u, _ = unit(x_ref[...])
    normed = (u * g1 + b1).astype(bf16)
    kv = nt(normed, wa_ref[D : 3 * D, :]).astype(bf16)
    kv_ref[...] = kv
    slots = xc_ref.shape[0]
    for i in range(slots):
        xc_ref[i : i + 1, :] = x_ref[pl.ds(cls_ref[i], 1), :]
    xc = xc_ref[...]
    uc, _ = unit(xc)
    q = nt((uc * g1 + b1).astype(bf16), wa_ref[:D, :]).astype(bf16)
    q_ref[...] = q
    same = sq_ref[...] == sk_ref[...]
    outs = []
    for h in range(HEADS):
        c = slice(h * HD, (h + 1) * HD)
        sc = jnp.where(same, nt(q[:, c], kv[:, c]) * HD ** (-0.5), -1e30)
        e = jnp.exp(sc - jnp.max(sc, axis=-1, keepdims=True))
        p = (e * (1.0 / jnp.sum(e, axis=-1, keepdims=True))).astype(bf16)
        outs.append(nn(p, kv[:, D + h * HD : D + (h + 1) * HD]))
    att = jnp.concatenate(outs, axis=1).astype(bf16)
    att_ref[...] = att
    x1 = xc + nt(att, wa_ref[3 * D :, :])
    x1_ref[...] = x1
    u2, _ = unit(x1)
    second = (u2 * g2 + b2).astype(bf16)
    hidden = gelu_value(nt(second, wu_ref[...])).astype(bf16)
    out = x1 + nn(hidden, wd_ref[...])
    out_ref[...] = out
    u3, _ = unit(out)
    feat_ref[...] = (u3 * g3 + b3).astype(bf16)


def put_halves(core_ref, acc_ref, keep_ref, send_ref):
    half = keep_ref.shape[1]
    mine = core_ref[0] * half
    other = (1 - core_ref[0]) * half
    for i in range(keep_ref.shape[0]):
        base = i * 2 * half
        keep_ref[i] = acc_ref[pl.ds(base + mine, half), :].astype(bf16)
        send_ref[i] = acc_ref[pl.ds(base + other, half), :].astype(bf16)


def smem_spec():
    return pl.BlockSpec(memory_space=pltpu.SMEM)


def vmem_spec():
    return pl.BlockSpec(memory_space=pltpu.VMEM)


def last_forward(cls, x, w, layer, gains, seg, seg_cls):
    rows, slots = x.shape[0], cls.shape[0]
    return pl.pallas_call(
        last_fwd_kernel,
        grid=(1,),
        in_specs=[smem_spec(), whole_spec(x.shape), *(third_spec(3 * layer + i) for i in range(3)), *[vmem_spec()] * 3],
        out_specs=[vmem_spec()] * 7,
        out_shape=[
            jax.ShapeDtypeStruct((rows, 2 * D), bf16),
            jax.ShapeDtypeStruct((slots, D), f32),
            jax.ShapeDtypeStruct((slots, D), bf16),
            jax.ShapeDtypeStruct((slots, D), bf16),
            jax.ShapeDtypeStruct((slots, D), f32),
            jax.ShapeDtypeStruct((slots, D), f32),
            jax.ShapeDtypeStruct((slots, D), bf16),
        ],
        compiler_params=params(),
        cost_estimate=lasting(9),
        name="last_fwd",
    )(cls, x, w, w, w, gains, seg[None, :], seg_cls[:, None])


def last_bwd_kernel(cls_ref, core_ref, df_ref, x_ref, wa_ref, wu_ref, wd_ref, g_ref, sk_ref, sq_ref, kv_ref, xc_ref, q_ref, att_ref, x1_ref, xo_ref, dx_ref, keep_ref, send_ref, dv_ref, dn_ref, dw_ref):
    g1, b1, g2, b2, g3, b3 = (g_ref[i : i + 1, :] for i in range(6))
    slots = xc_ref.shape[0]
    df = df_ref[...]
    u3, i3 = unit(xo_ref[...])
    dxo = unit_back(u3, i3, g3, df)
    dg3 = jnp.sum(df * u3, axis=0, keepdims=True)
    db3 = jnp.sum(df, axis=0, keepdims=True)
    branch = dxo.astype(bf16)
    u2, i2 = unit(x1_ref[...])
    second = (u2 * g2 + b2).astype(bf16)
    value, slope = gelu_both(nt(second, wu_ref[...]))
    dpre = (nt(branch, wd_ref[...]) * slope).astype(bf16)
    dw_ref[4 * D + MLP :, :] = tn(value.astype(bf16), branch)
    dw_ref[4 * D : 4 * D + MLP, :] = tn(dpre, second)
    dsecond = nn(dpre, wu_ref[...])
    dg2 = jnp.sum(dsecond * u2, axis=0, keepdims=True)
    db2 = jnp.sum(dsecond, axis=0, keepdims=True)
    dx1 = dxo + unit_back(u2, i2, g2, dsecond)
    ab = dx1.astype(bf16)
    datt = nn(ab, wa_ref[3 * D :, :]).astype(bf16)
    dw_ref[3 * D : 4 * D, :] = tn(ab, att_ref[...])
    same = sq_ref[...] == sk_ref[...]
    q, kv = q_ref[...], kv_ref[...]
    dqs, dks, dvs = [], [], []
    for h in range(HEADS):
        c = slice(h * HD, (h + 1) * HD)
        k, v = kv[:, c], kv[:, D + h * HD : D + (h + 1) * HD]
        sc = jnp.where(same, nt(q[:, c], k) * HD ** (-0.5), -1e30)
        e = jnp.exp(sc - jnp.max(sc, axis=-1, keepdims=True))
        p = e * (1.0 / jnp.sum(e, axis=-1, keepdims=True))
        dp = nt(datt[:, c], v)
        ds = (p * (dp - jnp.sum(dp * p, axis=-1, keepdims=True))).astype(bf16)
        dvs.append(tn(p.astype(bf16), datt[:, c]))
        dks.append(tn(ds, q[:, c]) * HD ** (-0.5))
        dqs.append(nn(ds, k) * HD ** (-0.5))
    dq = jnp.concatenate(dqs, axis=1).astype(bf16)
    dkv = jnp.concatenate(dks + dvs, axis=1).astype(bf16)
    u, i1 = unit(x_ref[...])
    normed = (u * g1 + b1).astype(bf16)
    dw_ref[D : 3 * D, :] = tn(dkv, normed)
    uc, _ = unit(xc_ref[...])
    dw_ref[:D, :] = tn(dq, (uc * g1 + b1).astype(bf16))
    dn_ref[...] = nn(dkv, wa_ref[D : 3 * D, :])
    dnc = nn(dq, wa_ref[:D, :])
    for i in range(slots):
        at = pl.ds(cls_ref[i], 1)
        dn_ref[at, :] = dn_ref[at, :] + dnc[i : i + 1, :]
    dn = dn_ref[...]
    dg1 = jnp.sum(dn * u, axis=0, keepdims=True)
    db1 = jnp.sum(dn, axis=0, keepdims=True)
    dx_ref[...] = unit_back(u, i1, g1, dn)
    for i in range(slots):
        at = pl.ds(cls_ref[i], 1)
        dx_ref[at, :] = dx_ref[at, :] + dx1[i : i + 1, :]
    dv_ref[...] = jnp.concatenate([dg1, db1, dg2, db2, dg3, db3, jnp.zeros((2, D), f32)], axis=0)
    put_halves(core_ref, dw_ref, keep_ref, send_ref)


def last_backward(cls, core, wide, df, x, w, layer, gains, seg, seg_cls, kv, xc, q, att, x1, xo):
    rows = x.shape[0]
    return pl.pallas_call(
        last_bwd_kernel,
        grid=(1,),
        in_specs=[smem_spec(), smem_spec(), vmem_spec(), whole_spec(x.shape), *(third_spec(3 * layer + i) for i in range(3)), *[vmem_spec()] * 9],
        out_specs=[vmem_spec()] * 4,
        out_shape=[
            jax.ShapeDtypeStruct((rows, D), f32),
            *[jax.ShapeDtypeStruct((12 * D // wide, wide // 2, D), bf16)] * 2,
            jax.ShapeDtypeStruct((8, D), f32),
        ],
        scratch_shapes=[pltpu.VMEM((rows, D), f32), pltpu.VMEM((12 * D, D), f32)],
        compiler_params=params(),
        cost_estimate=lasting(15),
        name="last_bwd",
    )(cls, core, df, x, w, w, w, gains, seg[None, :], seg_cls[:, None], kv, xc, q, att, x1, xo)


def mlp_bwd_kernel(core_ref, dxo_ref, x1_ref, att_ref, wu_ref, wd_ref, g_ref, dx1_ref, keep_ref, send_ref, dv_ref, acc_ref):
    step = pl.program_id(0)
    g2, b2 = g_ref[2:3, :], g_ref[3:4, :]
    dxo = dxo_ref[...]
    branch = dxo.astype(bf16)
    u2, i2 = unit(x1_ref[...])
    second = (u2 * g2 + b2).astype(bf16)
    value, slope = gelu_both(nt(second, wu_ref[...]))
    hidden = value.astype(bf16)
    dpre = (nt(branch, wd_ref[...]) * slope).astype(bf16)
    dsecond = nn(dpre, wu_ref[...])
    sums = jnp.concatenate([jnp.sum(dsecond * u2, axis=0, keepdims=True), jnp.sum(dsecond, axis=0, keepdims=True), jnp.zeros((6, D), f32)], axis=0)
    dx1 = dxo + unit_back(u2, i2, g2, dsecond)
    dx1_ref[...] = dx1
    ab = dx1.astype(bf16)
    last = pl.num_programs(0) - 1

    @pl.when(step == 0)
    def _():
        acc_ref[:D, :] = tn(ab, att_ref[...])
        acc_ref[D : D + MLP, :] = tn(dpre, second)
        acc_ref[D + MLP :, :] = tn(hidden, branch)
        dv_ref[...] = sums

    @pl.when(step > 0)
    def _():
        acc_ref[:D, :] += tn(ab, att_ref[...])
        acc_ref[D : D + MLP, :] += tn(dpre, second)
        acc_ref[D + MLP :, :] += tn(hidden, branch)
        dv_ref[...] += sums

    @pl.when(step == last)
    def _():
        put_halves(core_ref, acc_ref, keep_ref, send_ref)


def mlp_backward(core, wide, dxo, x1, att, w, layer, gains, step_rows=512):
    rows = x1.shape[0]
    steps = rows // step_rows
    return pl.pallas_call(
        mlp_bwd_kernel,
        grid=(steps,),
        in_specs=[smem_spec(), *[rows_spec(step_rows, D)] * 3, third_spec(3 * layer + 1), third_spec(3 * layer + 2), whole_spec(gains.shape)],
        out_specs=[rows_spec(step_rows, D), *[whole_spec((9 * D // wide, wide // 2, D))] * 2, whole_spec((8, D))],
        out_shape=[jax.ShapeDtypeStruct((rows, D), f32), *[jax.ShapeDtypeStruct((9 * D // wide, wide // 2, D), bf16)] * 2, jax.ShapeDtypeStruct((8, D), f32)],
        scratch_shapes=[pltpu.VMEM((9 * D, D), f32)],
        compiler_params=params(),
        cost_estimate=lasting(16),
        name="mlp_bwd",
    )(core, dxo, x1, att, w, w, gains)


def att_bwd_kernel(first_vec, *refs):
    core_ref, dx1_ref, x_ref, qkv_ref, w_ref, g_ref, sc_ref, sr_ref, *refs = refs
    if first_vec:
        in_ref, vec_ref, keep_ref, send_ref, tkeep_ref, tsend_ref, acc_ref, dv_ref, table_ref = refs
    else:
        dx_ref, keep_ref, send_ref, dv_ref, acc_ref = refs
    step = pl.program_id(0)
    g1, b1 = g_ref[0:1, :], g_ref[1:2, :]
    dx1 = dx1_ref[...]
    ab = dx1.astype(bf16)
    datt = nn(ab, w_ref[3 * D : 4 * D, :]).astype(bf16)
    qkv = qkv_ref[...]
    parts = []
    for s in range(x_ref.shape[0] // SEQ):
        r = slice(s * SEQ, (s + 1) * SEQ)
        same = sc_ref[r, :] == sr_ref[0][:, r]
        dqs, dks, dvs = [], [], []
        for h in range(HEADS):
            q = qkv[r, h * HD : (h + 1) * HD]
            k = qkv[r, D + h * HD : D + (h + 1) * HD]
            v = qkv[r, 2 * D + h * HD : 2 * D + (h + 1) * HD]
            da = datt[r, h * HD : (h + 1) * HD]
            sc = jnp.where(same, nt(k, q), -1e30)
            e = jnp.exp2((sc - jnp.max(sc, axis=0, keepdims=True)) * EXP_SCALE)
            p = e * (1.0 / jnp.sum(e, axis=0, keepdims=True))
            dp = nt(v, da)
            ds = (p * (dp - jnp.sum(dp * p, axis=0, keepdims=True))).astype(bf16)
            dvs.append(nn(p.astype(bf16), da))
            dks.append(nn(ds, q) * HD ** (-0.5))
            dqs.append(tn(ds, k) * HD ** (-0.5))
        parts.append(jnp.concatenate(dqs + dks + dvs, axis=1).astype(bf16))
    dqkv = jnp.concatenate(parts, axis=0)
    u, i1 = unit(x_ref[...])
    normed = (u * g1 + b1).astype(bf16)
    dn = nn(dqkv, w_ref[: 3 * D, :])
    sums = jnp.concatenate([jnp.sum(dn * u, axis=0, keepdims=True), jnp.sum(dn, axis=0, keepdims=True), jnp.zeros((6, D), f32)], axis=0)
    dx = dx1 + unit_back(u, i1, g1, dn)
    if first_vec:
        grad_table = tn(dx.astype(bf16), in_ref[...])
    else:
        dx_ref[...] = dx
    last = pl.num_programs(0) - 1

    @pl.when(step == 0)
    def _():
        acc_ref[...] = tn(dqkv, normed)
        if first_vec:
            table_ref[...] = grad_table
        dv_ref[...] = sums

    @pl.when(step > 0)
    def _():
        acc_ref[...] += tn(dqkv, normed)
        if first_vec:
            table_ref[...] += grad_table
        dv_ref[...] += sums

    @pl.when(step == last)
    def _():
        put_halves(core_ref, acc_ref, keep_ref, send_ref)
        if first_vec:
            rows, lanes = vec_ref.shape[0], table_ref.shape[1]
            vec = vec_ref[...] + jnp.concatenate([dv_ref[...], jnp.zeros((rows - 8, D), f32)], axis=0)
            at = lax.broadcasted_iota(jnp.int32, (rows, lanes), 1) - first_vec
            pick = (at == lax.broadcasted_iota(jnp.int32, (rows, lanes), 0)).astype(f32).astype(bf16)
            table_ref[...] += tn(vec.astype(bf16), pick)
            half = lanes // 2
            mine = pl.multiple_of(core_ref[0] * half, 128)
            other = pl.multiple_of((1 - core_ref[0]) * half, 128)
            if len(tkeep_ref.shape) == 2:
                tkeep_ref[...] = table_ref[:, pl.ds(mine, half)].astype(bf16)
                tsend_ref[...] = table_ref[:, pl.ds(other, half)].astype(bf16)
            else:
                put_cells(table_ref, mine, half, tkeep_ref)
                put_cells(table_ref, other, half, tsend_ref)


PACK = ((0, 0, 32, 0, 0), (0, 32, 16, 0, 1), (1, 0, 16, 16, 1), (1, 16, 32, 0, 2))


def put_cells(table_ref, base, half, out_ref):
    for d in range(D // 48):
        for y in range(half // 256):
            cell = d * (half // 256) + y
            for block, row, count, to_row, to_block in PACK:
                lane = pl.multiple_of(base + y * 256 + block * 128, 128)
                value = table_ref[d * 48 + row : d * 48 + row + count, pl.ds(lane, 128)]
                out_ref[cell, to_row : to_row + count, to_block * 128 : to_block * 128 + 128] = value.astype(bf16)


def att_backward(core, wide, dx1, x, qkv, w, layer, gains, seg, table=None, step_rows=512):
    rows = x.shape[0]
    steps = rows // step_rows
    parts = [jax.ShapeDtypeStruct((3 * D // wide, wide // 2, D), bf16)] * 2
    whole = [whole_spec(p.shape) for p in parts]
    acc = pltpu.VMEM((3 * D, D), f32)
    if table is None:
        first_vec, more, more_specs = 0, (), []
        out_specs = [rows_spec(step_rows, D), *whole, whole_spec((8, D))]
        out_shape = [jax.ShapeDtypeStruct((rows, D), f32), *parts, jax.ShapeDtypeStruct((8, D), f32)]
        scratch = [acc]
    else:
        first_vec, inputs, vec, packed = table
        lanes = inputs.shape[1]
        side = (D // 48 * (lanes // 512), 32, D) if packed else (D, lanes // 2)
        more, more_specs = (inputs, vec), [rows_spec(step_rows, lanes), whole_spec(vec.shape)]
        out_shape = [*parts, *[jax.ShapeDtypeStruct(side, bf16)] * 2]
        out_specs = [whole_spec(p.shape) for p in out_shape]
        scratch = [acc, pltpu.VMEM((8, D), f32), pltpu.VMEM((D, lanes), f32)]
    return pl.pallas_call(
        functools.partial(att_bwd_kernel, first_vec),
        grid=(steps,),
        in_specs=[
            smem_spec(),
            rows_spec(step_rows, D),
            rows_spec(step_rows, D),
            rows_spec(step_rows, 3 * D),
            third_spec(3 * layer),
            whole_spec(gains.shape),
            rows_spec(step_rows, 1),
            pl.BlockSpec((1, 1, step_rows), lambda i: (i, 0, 0)),
            *more_specs,
        ],
        out_specs=out_specs,
        out_shape=out_shape,
        scratch_shapes=scratch,
        compiler_params=params(),
        cost_estimate=lasting(18),
        name="att_bwd",
    )(core, dx1, x, qkv, w, gains, seg[:, None], seg.reshape(steps, 1, step_rows), *more)


HALF_PI = (1.5703125, 0.000483751296996, 7.54978995489e-08, 5.1266913e-12)


def sin_cos(x):
    k = jnp.round(x * 0.6366197723675814)
    r = x
    for part in HALF_PI:
        r = r - k * part
    r = jnp.clip(r, -1.0, 1.0)
    r2 = r * r
    s = r + r * r2 * (-1.6666654611e-1 + r2 * (8.3321608736e-3 + r2 * -1.9515295891e-4))
    c = 1.0 - 0.5 * r2 + r2 * r2 * (4.166664568298827e-2 + r2 * (-1.388731625493765e-3 + r2 * 2.443315711809948e-5))
    n = k.astype(jnp.int32)
    odd = (n & 1) == 1
    sin_v = jnp.where(odd, c, s)
    cos_v = jnp.where(odd, s, c)
    sin_v = jnp.where((n & 2) == 2, -sin_v, sin_v)
    cos_v = jnp.where(((n + 1) & 2) == 2, -cos_v, cos_v)
    return sin_v, cos_v


def head_kernel(several, skip, s_ref, all_ref, rff_ref, read_ref, w_ref, *refs):
    gread_ref, grff_ref, sums_ref, sin_ref, cos_ref, *sums = refs[skip:]
    features = all_ref[:, :D]
    logits = all_ref[:, D:]
    phases = nn(features, rff_ref[...])
    large = jnp.max(jnp.abs(phases)) > 5e4

    @pl.when(large)
    def _():
        sin_ref[...] = jnp.sin(phases)
        cos_ref[...] = jnp.cos(phases)

    @pl.when(jnp.logical_not(large))
    def _():
        sin_ref[...], cos_ref[...] = sin_cos(phases)

    lifted = cos_ref[...].astype(bf16)
    back = (-sin_ref[...] * nn(logits, read_ref[...])).astype(bf16)
    blocks = pl.num_programs(1)
    gread = tn(logits, lifted)
    grff = tn(features, back)
    if several:
        block = pl.program_id(1)

        read_sum, rff_sum = sums

        @pl.when(block == 0)
        def _():
            read_sum[...] = gread
            rff_sum[...] = grff

        @pl.when(block > 0)
        def _():
            read_sum[...] += gread
            rff_sum[...] += grff

        @pl.when(block == blocks - 1)
        def _():
            head_finish(s_ref, w_ref, read_sum[...], rff_sum[...], gread_ref, grff_ref, sums_ref)
    else:
        head_finish(s_ref, w_ref, gread, grff, gread_ref, grff_ref, sums_ref)


def head_finish(s_ref, w_ref, gread, grff, gread_ref, grff_ref, sums_ref):
    step = pl.program_id(0)
    w = w_ref[...]
    gread = gread * s_ref[0] + 2.0 * l2_weight * w
    grff = grff * s_ref[0]
    gread_ref[...] = gread.astype(bf16)
    grff_ref[...] = grff.astype(bf16)
    total = jnp.sum(jnp.sum(gread * gread, axis=0, keepdims=True)) + jnp.sum(jnp.sum(grff * grff, axis=0, keepdims=True))
    ridge = jnp.sum(jnp.sum(w * w, axis=0, keepdims=True))
    row = lax.broadcasted_iota(jnp.int32, (8, 128), 0)
    tile = jnp.where(row == 0, total, jnp.where(row == 1, ridge, 0.0))

    @pl.when(step == 0)
    def _():
        sums_ref[...] = tile

    @pl.when(step > 0)
    def _():
        sums_ref[...] += tile


def head_backward(scale, every, rff, read, w, part, parts, before=None, cols=256):
    n, classes = every.shape[0], read.shape[0]
    width = rff.shape[1]
    cols = min(cols, width // parts)
    rows = math.gcd(n, 768)
    steps = width // cols // parts
    base = part * steps
    col = lambda r: pl.BlockSpec((r, cols), lambda i, j: (0, base + i))
    more = () if before is None else before[:2]
    out = pl.pallas_call(
        functools.partial(head_kernel, n > rows, len(more)),
        grid=(steps, n // rows),
        in_specs=[smem_spec(), pl.BlockSpec((rows, every.shape[1]), lambda i, j: (j, 0)), col(D), col(classes), col(classes)] + [pl.BlockSpec(memory_space=pl.ANY)] * len(more),
        out_specs=[col(classes), col(D), whole_spec((8, 128))],
        out_shape=[jax.ShapeDtypeStruct((classes, width), bf16), jax.ShapeDtypeStruct((D, width), bf16), jax.ShapeDtypeStruct((8, 128), f32)],
        scratch_shapes=[pltpu.VMEM((rows, cols), f32)] * 2 + ([pltpu.VMEM((r, cols), f32) for r in (classes, D)] if n > rows else []),
        input_output_aliases={5 + i: i for i in range(len(more))},
        compiler_params=params(56, 2),
        cost_estimate=lasting(8),
        name="head_bwd",
    )(scale, every, rff, read, w, *more)
    return out if before is None else [*out[:2], before[2], out[2]]


def optimizer_kernel(plan, f_ref, *refs):
    step = pl.program_id(0)
    ins, outs = refs[: 5 * len(plan)], refs[5 * len(plan) :]
    low = 0
    for i, count in enumerate(plan):

        @pl.when((step >= low) & (step < low + count))
        def _(i=i):
            *state, g_ref = ins[5 * i : 5 * i + 5]
            out = adamw(*(r[...] for r in state), g_ref[...].astype(f32) * f_ref[0], rate_matrix, weight_decay)
            for o_ref, value in zip(outs[5 * i : 5 * i + 5], out):
                o_ref[...] = value

        low += count


def optimizer(factor, groups, us):
    plan = [arrays[-1].shape[0] // rows for arrays, rows in groups]
    specs, out_specs, out_shape, args = [], [], [], []
    low = 0
    for (arrays, rows), count in zip(groups, plan):
        shape = arrays[-1].shape
        spec = pl.BlockSpec((rows, shape[1]), lambda i, low=low, count=count: (jnp.clip(i - low, 0, count - 1), 0))
        specs += [spec] * 5
        out_specs += [spec] * 5
        out_shape += [jax.ShapeDtypeStruct(shape, f32)] * 4 + [jax.ShapeDtypeStruct(shape, bf16)]
        args += arrays
        low += count
    out = pl.pallas_call(
        functools.partial(optimizer_kernel, plan),
        grid=(low,),
        in_specs=[smem_spec(), *specs],
        out_specs=out_specs,
        out_shape=out_shape,
        compiler_params=params(48),
        cost_estimate=lasting(us),
        name="optimizer",
    )(factor.reshape(1), *args)
    return [out[5 * i : 5 * i + 5] for i in range(len(groups))]


POS = 197
CLASSES = 1000
L = 3
IMG_SEQ = 6
STEP = 10
PART = 4 * D
WIDE = 3 * PART
clip_bound = 0.02
l2_weight = 0.1
beta_first = 0.5
beta_second = 0.5
adam_eps = 1e-08
weight_decay = 0.05
rate_matrix = 0.05
rate_vector = 0.5
ema_rate = 0.5
DP = ("dph", "dpl")
NARROW = ("ny", "nc")
ALL = DP + NARROW


def swap(rows, axis, mask):
    return lax.ppermute(rows, axis, [(i, i ^ mask) for i in range(lax.axis_size(axis))])


def add_up(terms):
    return sum(t.astype(f32) for t in terms)


def bits_of(size):
    return size.bit_length() - 1


def spread(cells, axes=DP):
    return lax.all_to_all(cells, axes, 0, 0)


def hop_y(cells):
    ny = lax.axis_size("ny")
    cells = cells.reshape(-1, ny, *cells.shape[1:])
    if ny > 2:
        return [lax.psum_scatter(cells, "ny", scatter_dimension=1, tiled=False)], None
    mine = lax.axis_index("ny")
    keep = lax.dynamic_index_in_dim(cells, mine, 1, keepdims=False)
    return [keep], swap(lax.dynamic_index_in_dim(cells, 1 - mine, 1, keepdims=False), "ny", 1)


def hop_x(rows):
    rows = rows.reshape(-1, 2, *rows.shape[1:])
    mine = lax.axis_index("dpl")
    keep = lax.dynamic_index_in_dim(rows, mine, 1, keepdims=False)
    return [keep], swap(lax.dynamic_index_in_dim(rows, 1 - mine, 1, keepdims=False), "dpl", 1)


def after(terms, got):
    return terms[0] if got is None else add_up([*terms, got]).astype(bf16)


def pair(keep, got, rows):
    return add_up([keep, got]).astype(bf16).reshape(-1, rows, D)


def unpacked(cell):
    left = jnp.concatenate([cell[:, :128], cell[:16, 128:256]])
    right = jnp.concatenate([cell[16:, 128:256], cell[:, 256:]])
    return jnp.concatenate([left, right], axis=1)


def join_narrow(piece):
    every = lax.all_gather(piece, NARROW, axis=0, tiled=False)
    cores, ys = lax.axis_size("nc"), lax.axis_size("ny")
    return [every[y * cores + core] for core in range(cores) for y in range(ys)]


def total_of(scalars):
    lane = lax.broadcasted_iota(jnp.int32, (8, 128), 1)
    tile = jnp.zeros((8, 128), f32)
    for i, value in enumerate(scalars):
        tile = jnp.where(lane == i, value, tile)
    world = lax.axis_size(ALL)
    every = lax.all_to_all(jnp.broadcast_to(tile[None], (world, 8, 128)), ALL, 0, 0)
    row = jnp.sum(every, axis=0)[0]
    return [row[i] for i in range(len(scalars))]


def adamw(weight, first, second, average, grad, rate, decay):
    first = beta_first * first + (1.0 - beta_first) * grad
    second = beta_second * second + (1.0 - beta_second) * grad * grad
    ahead = first / (1.0 - beta_first**STEP)
    behind = second / (1.0 - beta_second**STEP)
    weight = weight - rate * (ahead / (jnp.sqrt(behind) + adam_eps) + decay * weight)
    average = ema_rate * average + (1.0 - ema_rate) * weight
    return (weight, first, second, average, weight.astype(bf16))


def square_sum(arrays):
    return sum(jnp.sum(a.astype(f32) * a.astype(f32)) for a in arrays)


def shards(
    patches,
    pos_index,
    segments,
    cls_row,
    labels,
    img_count,
    embed_w,
    embed_m,
    embed_v,
    embed_e,
    vector_w,
    vector_m,
    vector_v,
    vector_e,
    mats_w,
    mats_m,
    mats_v,
    mats_e,
    rff_w,
    rff_m,
    rff_v,
    rff_e,
    read_w,
    read_m,
    read_v,
    read_e,
):
    n_dp, n_narrow = lax.axis_size(DP), lax.axis_size(NARROW)
    me_dp, me_narrow = lax.axis_index(DP), lax.axis_index(NARROW)
    own_dim = embed_w.shape[1]
    own_wide = mats_w.shape[2]
    core = lax.axis_index("nc").astype(jnp.int32).reshape(1)
    slots = cls_row.shape[0]
    table_rows = -(-(embed_w.shape[0] + vector_w.shape[0]) // 256) * 256
    chunk = table_rows // n_narrow

    tie = lax.optimization_barrier

    def small_facts():
        return total_of([jnp.sum(img_count).astype(f32)])[0]

    def low_head():
        pad = -slots % 16
        cls = jnp.concatenate([cls_row, jnp.broadcast_to(cls_row[-1:], (pad,))])
        slot_ids = jnp.arange(slots)
        valid = (slot_ids % IMG_SEQ < jnp.repeat(img_count, IMG_SEQ, total_repeat_length=slots)).astype(jnp.int32)
        facts = lax.all_gather(jnp.stack([labels, valid]), NARROW, axis=0)
        return rff_w.astype(bf16), read_w.T.astype(bf16), cls, segments[cls], facts

    table = jnp.concatenate([embed_w.T, vector_w.T], axis=1).astype(bf16)
    table = jnp.pad(table, ((0, 0), (0, table_rows - table.shape[1])))
    table = lax.dynamic_slice_in_dim(table, me_narrow * chunk, chunk, 1)
    quarter = own_wide // n_narrow
    mats_own = lax.dynamic_slice_in_dim(jnp.swapaxes(mats_w, 1, 2), me_narrow * quarter, quarter, 1).astype(bf16)
    first_vec, vectors = embed_w.shape[0], vector_w.shape[0]
    rest = lax.all_gather(mats_own[1:], ALL, axis=1, tiled=True).reshape((L - 1) * WIDE, D)
    dph, dpl, ny = (lax.axis_size(a) for a in ("dph", "dpl", "ny"))

    if (dph, dpl, ny) == (4, 2, 2) and quarter % 16 == 0 and own_dim % 16 == 0 and chunk % 128 == 0:
        cut = quarter // 32 * 16

        def flag(axis, bit=0):
            return ((lax.axis_index(axis) >> bit) & 1).astype(jnp.int32).reshape(1)

        def both(src, got, dst, put):
            return lambda f, i, o: [(i[src], put(o[dst], f)), (i[got], put(o[dst], 1 - f))]

        def plan_of(*moves):
            return lambda f, i, o: [c for move in moves for c in move(f, i, o)]

        a, e = mats_own[:1], table[None]
        ga, ge = swap(a, "dph", 2), swap(e, "dph", 2)
        ahead = lambda o, f: o.at[:, f]
        a, e = join(plan_of(both(0, 1, 0, ahead), both(2, 3, 1, ahead)), flag("dph", 1), (a, ga, e, ge), ((1, 2, quarter, D), (1, 2, own_dim, chunk)))
        a, e = a.reshape(2, quarter, D), e.reshape(2, own_dim, chunk)
        (ga, ge), image_total = tie(((swap(a, "dph", 1), swap(e, "dph", 1)), small_facts()))

        def split(f, i, o):
            out = []
            for src, at in ((i[0], f), (i[1], 1 - f)):
                out += [(src.at[:, :cut], o[0].at[:, at]), (src.at[:, cut:], o[1].at[:, at])]
            return out + [(i[2], o[2].at[:, f]), (i[3], o[2].at[:, 1 - f])]

        p, q, e = join(split, flag("dph"), (a, ga, e, ge), ((2, 2, cut, D), (2, 2, quarter - cut, D), (2, 2, own_dim, chunk)))
        p, q, e = (t.reshape(4, *t.shape[2:]) for t in (p, q, e))
        gp, gq, ge = swap(p, "dpl", 1), swap(q, "ny", 1), swap(e, "dpl", 1)
        (p,) = join(both(0, 1, 0, ahead), flag("dpl"), (p, gp), ((4, 2, cut, D),))
        (q,) = join(both(0, 1, 0, ahead), flag("ny"), (q, gq), ((4, 2, quarter - cut, D),))
        (e,) = join(both(0, 1, 0, ahead), flag("dpl"), (e, ge), ((4, 2, own_dim, chunk),))
        (gp, gq, ge), low_parts = tie(((swap(p, "ny", 1), swap(q, "dpl", 1), swap(e, "ny", 1)), low_head()))

        def last(f, i, o):
            fx, fy = f
            return [
                (i[0], o[0].at[:, :, fy, :cut]),
                (i[1], o[0].at[:, :, 1 - fy, :cut]),
                (i[2], o[0].at[:, fx, :, cut:]),
                (i[3], o[0].at[:, 1 - fx, :, cut:]),
                (i[4], o[1].at[:, :, fy]),
                (i[5], o[1].at[:, :, 1 - fy]),
            ]

        half, e = join(
            lambda f, i, o: last((f & 1, f >> 1), i, o),
            flag("dpl") + 2 * flag("ny"),
            (p, gp, q, gq, e, ge),
            ((4, 2, 2, quarter, D), (4, 2, 2, own_dim, chunk)),
        )
        half, e = half.reshape(n_dp * ny, quarter, D), e.reshape(n_dp, ny, own_dim, chunk)
        got, ge = swap(half, "nc", 1), swap(e, "nc", 1)
        holder, lane = first_vec // chunk, first_vec % chunk
        piece = jnp.where(core[0] == holder % 2, e[:, holder // 2], ge[:, holder // 2])
        gains = piece[:, :, lane : lane + vectors].reshape(D, vectors).T.astype(f32)
        outs = joined_forward(core, half, got, e, ge, patches, pos_index, gains[0:4], segments)
        inputs, x0, qkv0, att0, mid0, x1, mats0 = outs
    else:
        image_total = small_facts()
        low_parts = low_head()
        table = lax.all_gather(table, ALL, axis=0)
        table = table.reshape(n_dp, n_narrow, own_dim, chunk).transpose(0, 2, 1, 3).reshape(D, table_rows)
        mats0 = lax.all_gather(mats_own[0], ALL, axis=0, tiled=True)
        gains = table[:, first_vec : first_vec + vectors].T.astype(f32)
        inputs, x0, qkv0, att0, mid0, x1 = first_forward(patches, pos_index, table, mats0, 0, gains[0:4], segments)
    rff_low, read_low, cls, seg_cls, facts = low_parts
    group_labels = facts[:, 0].reshape(-1)
    group_valid = facts[:, 1].reshape(-1).astype(f32)[:, None]
    pad = cls.shape[0] - slots
    weights = [(mats0, 0)] + [(rest, i) for i in range(L - 1)]

    states = [(x0, qkv0, att0, mid0)]
    for layer in range(1, L - 1):
        qkv, att, mid, x2 = layer_forward(x1, *weights[layer], gains[4 * layer : 4 * layer + 4], segments)
        states.append((x1, qkv, att, mid))
        x1 = x2
    last_gains = gains[4 * L - 4 :]
    kept = last_forward(cls, x1, *weights[-1], last_gains, segments, seg_cls)
    features = kept[-1][:slots]

    group_rows = lax.all_gather(features, NARROW, axis=0, tiled=True)
    phases = nn(group_rows, rff_low)
    lifted = jnp.cos(phases).astype(bf16)
    partial = lax.all_gather(nt(lifted, read_low).astype(bf16), NARROW, axis=0)
    logits = jnp.sum(partial.astype(f32), axis=0)
    error = logits - (group_labels[:, None] == jnp.arange(CLASSES)[None, :]).astype(f32)
    error_sum = jnp.sum(group_valid * error * error)
    grad_logits = (2.0 * group_valid * error).astype(bf16)
    grad_phases = (-jnp.sin(phases) * nn(grad_logits, read_low)).astype(bf16)
    grad_pieces = nt(grad_phases, rff_low).reshape(n_narrow, slots, D)
    grad_features = jnp.sum(lax.all_to_all(grad_pieces, NARROW, 0, 0), axis=0)
    grad_features = jnp.pad(grad_features, ((0, pad), (0, 0)))

    own_logits = lax.dynamic_slice_in_dim(grad_logits, me_narrow * slots, slots, 0)
    own_rows, grad_features = tie((jnp.concatenate([features, own_logits], axis=1), grad_features))
    every = lax.all_gather(own_rows, ALL, axis=0, tiled=True)
    scale = 1.0 / image_total

    def flat(*arrays):
        turned = [jnp.swapaxes(a, -1, -2) for a in arrays]
        return [t.reshape(-1, t.shape[-1]) for t in turned]

    packed = own_dim == 48 and chunk == 256
    state, keep, send, vec = last_backward(cls, core, own_wide, grad_features, x1, *weights[-1], last_gains, segments, seg_cls, *kept[:-1])
    vecs = [vec[:6]]
    summed = {}
    above, got = [keep], [swap(send, "nc", 1)]
    for layer in reversed(range(L - 1)):
        x, qkv, att, mid = states[layer]
        lg = gains[4 * layer : 4 * layer + 4]
        outs = mlp_backward(core, own_wide, state, mid, att, *weights[layer], lg)
        (grad_mid, mkeep, send, vec_mlp), got, summed = tie((outs, got, summed))
        moving = hop_y(jnp.concatenate([pair(k, g, quarter) for k, g in zip(above, got)]))
        mgot = swap(send, "nc", 1)
        if layer:
            outs = att_backward(core, own_wide, grad_mid, x, qkv, *weights[layer], lg, segments)
            (state, akeep, send, vec_att), mgot, moving = tie((outs, mgot, moving))
            summed[layer + 1] = spread(after(*moving))
            vecs = [vec_att[:2], vec_mlp[:2]] + vecs
            above, got = [akeep, mkeep], [swap(send, "nc", 1), mgot]
        else:
            vec = jnp.concatenate([jnp.zeros((2, D), f32), vec_mlp[:2]] + vecs)
            vec = jnp.pad(vec, ((0, -vec.shape[0] % 16), (0, 0)))
            outs = att_backward(core, own_wide, grad_mid, x, qkv, *weights[layer], lg, segments, (first_vec, inputs, vec, packed))
            (akeep, send, tkeep, tsend), mgot, moving = tie((outs, mgot, moving))
            got = [swap(send, "nc", 1), swap(tsend, "nc", 1)]
            cells, moving = tie((pair(mkeep, mgot, quarter), moving))
            mlp = hop_y(cells)
            summed[1] = spread(after(*moving))
    head_in = (scale.reshape(1), every, rff_low, read_low, read_w.T)
    head, got, mlp, summed = tie((head_backward(*head_in, 0, 2), got, mlp, summed))
    first = hop_y(pair(akeep, got[0], quarter))
    if packed:
        side = pair(tkeep, got[1], 32)
    else:
        side = add_up([tkeep, got[1]]).astype(bf16).reshape(n_dp, own_dim, ny, chunk).swapaxes(1, 2).reshape(n_dp * ny, -1, D)
    side = hop_y(side)
    mlp = hop_x(after(*mlp))
    (read_step, rff_step, sums0, sums1), first, side, mlp = tie((head_backward(*head_in, 1, 2, head), first, side, mlp))
    head_sums = sums0 + sums1
    side, first = hop_x(after(*side)), hop_x(after(*first))
    low = jnp.concatenate([after(*first), after(*mlp)])
    summed[0] = spread(jnp.concatenate([low, after(*side)], axis=1), "dph")
    side = side[0][0]
    sums = jnp.concatenate([add_up(list(summed[i])) for i in range(L)])

    first_dp = (me_dp == 0).astype(f32)
    first_narrow = (me_narrow == 0).astype(f32)
    local = square_sum([sums]) * (scale * scale)
    local = local + first_dp * head_sums[0, 0]
    ridge = first_dp * head_sums[1, 0]
    total_square, error_total, ridge_total = total_of([local, first_narrow * error_sum, ridge])
    loss_sum = error_total + l2_weight * image_total * ridge_total
    clip_norm = jnp.sqrt(total_square)
    factor = jnp.minimum(1.0, clip_bound / clip_norm)

    sums, factor = tie((sums, factor))
    shares = join_narrow(sums.astype(bf16))
    low = quarter + side.shape[1]
    starts = [0, *(low + i * quarter for i in range(L - 1))]
    rows = jnp.stack([jnp.concatenate([s[a : a + quarter] for s in shares]) for a in starts])
    grad_mats = rows
    tables = [s[quarter:low] for s in shares]
    lanes = jnp.concatenate([unpacked(t) if packed else t.reshape(own_dim, chunk) for t in tables], axis=1)
    grad_embed = lanes[:, :first_vec]
    grad_vector = lanes[:, first_vec : first_vec + vectors].T.astype(f32)

    def back(arrays, shape):
        return [jnp.swapaxes(a.reshape(shape), -1, -2) for a in arrays]

    of_read, of_rff = optimizer(
        factor,
        [([*flat(read_w, read_m, read_v, read_e), read_step], 200), ([rff_w, rff_m, rff_v, rff_e, rff_step], 128)],
        16,
    )
    of_mats, of_embed = optimizer(
        factor * scale,
        [
            ([*flat(mats_w, mats_m, mats_v, mats_e), grad_mats.reshape(-1, D)], math.gcd(L * own_wide, 432)),
            ([*flat(embed_w, embed_m, embed_v, embed_e), grad_embed], own_dim),
        ],
        11,
    )
    outs = [loss_sum, image_total, clip_norm]
    outs += back(of_embed, (own_dim, first_vec))
    outs += adamw(vector_w, vector_m, vector_v, vector_e, grad_vector * (factor * scale), rate_vector, 0.0)
    outs += back(of_mats, (L, own_wide, D))
    outs += of_rff
    outs += back(of_read, read_step.shape)
    return tuple(outs)


def solution(mesh):
    n_dp, n_narrow = mesh.shape["dp"], mesh.shape["narrow"]
    fine = jax.sharding.Mesh(mesh.devices.reshape(n_dp // 2, 2, n_narrow // 2, 2), ALL)
    rows = P(ALL)
    table, mats, rff, read = P(None, DP), P(None, None, DP), P(None, NARROW), P(NARROW, None)
    ins = (P(ALL, None),) + (rows,) * 5 + (table,) * 8 + (mats,) * 4 + (rff,) * 4 + (read,) * 4
    outs = (P(),) * 3 + (table,) * 10 + (mats,) * 5 + (rff,) * 5 + (read,) * 5
    return jax.shard_map(shards, mesh=fine, in_specs=ins, out_specs=outs, check_vma=False)
```
